128 devices in a mesh: day: 16 (over z, x), blk: 8 (over y, core).
Axes of the slice: x: 4, y: 4, z: 4, core: 2. Of those that a mesh axis runs over, the one named last changes fastest.
Arguments:
- diag_blocks: float32 [32, 2560, 2560], P('day', 'blk'), may hold values from -1 to 3, as said below
- off_blocks: float32 [32, 2560, 2560], P('day', 'blk'), may hold values from -1 to 1
- leakage: float32 [32, 2560], P('day', 'blk'), may hold values from 0.001 to 0.3
- obs_count: int32 [32], P('day'), may hold values from 1 to 1024, 16384 in all
- obs_triangle: int32 [32, 1024], P('day', 'blk'), may hold values from 0 to 5115
- obs_bary: float32 [3, 32, 1024], P(None, 'day', 'blk'), may hold values from 0.05 to 1
- obs_prec: float32 [32, 1024], P('day', 'blk'), may hold values from 0.3 to 3
- obs_value: float32 [32, 1024], P('day', 'blk'), may hold values from -6 to 6
- covariates: float32 [64, 32, 1024], P(None, 'day', 'blk'), may hold values from -0.0625 to 0.0625
- triangles: int32 [3, 5116], replicated, may hold values from 0 to 2559
- prior_prec: float32 [64], replicated, may hold values from 0.5 to 2
- probes: float32 [15, 32, 2560], P(None, 'day', 'blk'), may hold values from -6 to 6
- probes_cov: float32 [15, 64], replicated, may hold values from -6 to 6
Outputs:
- step_field: float32 [16, 32, 2560], P(None, 'day', 'blk')
- step_cov: float32 [16, 64], replicated
The draws below stay inside these ranges and needn't reach their ends.
Inputs may be any that keep to these rules, and one draw needn't show every extreme that they name: Every block diag_blocks[t] is symmetric, and the whole precision made of diag_blocks and off_blocks is positive definite. Slots 0 to obs_count[t] - 1 of day t hold observations, the others are empty; the counts sum to 16384.
All inputs are finite; a program needn't handle non-finite values. No bound on the sum of `obs_count` on one device may be relied on, other than what follows from the above.
Results may differ from the reference program's by a relative error of at most 0.0002.
Values sent between devices are 32-bit elements; how exact they have to be, the bound alone decides.
No kernel may reach another device: no remote copies, remote signals or barrier semaphores. Data moves between devices by JAX's collectives and lax.ppermute only.
A program may use at most 192 MiB of HBM per device.

```python
import math
import jax
import jax.numpy as jnp
import numpy as np
from jax import lax

S = 2560
COV = 64
PROBES = 15
ITERS = 3
OBS_CAP = 1024
DAYS = 32
NTRI = 5116


def draw_diag_blocks(key, part):
    first_key, second_key = jax.random.split(jax.random.fold_in(key, 11))
    raw_entries = jax.random.normal(first_key, (DAYS, S, S), jnp.float32)
    symmetric = (raw_entries + jnp.swapaxes(raw_entries, 1, 2)) * (0.3 / math.sqrt(2.0 * S))
    levels = jax.random.uniform(second_key, (DAYS, S), jnp.float32, 1.2, 2.2)
    return symmetric + levels[:, :, None] * jnp.eye(S, dtype=jnp.float32)


def draw_off_blocks(key, part):
    entry_key = jax.random.fold_in(key, 23)
    raw_entries = jax.random.normal(entry_key, (DAYS, S, S), jnp.float32)
    return raw_entries * (0.125 / math.sqrt(S))


def with_ends(array, key, low, top_value):
    place = [jax.random.randint(jax.random.fold_in(key, axis), (), 0, length) for axis, length in enumerate(array.shape)]
    main_axis = array.shape.index(max(array.shape))
    next_to = place[:main_axis] + [(place[main_axis] + 1) % array.shape[main_axis]] + place[main_axis + 1:]
    return array.at[tuple(place)].set(low).at[tuple(next_to)].set(top_value)


def steps_of(rng, dims, pieces, low, top_value):
    def one(position, blocks):
        heights = jax.random.uniform(jax.random.fold_in(jax.random.fold_in(rng, 6), position), (blocks,), jnp.float32, low / len(pieces), top_value / len(pieces))
        return jnp.repeat(jnp.exp(heights), dims[position] // blocks).reshape((-1,) + (1,) * (len(dims) - position - 1))

    loudness = one(*pieces[0])
    for cut in pieces[1:]:
        loudness = loudness * one(*cut)
    return loudness


def profile(amount, total, reach, lean):
    loads = [(1 << 20) // math.isqrt(rank ** lean) + 1 for rank in range(2, amount + 1)]
    spare, holding = total - reach - (amount - 1), [1] * (amount - 1)
    while spare > 0:
        candidates = [i for i in range(amount - 1) if holding[i] < reach]
        mass, budget = sum([loads[i] for i in candidates]), spare
        for i in candidates:
            extra = min(reach - holding[i], max(1, budget * loads[i] // mass), spare)
            holding[i] = holding[i] + extra
            spare = spare - extra
    return np.array([reach] + holding)


def uneven_parts(stream_key, number_of, total, bound, slope):
    if number_of == 2:
        one = jax.random.randint(stream_key, (), max(1, total - bound), min(bound, total - 1) + 1)
        return jnp.stack([one, total - one])
    lengths = jnp.asarray(profile(number_of, total, bound, slope), jnp.int32)
    pairs = (number_of - 1) // 2
    source_of, sink = lengths[1:1 + 2 * pairs:2], lengths[2:2 + 2 * pairs:2]
    margin = jnp.minimum(source_of - 1, bound - sink)
    shifted = jax.random.randint(jax.random.fold_in(stream_key, 1), (pairs,), 0, 1 << 20) % (margin + 1)
    lengths = lengths.at[1:1 + 2 * pairs:2].set(source_of - shifted).at[2:2 + 2 * pairs:2].set(sink + shifted)
    return lengths[jax.random.permutation(jax.random.fold_in(stream_key, 2), number_of)]


def noise(stream_key, shape, deviation, bound, cuts=(), kind=jnp.bfloat16):
    gain = steps_of(stream_key, shape, cuts, -0.22, 0.18) if cuts else 1.0
    entries = jax.random.normal(stream_key, shape, jnp.float32) * deviation * gain
    return jnp.minimum(jnp.maximum(entries, -bound), bound).astype(kind)


def setup_inputs(seed: int = 0) -> dict:
    keys = jax.random.split(jax.random.key(seed), 14)
    return {
        "diag_blocks": draw_diag_blocks(jax.random.fold_in(keys[13], 71), 0),
        "off_blocks": draw_off_blocks(jax.random.fold_in(keys[13], 71), 0),
        "leakage": jnp.clip(jnp.exp(math.log(0.3) - 5.7037825 * jax.random.uniform(keys[2], (DAYS, S), jnp.float32) ** steps_of(keys[2], (DAYS, S), ((0, 16), (1, 8)), -0.2, 0.2)), 0.001, 0.3),
        "obs_count": uneven_parts(keys[3], DAYS, DAYS * OBS_CAP // 2, OBS_CAP, 2).astype(jnp.int32),
        "obs_triangle": with_ends(jax.random.randint(keys[4], (DAYS, OBS_CAP), 0, NTRI), jax.random.fold_in(keys[4], 1), 0, NTRI - 1).astype(jnp.int32),
        "obs_bary": jnp.clip(jnp.exp(math.log(1.0) - 2.9957323 * jax.random.uniform(keys[5], (3, DAYS, OBS_CAP), jnp.float32) ** steps_of(keys[5], (3, DAYS, OBS_CAP), ((1, 16), (2, 8)), -0.2, 0.2)), 0.05, 1.0),
        "obs_prec": jnp.clip(jnp.exp(math.log(3.0) - 2.3025851 * jax.random.uniform(keys[6], (DAYS, OBS_CAP), jnp.float32) ** steps_of(keys[6], (DAYS, OBS_CAP), ((0, 16), (1, 8)), -0.2, 0.2)), 0.3, 3.0),
        "obs_value": noise(keys[7], (DAYS, OBS_CAP), 1.0, 6.0, ((0, 16), (1, 8)), jnp.float32),
        "covariates": noise(keys[8], (COV, DAYS, OBS_CAP), (DAYS * OBS_CAP // 4) ** -0.5, 0.0625, ((1, 16), (2, 8)), jnp.float32),
        "triangles": with_ends(jax.random.randint(keys[9], (3, NTRI), 0, S), jax.random.fold_in(keys[9], 1), 0, S - 1).astype(jnp.int32),
        "prior_prec": jnp.clip(jnp.exp(jax.random.uniform(keys[10], (COV,), jnp.float32, math.log(0.5), math.log(2.0))), 0.5, 2.0),
        "probes": noise(keys[11], (PROBES, DAYS, S), 1.0, 6.0, ((1, 16), (2, 8)), jnp.float32),
        "probes_cov": noise(keys[12], (PROBES, COV), 1.0, 6.0, (), jnp.float32),
    }


def spread(values, flat_ids, segments):
    leading = values.shape[0]
    summed = jax.ops.segment_sum(values.reshape(leading, -1).T, flat_ids, num_segments=segments)
    return summed.T


def observation_setup(obs_count, obs_triangle, obs_bary, obs_prec, triangles):
    slot_index = lax.broadcasted_iota(jnp.int32, obs_triangle.shape, 1)
    slot_weight = jnp.where(slot_index < obs_count[:, None], obs_prec, jnp.zeros_like(obs_prec))
    vertices = triangles[:, obs_triangle].astype(jnp.int32)
    day_index = lax.broadcasted_iota(jnp.int32, vertices.shape, 1)
    flat_ids = (vertices + S * day_index).reshape(-1).astype(jnp.int32)
    barycentric = obs_bary / jnp.sum(obs_bary, axis=0, keepdims=True)
    return flat_ids, barycentric, slot_weight


def apply_hessian(direction, direction_cov, diag_blocks, off_blocks, flat_ids, barycentric, slot_weight, covariates, prior_prec):
    rhs_count = direction.shape[0]
    exact = lax.Precision.HIGHEST
    diagonal_terms = jnp.einsum('tij,rtj->rti', diag_blocks, direction, precision=exact)
    ahead_terms = jnp.einsum('tij,rtj->rti', off_blocks[:-1], direction[:, 1:], precision=exact)
    behind_terms = jnp.einsum('tji,rtj->rti', off_blocks[:-1], direction[:, :-1], precision=exact)
    empty_day = jnp.zeros((rhs_count, 1, S), jnp.float32)
    coupled = diagonal_terms + jnp.concatenate([ahead_terms, empty_day], axis=1) + jnp.concatenate([empty_day, behind_terms], axis=1)
    picked = direction.reshape(rhs_count, -1)[:, flat_ids].reshape((rhs_count,) + barycentric.shape)
    predictor = jnp.sum(barycentric[None] * picked, axis=1) + jnp.einsum('ctj,rc->rtj', covariates, direction_cov, precision=exact)
    weighted = slot_weight[None] * predictor
    obs_terms = spread(barycentric[None] * weighted[:, None], flat_ids, DAYS * S).reshape(rhs_count, DAYS, S)
    image_cov = jnp.einsum('ctj,rtj->rc', covariates, weighted, precision=exact) + prior_prec[None] * direction_cov
    return coupled + obs_terms, image_cov


def precondition(residual, decays, dominant):
    start = jnp.zeros((residual.shape[0], S), jnp.float32)

    def forward(running, pair):
        value_day, decay_day = pair
        running = value_day + decay_day[None] * running
        return running, running

    unused, lowered = lax.scan(forward, start, (jnp.swapaxes(residual, 0, 1), decays))
    scaled = lowered / dominant[:, None, :]
    decay_next = jnp.concatenate([decays[1:], jnp.zeros((1, S), jnp.float32)], axis=0)

    def backward(running, pair):
        value_day, decay_day = pair
        running = value_day + decay_day[None] * running
        return running, running

    unused, raised = lax.scan(backward, start, (scaled, decay_next), reverse=True)
    return jnp.swapaxes(raised, 0, 1)


def reference(diag_blocks, off_blocks, leakage, obs_count, obs_triangle, obs_bary, obs_prec, obs_value, covariates, triangles, prior_prec, probes, probes_cov):
    flat_ids, barycentric, slot_weight = observation_setup(obs_count, obs_triangle, obs_bary, obs_prec, triangles)
    decays = 1.0 - leakage
    dominant = jnp.diagonal(diag_blocks, axis1=1, axis2=2)
    weighted_value = slot_weight * obs_value
    grad_field = spread((barycentric * weighted_value[None])[None], flat_ids, DAYS * S).reshape(1, DAYS, S)
    grad_cov = jnp.einsum('ctj,tj->c', covariates, weighted_value, precision=lax.Precision.HIGHEST)
    residual = jnp.concatenate([grad_field, probes], axis=0)
    residual_cov = jnp.concatenate([grad_cov[None], probes_cov], axis=0)
    solution = jnp.zeros_like(residual)
    solution_cov = jnp.zeros_like(residual_cov)
    preconditioned = precondition(residual, decays, dominant)
    direction = preconditioned
    direction_cov = residual_cov
    norm_now = jnp.sum(residual * preconditioned, axis=(1, 2)) + jnp.sum(residual_cov * residual_cov, axis=1)
    for iteration in range(ITERS):
        image, image_cov = apply_hessian(direction, direction_cov, diag_blocks, off_blocks, flat_ids, barycentric, slot_weight, covariates, prior_prec)
        curvature = jnp.sum(direction * image, axis=(1, 2)) + jnp.sum(direction_cov * image_cov, axis=1)
        step_length = norm_now / curvature
        solution = solution + step_length[:, None, None] * direction
        solution_cov = solution_cov + step_length[:, None] * direction_cov
        if iteration + 1 < ITERS:
            residual = residual - step_length[:, None, None] * image
            residual_cov = residual_cov - step_length[:, None] * image_cov
            preconditioned = precondition(residual, decays, dominant)
            norm_next = jnp.sum(residual * preconditioned, axis=(1, 2)) + jnp.sum(residual_cov * residual_cov, axis=1)
            conjugacy = norm_next / norm_now
            direction = preconditioned + conjugacy[:, None, None] * direction
            direction_cov = residual_cov + conjugacy[:, None] * direction_cov
            norm_now = norm_next
    return solution, solution_cov
```

```python
import jax
import jax.numpy as jnp
from jax import lax
from jax.sharding import Mesh
from jax.sharding import PartitionSpec as P

DAY = ("day_0", "day_1")
BLK = ("blk_0", "blk_1")
HIGH = lax.Precision.HIGH


def shift(value, axis, distance):
    size = lax.axis_size(axis)
    return lax.ppermute(value, axis, [(i, (i + distance) % size) for i in range(size)])


def swapped(value):
    return lax.ppermute(value, "blk_1", [(0, 1), (1, 0)])


def ring_gather(value, axis):
    return [value] + [shift(value, axis, k) for k in (1, 2, 3)]


def ring_sum(relative):
    return (relative[0] + relative[2]) + (relative[1] + relative[3])


def absolute(relative, place):
    stacked = jnp.stack(relative)
    return jnp.stack([lax.dynamic_index_in_dim(stacked, (place - j) % 4, 0, False) for j in range(4)])


def reduce_scatter_nodes(part):
    core, row = lax.axis_index("blk_1"), lax.axis_index("blk_0")
    lead = part.shape[:-1]
    part = jnp.moveaxis(part.reshape(*lead, 4, 2, 320), (-3, -2), (0, 1))
    kept = jnp.where(core == 0, part[:, 0], part[:, 1])
    sent = jnp.where(core == 0, part[:, 1], part[:, 0])
    half = kept + swapped(sent)
    own = lax.dynamic_index_in_dim(half, row, 0, False)
    for k in (1, 2, 3):
        piece = lax.dynamic_index_in_dim(half, (row + k) % 4, 0, False)
        own = own + shift(piece, "blk_0", k)
    return own


def gather_nodes(message):
    core, row = lax.axis_index("blk_1"), lax.axis_index("blk_0")
    column = absolute(ring_gather(message, "blk_0"), row)
    other = swapped(column)
    first = jnp.where(core == 0, column, other)
    second = jnp.where(core == 0, other, column)
    return jnp.stack([first, second], axis=1)


def chain_coefficients(decay, dominant):
    group, place = lax.axis_index("day_0"), lax.axis_index("day_1")
    me = 4 * group + place
    decays = decay.reshape(32, 320)
    dominants = dominant.reshape(32, 320)
    gain = [None] * 33
    gain[32] = jnp.zeros_like(decays[0])
    follow = jnp.concatenate([decays[1:], jnp.zeros((1, 320), jnp.float32)])
    for day in range(31, -1, -1):
        gain[day] = 1.0 / dominants[day] + follow[day] * follow[day] * gain[day + 1]
    gains = jnp.stack(gain)
    follows = jnp.concatenate([decays, jnp.zeros((1, 320), jnp.float32)])
    days = lax.dynamic_slice_in_dim(gains, 2 * me, 3, 0)
    decs = lax.dynamic_slice_in_dim(follows, 2 * me, 3, 0)
    step = (follows[1::2] * follows[2::2]).reshape(4, 4, 320)
    mine = lax.dynamic_index_in_dim(step, group, 0, False)
    one, zero = jnp.ones((320,), jnp.float32), jnp.zeros((320,), jnp.float32)
    index = jnp.arange(4)[:, None]

    def product(factors, low, high):
        kept = jnp.where((index >= low) & (index < high), factors, 1.0)
        return kept[0] * kept[1] * kept[2] * kept[3]

    whole = jnp.prod(step, axis=1)
    local_f, local_b, total_f, total_b, far = [], [], [], [], []
    for k in range(4):
        source = (place - k) % 4
        total_f.append(product(mine, source + 1, 4))
        total_b.append(product(mine, 0, source))
        if k:
            local_f.append(jnp.where(source < place, product(mine, source + 1, place), zero))
            local_b.append(jnp.where(source > place, product(mine, place + 1, source), zero))
            origin = (group - k) % 4
            low, high = jnp.minimum(origin, group) + 1, jnp.maximum(origin, group)
            far.append(product(whole, low, high))
    return dict(
        gain=days, dec=decs, local_f=local_f, local_b=local_b, total_f=total_f, total_b=total_b,
        far=far, before=product(mine, 0, place), after=product(mine, place + 1, 4),
    )


def precondition(field, pack, co):
    group = lax.axis_index("day_0")
    w0, w1, x = field
    (g0, g1, gg), (_, d1, dg) = co["gain"], co["dec"]
    ahead = dg * (w1 + d1 * w0) + x
    behind = g0 * w0 + d1 * (g1 * w1 + dg * gg * x)
    pieces = ring_gather(jnp.concatenate([ahead, behind, pack], axis=1), "day_1")
    fs, bs, packs = zip(*[(p[:, :320], p[:, 320:640], p[:, 640:]) for p in pieces])
    pack = ring_sum(packs)
    local_f = sum(co["local_f"][k - 1] * fs[k] for k in (1, 2, 3))
    local_b = sum(co["local_b"][k - 1] * bs[k] for k in (1, 2, 3))
    total_f = sum(co["total_f"][k] * fs[k] for k in range(4))
    total_b = sum(co["total_b"][k] * bs[k] for k in range(4))
    far_f, far_b = jnp.zeros_like(w0), jnp.zeros_like(w0)
    far_packs = [pack]
    for k in (1, 2, 3):
        sent = jnp.where(group + k < 4, total_f, total_b)
        got = shift(jnp.concatenate([sent, pack], axis=1), "day_0", k)
        far_packs.append(got[:, 320:])
        value = co["far"][k - 1] * got[:, :320]
        far_f = far_f + jnp.where(group >= k, value, 0.0)
        far_b = far_b + jnp.where(group >= k, 0.0, value)
    come_f = local_f + co["before"] * far_f
    come_b = local_b + co["after"] * far_b
    l0 = w0 + come_f
    l1 = w1 + d1 * l0
    u1 = dg * (come_b + gg * x)
    u0 = d1 * (g1 * w1 + u1)
    return (g0 * l0 + u0, g1 * l1 + u1, gg * (dg * l1 + x) + come_b), ring_sum(far_packs)


def dot(first, second):
    return sum(jnp.sum(a * b, axis=1) for a, b in zip(first, second))


def mix(first, scale, second):
    return tuple(a + scale[:, None] * b for a, b in zip(first, second))


def on_device(
    diag_blocks,
    off_blocks,
    leakage,
    obs_count,
    obs_triangle,
    obs_bary,
    obs_prec,
    obs_value,
    covariates,
    triangles,
    prior_prec,
    probes,
    probes_cov,
):
    row_start = lax.axis_index(BLK) * 320
    slot_start = lax.axis_index(BLK) * 128
    last = (lax.axis_index("day_0") == 3) & (lax.axis_index("day_1") == 3)
    slot_index = lax.broadcasted_iota(jnp.int32, obs_triangle.shape, 1) + slot_start
    slot_weight = jnp.where(slot_index < obs_count[:, None], obs_prec, jnp.zeros_like(obs_prec))
    vertices = triangles[:, obs_triangle]
    barycentric = obs_bary / jnp.sum(obs_bary, axis=0, keepdims=True)
    nodes = lax.broadcasted_iota(jnp.int32, (2, 128, 2560), 2)
    spread = sum(
        jnp.where(nodes == vertices[k][:, :, None], barycentric[k][:, :, None], 0.0) for k in range(3)
    )
    square = lax.dynamic_slice_in_dim(diag_blocks, row_start, 320, 2)
    rows = lax.broadcasted_iota(jnp.int32, (2, 320, 320), 1)
    columns = lax.broadcasted_iota(jnp.int32, (2, 320, 320), 2)
    dominant = jnp.sum(jnp.where(rows == columns, square, 0.0), axis=1)

    both = jnp.stack([1.0 - leakage, dominant])
    near = absolute(ring_gather(both, "day_1"), lax.axis_index("day_1"))
    every = absolute(ring_gather(near, "day_0"), lax.axis_index("day_0")).reshape(16, 2, 2, 320)
    co = chain_coefficients(every[:, 0], every[:, 1])

    weighted_value = slot_weight * obs_value
    grad = reduce_scatter_nodes(jnp.einsum("tj,tjs->ts", weighted_value, spread, precision=HIGH))
    grad_cov = jnp.einsum("ctj,tj->c", covariates, weighted_value, precision=lax.Precision.HIGHEST)
    b = tuple(jnp.concatenate([grad[t][None], probes[:, t]], axis=0) for t in range(2))
    zero = jnp.zeros((16, 320), jnp.float32)

    def packed_with(cov, *scalars):
        pack = jnp.concatenate([cov] + [s[:, None] for s in scalars], axis=1)
        return jnp.pad(pack, ((0, 0), (0, 128 - pack.shape[1])))

    def all_nodes(vector, pack):
        message = gather_nodes(jnp.concatenate(vector + (pack,), axis=1))
        whole = message[..., :960].reshape(4, 2, 16, 3, 320)
        whole = jnp.moveaxis(whole, (0, 1), (2, 3)).reshape(16, 3, 2560)
        return whole, jnp.sum(message[:, :, :, 960:], axis=(0, 1))

    def product(whole, cov):
        own_rows = jnp.einsum("tis,rts->tri", diag_blocks, whole[:, :2], precision=HIGH)
        ahead = jnp.einsum("tis,rts->tri", off_blocks, whole[:, 1:], precision=HIGH)
        predictor = jnp.einsum("rts,tjs->rtj", whole[:, :2], spread, precision=HIGH) + jnp.einsum(
            "ctj,rc->rtj", covariates, cov, precision=HIGH
        )
        return own_rows, ahead, predictor

    def hessian(vector, whole, cov):
        own_rows, ahead, predictor = product(whole, cov)
        weighted = slot_weight[None] * predictor
        obs = jnp.einsum("rtj,tjs->trs", weighted, spread, precision=HIGH)
        own = jnp.stack(vector[:2])
        behind = jnp.einsum("tis,tri->trs", off_blocks, own, precision=HIGH)
        part = jnp.stack([obs[0], obs[1] + behind[0], jnp.where(last, 0.0, behind[1])])
        done = reduce_scatter_nodes(part)
        cov_terms = jnp.einsum("ctj,rtj->rc", covariates, weighted, precision=HIGH)
        rows_sum = own_rows + ahead
        return (rows_sum[0] + done[0], rows_sum[1] + done[1], done[2]), cov_terms

    v1, pack = precondition(
        b + (zero,), packed_with(jnp.pad(grad_cov[None], ((0, 15), (0, 0)))), co
    )
    whole1, pack = all_nodes(v1, pack)
    c0 = jnp.concatenate([pack[:1, :64], probes_cov], axis=0)
    w1, cov1 = hessian(v1, whole1, c0)
    bx = b + (zero,)

    v2, pack = precondition(w1, packed_with(cov1, dot(bx, v1), dot(v1, w1)), co)
    whole2, pack = all_nodes(v2, pack)
    hcov1 = pack[:, :64] + prior_prec[None] * c0
    norm0 = pack[:, 64] + jnp.sum(c0 * c0, axis=1)
    curve0 = pack[:, 65] + jnp.sum(c0 * hcov1, axis=1)
    step0 = norm0 / curve0
    r1 = mix(bx, -step0, w1)
    z1 = mix(v1, -step0, v2)
    z1whole = whole1 - step0[:, None, None] * whole2
    r1cov = c0 - step0[:, None] * hcov1
    w2, cov2 = hessian(z1, z1whole, r1cov)

    v3, pack = precondition(w2, packed_with(cov2, dot(r1, z1), dot(z1, w2), dot(z1, w1)), co)
    whole3, pack = all_nodes(v3, pack)
    hcov2 = pack[:, :64] + prior_prec[None] * r1cov
    norm1 = pack[:, 64] + jnp.sum(r1cov * r1cov, axis=1)
    beta1 = norm1 / norm0
    curve1 = (
        pack[:, 65]
        + jnp.sum(r1cov * hcov2, axis=1)
        + 2.0 * beta1 * (pack[:, 66] + jnp.sum(r1cov * hcov1, axis=1))
        + beta1 * beta1 * curve0
    )
    step1 = norm1 / curve1
    hp1 = mix(w2, beta1, w1)
    mhp1 = mix(v3, beta1, v2)
    r2 = mix(r1, -step1, hp1)
    z2 = mix(z1, -step1, mhp1)
    z2whole = z1whole - step1[:, None, None] * (whole3 + beta1[:, None, None] * whole2)
    p1 = mix(z1, beta1, v1)
    hp1cov = hcov2 + beta1[:, None] * hcov1
    r2cov = r1cov - step1[:, None] * hp1cov
    p1cov = r1cov + beta1[:, None] * c0

    own_rows, ahead, predictor = product(z2whole, r2cov)
    own = jnp.stack(z2[:2])
    quadratic = jnp.sum(own * (own_rows + 2.0 * ahead), axis=(0, 2)) + jnp.sum(
        slot_weight[None] * predictor * predictor, axis=(1, 2)
    )
    sums = jnp.stack([dot(r2, z2), quadratic, dot(z2, hp1)])
    sums = sums + swapped(sums)
    for axis in ("day_1", "day_0", "blk_0"):
        sums = ring_sum(ring_gather(sums, axis))
    norm2 = sums[0] + jnp.sum(r2cov * r2cov, axis=1)
    beta2 = norm2 / norm1
    curve2 = (
        sums[1]
        + jnp.sum(r2cov * prior_prec[None] * r2cov, axis=1)
        + 2.0 * beta2 * (sums[2] + jnp.sum(r2cov * hp1cov, axis=1))
        + beta2 * beta2 * curve1
    )
    step2 = norm2 / curve2

    def solved(p0, p1, z2):
        scale0, scale1, scale2 = (s.reshape((16,) + (1,) * (p0.ndim - 1)) for s in (step0, step1 + step2 * beta2, step2))
        return scale0 * p0 + scale1 * p1 + scale2 * z2

    field = jnp.stack([solved(v1[t], p1[t], z2[t]) for t in range(2)], axis=1)
    return field, solved(c0, p1cov, r2cov)


def solution(mesh):
    split = Mesh(mesh.devices.reshape(4, 4, 4, 2), ("day_0", "day_1", "blk_0", "blk_1"))
    in_specs = (
        P(DAY, BLK, None),
        P(DAY, BLK, None),
        P(DAY, BLK),
        P(DAY),
        P(DAY, BLK),
        P(None, DAY, BLK),
        P(DAY, BLK),
        P(DAY, BLK),
        P(None, DAY, BLK),
        P(),
        P(),
        P(None, DAY, BLK),
        P(),
    )
    out_specs = (P(None, DAY, BLK), P())
    return jax.shard_map(
        on_device, mesh=split, in_specs=in_specs, out_specs=out_specs, check_vma=False
    )
```

```python
import jax
import jax.numpy as jnp
from jax import lax
from jax.experimental import pallas as pl
from jax.experimental.pallas import tpu as pltpu
from jax.sharding import Mesh
from jax.sharding import PartitionSpec as P

DAY = ("day_0", "day_1")
BLK = ("blk_0", "blk_1")
F32 = jnp.float32
BF16 = jnp.bfloat16
NT = (((1,), (1,)), ((), ()))
NN = (((1,), (0,)), ((), ()))


def shift(value, axis, distance):
    size = lax.axis_size(axis)
    return lax.ppermute(value, axis, [(i, (i + distance) % size) for i in range(size)])


def swapped(value):
    return lax.ppermute(value, "blk_1", [(0, 1), (1, 0)])


def ring_gather(value, axis):
    return [value] + [shift(value, axis, k) for k in (1, 2, 3)]


def ring_sum(relative):
    return (relative[0] + relative[2]) + (relative[1] + relative[3])


def scattered_pieces(kept, sent):
    row = lax.axis_index("blk_0")
    half = kept + swapped(sent)
    pieces = [lax.dynamic_index_in_dim(half, (row + k) % 4, 0, False) for k in range(4)]
    return [pieces[0]] + [shift(pieces[k], "blk_0", k) for k in (1, 2, 3)]


def gather_nodes(message):
    column = jnp.stack(ring_gather(message, "blk_0"))
    return column, swapped(column)


def chain_coefficients(decay, dominant):
    group, place = lax.axis_index("day_0"), lax.axis_index("day_1")
    me = 4 * group + place
    decays = decay.reshape(32, 320)
    dominants = dominant.reshape(32, 320)
    gain = [None] * 33
    gain[32] = jnp.zeros_like(decays[0])
    follow = jnp.concatenate([decays[1:], jnp.zeros((1, 320), jnp.float32)])
    for day in range(31, -1, -1):
        gain[day] = 1.0 / dominants[day] + follow[day] * follow[day] * gain[day + 1]
    gains = jnp.stack(gain)
    follows = jnp.concatenate([decays, jnp.zeros((1, 320), jnp.float32)])
    days = lax.dynamic_slice_in_dim(gains, 2 * me, 3, 0)
    decs = lax.dynamic_slice_in_dim(follows, 2 * me, 3, 0)
    step = (follows[1::2] * follows[2::2]).reshape(4, 4, 320)
    mine = lax.dynamic_index_in_dim(step, group, 0, False)
    one, zero = jnp.ones((320,), jnp.float32), jnp.zeros((320,), jnp.float32)
    index = jnp.arange(4)[:, None]

    def product(factors, low, high):
        kept = jnp.where((index >= low) & (index < high), factors, 1.0)
        return kept[0] * kept[1] * kept[2] * kept[3]

    whole = jnp.prod(step, axis=1)
    local_f, local_b, total_f, total_b, far = [], [], [], [], []
    for k in range(4):
        source = (place - k) % 4
        total_f.append(product(mine, source + 1, 4))
        total_b.append(product(mine, 0, source))
        if k:
            local_f.append(jnp.where(source < place, product(mine, source + 1, place), zero))
            local_b.append(jnp.where(source > place, product(mine, place + 1, source), zero))
            origin = (group - k) % 4
            low, high = jnp.minimum(origin, group) + 1, jnp.maximum(origin, group)
            far.append(product(whole, low, high))
    rows = [days[0], days[1], days[2], decs[0], decs[1], decs[2]]
    rows += local_f + local_b + total_f + total_b + far
    rows += [product(mine, 0, place), product(mine, place + 1, 4)]
    return jnp.stack(rows)


def ring_message(w, co):
    g0, g1, gg, d1, dg = co[0:1], co[1:2], co[2:3], co[4:5], co[5:6]
    ahead = dg * (w[1] + d1 * w[0]) + w[2]
    behind = g0 * w[0] + d1 * (g1 * w[1] + dg * gg * w[2])
    return ahead, behind


def weighted(co, first, values):
    return sum(co[first + k : first + k + 1] * value for k, value in enumerate(values))


def middle_kernel(m0, m1, m2, m3, co, out1, out2, out3, local):
    messages = (m0, m1, m2, m3)
    fs = [m[:, :320] for m in messages]
    bs = [m[:, 320:640] for m in messages]
    pack = ring_sum([m[:, 640:] for m in messages])
    local[0] = weighted(co, 6, fs[1:])
    local[1] = weighted(co, 9, bs[1:])
    local[2] = jnp.zeros((16, 320), F32)
    local[2, :, :128] = pack
    total_f = weighted(co, 12, fs)
    total_b = weighted(co, 16, bs)
    group = lax.axis_index("day_0")
    for k, out in ((1, out1), (2, out2), (3, out3)):
        out[:, :320] = jnp.where(group + k < 4, total_f, total_b)
        out[:, 320:] = pack


def last_kernel(r1, r2, r3, local, w, co, v, message):
    group = lax.axis_index("day_0")
    g0, g1, gg, d1, dg = co[0:1], co[1:2], co[2:3], co[4:5], co[5:6]
    far_f, far_b = jnp.zeros((16, 320), F32), jnp.zeros((16, 320), F32)
    packs = [local[2, :, :128]]
    for k, r in ((1, r1), (2, r2), (3, r3)):
        packs.append(r[:, 320:])
        value = co[19 + k : 20 + k] * r[:, :320]
        far_f = far_f + jnp.where(group >= k, value, 0.0)
        far_b = far_b + jnp.where(group >= k, 0.0, value)
    come_f = local[0] + co[23:24] * far_f
    come_b = local[1] + co[24:25] * far_b
    l0 = w[0] + come_f
    l1 = w[1] + d1 * l0
    u1 = dg * (come_b + gg * w[2])
    u0 = d1 * (g1 * w[1] + u1)
    days = (g0 * l0 + u0, g1 * l1 + u1, gg * (dg * l1 + w[2]) + come_b)
    for day, value in enumerate(days):
        v[day] = value
        message[:, day * 320 : day * 320 + 320] = value
    message[:, 960:] = ring_sum(packs)


def precondition(w, message, co):
    pieces = ring_gather(message, "day_1")
    one = shaped(16, 448)
    *out, local = call(
        middle_kernel, "middle", (one, one, one, shaped(3, 16, 320)), [VMEM_BLOCK] * 5, *pieces, co
    )
    got = [shift(out[k - 1], "day_0", k) for k in (1, 2, 3)]
    return call(
        last_kernel, "last", (shaped(3, 16, 320), shaped(16, 1088)), [VMEM_BLOCK] * 6, *got, local, w, co
    )


def halves(value):
    high = value.astype(BF16)
    return high, (value - high.astype(F32)).astype(BF16)


def stacked_halves(value):
    return jnp.concatenate(halves(value), axis=0)


def matmul(first, second, dims):
    return lax.dot_general(first, second, dims, preferred_element_type=F32)


def times_rows(value, pair):
    n = pair.shape[0] // 2
    out = matmul(stacked_halves(value), pair, NT)
    return (out[:16, :n] + out[16:, :n]) + (out[:16, n:] + out[16:, n:])


def times_matrix(value, pair):
    high, low = halves(value)
    both = jnp.concatenate(
        [jnp.concatenate([high, high], axis=1), jnp.concatenate([low, low], axis=1)], axis=0
    )
    out = matmul(both, pair, NN)
    return out[:16] + out[16:]


VMEM_BLOCK = pl.BlockSpec(memory_space=pltpu.VMEM)
SMEM_BLOCK = pl.BlockSpec(memory_space=pltpu.SMEM)
HBM_BLOCK = pl.BlockSpec(memory_space=pltpu.HBM)


def shaped(*shape):
    return jax.ShapeDtypeStruct(shape, F32)


def call(kernel, name, outs, in_specs, *operands, scratch=(), limit=16):
    return pl.pallas_call(
        kernel,
        out_shape=outs,
        in_specs=in_specs,
        out_specs=jax.tree.map(lambda _: VMEM_BLOCK, outs),
        scratch_shapes=scratch,
        compiler_params=pltpu.CompilerParams(vmem_limit_bytes=limit << 20),
        name=name,
    )(*operands)


CHUNK = 80


def split_kernel(diag, off, diag_pair, off_pair, buffer, sem):
    jobs = [
        (source, target, day, row)
        for source, target in ((off, off_pair), (diag, diag_pair))
        for day in range(2)
        for row in range(0, 320, CHUNK)
    ]

    def fetch(index):
        source, _, day, row = jobs[index]
        slot = index % 3
        return pltpu.make_async_copy(source.at[day, pl.ds(row, CHUNK)], buffer.at[slot], sem.at[slot])

    fetch(0).start()
    fetch(1).start()
    for index, (_, target, day, row) in enumerate(jobs):
        if index + 2 < len(jobs):
            fetch(index + 2).start()
        fetch(index).wait()
        high, low = halves(buffer[index % 3])
        target[day, pl.ds(row, CHUNK)] = high
        target[day, pl.ds(320 + row, CHUNK)] = low


def split_blocks(diag, off):
    pair = pltpu.VMEM((2, 640, 2560), BF16)
    return call(
        split_kernel,
        "split_blocks",
        (pair, pair),
        [HBM_BLOCK, HBM_BLOCK],
        diag,
        off,
        scratch=[pltpu.VMEM((3, CHUNK, 2560), F32), pltpu.SemaphoreType.DMA((3,))],
    )


def behind_kernel(off_pair, own, out):
    for day in range(2):
        out[day] = times_matrix(own[day], off_pair[day])


def behind_terms(off_pair, own):
    return call(behind_kernel, "behind_terms", shaped(2, 16, 2560), [VMEM_BLOCK] * 2, off_pair, own)


def rows_into(diag_pair, off_pair, whole, out):
    for day in range(2):
        out[day] = times_rows(whole[day], diag_pair[day]) + times_rows(whole[day + 1], off_pair[day])


def lanes(*values):
    lane = lax.broadcasted_iota(jnp.int32, (16, 64), 1)
    out = jnp.zeros((16, 64), F32)
    for index, value in enumerate(values):
        out = jnp.where(lane == index, value, out)
    return out


def first_rows_kernel(diag_pair, off_pair, whole, bx, v1, out, dots):
    rows_into(diag_pair, off_pair, whole, out)
    dots[...] = lanes(sum(row_sum(bx[day] * v1[day]) for day in range(2)))


def first_rows(*operands):
    return call(
        first_rows_kernel, "first_rows", (shaped(2, 16, 320), shaped(16, 64)), [VMEM_BLOCK] * 5, *operands
    )


def second_rows_kernel(diag_pair, off_pair, whole, bx, v1, v2, w1, scalars, out, dots, r1, z1):
    rows_into(diag_pair, off_pair, whole, out)
    step0 = scalars[:, 0:1]
    norm = cross = jnp.zeros((16, 1), F32)
    for day in range(3):
        z = v1[day] - step0 * v2[day]
        r = (bx[day] if day < 2 else 0.0) - step0 * w1[day]
        z1[day] = z
        r1[day] = r
        norm = norm + row_sum(r * z)
        cross = cross + row_sum(z * w1[day])
    dots[...] = lanes(norm, 0.0, cross)


def second_rows(*operands):
    own = shaped(3, 16, 320)
    return call(
        second_rows_kernel,
        "second_rows",
        (shaped(2, 16, 320), shaped(16, 64), own, own),
        [VMEM_BLOCK] * 8,
        *operands,
    )


def start_kernel(p0, p1, p2, p3, probes, grad_cov, co, bx, w, message):
    grad = ring_sum([p0[...], p1[...], p2[...], p3[...]])
    for day in range(2):
        bx[day, 0:1] = grad[day : day + 1]
        bx[day, 1:16] = probes[:, day, :]
        w[day] = bx[day]
    w[2] = jnp.zeros((16, 320), F32)
    ahead, behind = ring_message(w, co)
    message[:, :320] = ahead
    message[:, 320:640] = behind
    message[:, 640:] = jnp.zeros((16, 128), F32)
    message[0:1, 640:704] = grad_cov[...]


def start_stage(*operands):
    return call(
        start_kernel,
        "start_stage",
        (shaped(2, 16, 320), shaped(3, 16, 320), shaped(16, 768)),
        [VMEM_BLOCK] * 7,
        *operands,
    )


def image_kernel(p0, p1, p2, p3, rows, vector, cov_terms, dots, co, w, message):
    pieces = (p0, p1, p2, p3)
    total = jnp.zeros((16, 1), F32)
    for day in range(3):
        value = ring_sum([p[day] for p in pieces])
        if day < 2:
            value = value + rows[day]
        w[day] = value
        total = total + row_sum(vector[day] * value)
    ahead, behind = ring_message(w, co)
    message[:, :320] = ahead
    message[:, 320:640] = behind
    message[:, 640:704] = cov_terms[...]
    message[:, 704:] = dots[...] + lanes(0.0, total)


def image_stage(*operands):
    return call(
        image_kernel,
        "image_stage",
        (shaped(3, 16, 320), shaped(16, 768)),
        [VMEM_BLOCK] * 9,
        *operands,
    )


def assemble(mine, other, whole):
    row, core = lax.axis_index("blk_0"), lax.axis_index("blk_1")
    packs = []
    for k in range(4):
        at = pl.multiple_of(lax.rem(row + (4 - k), 4) * 640, 128)
        for day in range(3):
            a = mine[k, :, day * 320 : day * 320 + 320]
            b = other[k, :, day * 320 : day * 320 + 320]
            first = jnp.where(core == 0, a, b)
            second = jnp.where(core == 0, b, a)
            whole[day, :, pl.ds(at, 640)] = jnp.concatenate([first, second], axis=1)
        packs.append(mine[k, :, 960:1088] + other[k, :, 960:1088])
    return (packs[0] + packs[2]) + (packs[1] + packs[3])


def scatter_parts(obs0, obs1, behind0, behind1, kept, sent):
    core = lax.axis_index("blk_1")
    last = lax.axis_index("day_0") * 4 + lax.axis_index("day_1") == 15
    days = (obs0, obs1 + behind0, jnp.where(last, 0.0, behind1))
    for day, part in enumerate(days):
        for row in range(4):
            first = part[:, row * 640 : row * 640 + 320]
            second = part[:, row * 640 + 320 : row * 640 + 640]
            kept[row, day] = jnp.where(core == 0, first, second)
            sent[row, day] = jnp.where(core == 0, second, first)


def observe(whole, cov, spread, covariates, weight):
    result = []
    for day in range(2):
        out = matmul(stacked_halves(whole[day]), spread[day], NN)
        out = (out[:16, :128] + out[16:, :128]) + (out[:16, 128:] + out[16:, 128:])
        predictor = out + times_matrix(cov, stacked_halves(covariates[day]))
        result.append((predictor, weight[day : day + 1] * predictor))
    return result


def spread_out(value, pair):
    high, low = halves(value)
    both = jnp.concatenate(
        [jnp.concatenate([high, high], axis=1), jnp.concatenate([low, low], axis=1)], axis=0
    )
    out = matmul(both, pair, NT)
    return out[:16] + out[16:]


def observe_back(observed, behind, spread, covariates, kept, sent, cov_terms):
    weights = [pair[1] for pair in observed]
    obs = [spread_out(weights[day], spread[day]) for day in range(2)]
    scatter_parts(obs[0], obs[1], behind[0], behind[1], kept, sent)
    cov_terms[...] = sum(times_rows(weights[day], stacked_halves(covariates[day])) for day in range(2))


def row_sum(value):
    return jnp.sum(value, axis=1, keepdims=True)


PARTS = (shaped(4, 3, 16, 320), shaped(4, 3, 16, 320), shaped(16, 64))


def first_kernel(mine, other, probes_cov, spread, covariates, weight, behind, kept, sent, cov_terms, whole, cov):
    pack = assemble(mine, other, whole)
    cov[...] = jnp.where(
        lax.broadcasted_iota(jnp.int32, (16, 64), 0) == 0, pack[:, :64], probes_cov[...]
    )
    observed = observe(whole, cov[...], spread, covariates, weight)
    observe_back(observed, behind, spread, covariates, kept, sent, cov_terms)


def first_stage(mine, other, probes_cov, spread, covariates, weight, behind):
    return call(
        first_kernel,
        "first_stage",
        PARTS + (shaped(3, 16, 2560), shaped(16, 64)),
        [VMEM_BLOCK] * 7,
        mine, other, probes_cov, spread, covariates, weight, behind,
    )


def second_kernel(
    mine, other, whole1, c0, prior, spread, covariates, weight, behind1, behind2,
    kept, sent, cov_terms, whole2, whole, cov, hcov, scalars, behind,
):
    pack = assemble(mine, other, whole2)
    hcov1 = pack[:, :64] + prior[...] * c0[...]
    norm0 = pack[:, 64:65] + row_sum(c0[...] * c0[...])
    curve0 = pack[:, 65:66] + row_sum(c0[...] * hcov1)
    step0 = norm0 / curve0
    for day in range(3):
        whole[day] = whole1[day] - step0 * whole2[day]
    for day in range(2):
        behind[day] = behind1[day] - step0 * behind2[day]
    cov[...] = c0[...] - step0 * hcov1
    hcov[...] = hcov1
    lane = lax.broadcasted_iota(jnp.int32, (16, 128), 1)
    scalars[...] = jnp.where(lane == 0, step0, jnp.where(lane == 1, norm0, curve0))
    observed = observe(whole, cov[...], spread, covariates, weight)
    observe_back(observed, behind, spread, covariates, kept, sent, cov_terms)


def second_stage(mine, other, whole1, c0, prior, spread, covariates, weight, behind1, behind2):
    whole = shaped(3, 16, 2560)
    return call(
        second_kernel,
        "second_stage",
        PARTS + (whole, whole, shaped(16, 64), shaped(16, 64), shaped(16, 128)),
        [VMEM_BLOCK] * 10,
        mine, other, whole1, c0, prior, spread, covariates, weight, behind1, behind2,
        scratch=[pltpu.VMEM((2, 16, 2560), F32)],
    )


def third_kernel(
    mine, other, whole2, z1whole, scalars, c0, z1cov, hcov1, prior, spread, covariates, weight,
    diag_pair, off_pair, r1, z1, w1, w2, v1, v2, v3,
    sums, z2, p1, scalars_out, covs, whole,
):
    pack = assemble(mine, other, whole)
    norm0, curve0 = scalars[:, 1:2], scalars[:, 2:3]
    hcov2 = pack[:, :64] + prior[...] * z1cov[...]
    norm1 = pack[:, 64:65] + row_sum(z1cov[...] * z1cov[...])
    beta1 = norm1 / norm0
    curve1 = (
        pack[:, 65:66]
        + row_sum(z1cov[...] * hcov2)
        + 2.0 * beta1 * (pack[:, 66:67] + row_sum(z1cov[...] * hcov1[...]))
        + beta1 * beta1 * curve0
    )
    step1 = norm1 / curve1
    hp1cov = hcov2 + beta1 * hcov1[...]
    r2cov = z1cov[...] - step1 * hp1cov
    covs[0] = r2cov
    covs[1] = z1cov[...] + beta1 * c0[...]
    own_norm = jnp.zeros((16, 1), F32)
    cross = jnp.zeros((16, 1), F32)
    for day in range(3):
        hp1 = w2[day] + beta1 * w1[day]
        r2 = r1[day] - step1 * hp1
        z2day = z1[day] - step1 * (v3[day] + beta1 * v2[day])
        own_norm = own_norm + row_sum(r2 * z2day)
        cross = cross + row_sum(z2day * hp1)
        if day < 2:
            z2[day] = z2day
            p1[day] = z1[day] + beta1 * v1[day]
        whole[day] = z1whole[day] - step1 * (whole[day] + beta1 * whole2[day])
    observed = observe(whole, r2cov, spread, covariates, weight)
    quadratic = sum(row_sum(predictor * weighted) for predictor, weighted in observed)
    for day in range(2):
        rows = times_rows(whole[day], diag_pair[day]) + 2.0 * times_rows(whole[day + 1], off_pair[day])
        quadratic = quadratic + row_sum(z2[day] * rows)
    lane = lax.broadcasted_iota(jnp.int32, (16, 128), 1)
    sub = lax.broadcasted_iota(jnp.int32, (16, 128), 0)
    line = jnp.zeros((16, 128), F32)
    for index, value in enumerate((own_norm, quadratic, cross)):
        line = jnp.where(lane == sub + 16 * index, value, line)
    sums[...] = jnp.broadcast_to(jnp.sum(line, axis=0, keepdims=True), (128, 128))
    norm2cov = row_sum(r2cov * r2cov)
    quadcov = row_sum(r2cov * prior[...] * r2cov)
    crosscov = row_sum(r2cov * hp1cov)
    values = (scalars[:, 0:1], step1, norm1, curve1, norm2cov, quadcov, crosscov)
    out = jnp.zeros((16, 128), F32)
    for index, value in enumerate(values):
        out = jnp.where(lane == index, value, out)
    scalars_out[...] = out


def third_stage(*operands):
    own = shaped(2, 16, 320)
    return call(
        third_kernel,
        "third_stage",
        (shaped(128, 128), own, own, shaped(16, 128), shaped(2, 16, 64)),
        [VMEM_BLOCK] * len(operands),
        *operands,
        scratch=[pltpu.VMEM((3, 16, 2560), F32)],
    )


def final_kernel(sums, scalars, v1, p1, z2, c0, covs, field, cov):
    step0, step1, norm1, curve1, norm2cov, quadcov, crosscov = (
        scalars[:, i : i + 1] for i in range(7)
    )
    lane = lax.broadcasted_iota(jnp.int32, (16, 128), 1)
    sub = lax.broadcasted_iota(jnp.int32, (16, 128), 0)
    line = jnp.sum(sums[...], axis=0, keepdims=True)
    own_norm, quadratic, cross = (
        row_sum(jnp.where(lane == sub + 16 * index, line, 0.0)) for index in range(3)
    )
    norm2 = own_norm + norm2cov
    beta2 = norm2 / norm1
    curve2 = (
        quadratic + quadcov + 2.0 * beta2 * (cross + crosscov) + beta2 * beta2 * curve1
    )
    step2 = norm2 / curve2
    middle = step1 + step2 * beta2
    for day in range(2):
        field[:, day, :] = step0 * v1[day] + middle * p1[day] + step2 * z2[day]
    cov[...] = step0 * c0[...] + middle * covs[1] + step2 * covs[0]


def final_stage(*operands):
    return call(
        final_kernel,
        "final_stage",
        (shaped(16, 2, 320), shaped(16, 64)),
        [VMEM_BLOCK] * len(operands),
        *operands,
    )


def setup_kernel(count, vertices, bary, prec, value, covariates, spread, weight, kept, sent, grad_cov):
    core = lax.axis_index("blk_1")
    slot_start = (lax.axis_index("blk_0") * 2 + core) * 128
    cov_sum = jnp.zeros((1, 64), F32)
    for day in range(2):
        shares = [bary[k, day : day + 1, :] for k in range(3)]
        total = shares[0] + shares[1] + shares[2]
        nodes = lax.broadcasted_iota(jnp.int32, (2560, 128), 0)
        dense = jnp.zeros((2560, 128), F32)
        for k in range(3):
            dense = dense + jnp.where(nodes == vertices[k, day : day + 1, :], shares[k] / total, 0.0)
        high, low = halves(dense)
        spread[day, :, :128] = high
        spread[day, :, 128:] = low
        slot = lax.broadcasted_iota(jnp.int32, (1, 128), 1) + slot_start
        slot_weight = jnp.where(slot < count[day], prec[day : day + 1], 0.0)
        weight[day : day + 1] = slot_weight
        weighted_value = jnp.broadcast_to(slot_weight * value[day : day + 1], (16, 128))
        grad = spread_out(weighted_value, spread[day])[:1]
        for row in range(4):
            first = grad[:, row * 640 : row * 640 + 320]
            second = grad[:, row * 640 + 320 : row * 640 + 640]
            kept[row, day : day + 1] = jnp.where(core == 0, first, second)
            sent[row, day : day + 1] = jnp.where(core == 0, second, first)
        cov_sum = cov_sum + times_rows(weighted_value, stacked_halves(covariates[day]))[:1]
    grad_cov[...] = cov_sum


def setup_stage(*operands):
    return call(
        setup_kernel,
        "setup_stage",
        (
            pltpu.VMEM((2, 2560, 256), BF16), shaped(2, 128), shaped(4, 2, 320), shaped(4, 2, 320),
            shaped(1, 64),
        ),
        [SMEM_BLOCK] + [VMEM_BLOCK] * (len(operands) - 1),
        *operands,
    )


def on_device(
    diag_blocks,
    off_blocks,
    leakage,
    obs_count,
    obs_triangle,
    obs_bary,
    obs_prec,
    obs_value,
    covariates,
    triangles,
    prior_prec,
    probes,
    probes_cov,
):
    row_start = lax.axis_index(BLK) * 320
    square = lax.dynamic_slice_in_dim(diag_blocks, row_start, 320, 2)
    rows = lax.broadcasted_iota(jnp.int32, (2, 320, 320), 1)
    columns = lax.broadcasted_iota(jnp.int32, (2, 320, 320), 2)
    dominant = jnp.sum(jnp.where(rows == columns, square, 0.0), axis=1)
    both = jnp.concatenate([1.0 - leakage, dominant])
    every = lax.all_to_all(jnp.broadcast_to(both, (16, 4, 320)), DAY, 0, 0, tiled=True)
    co = chain_coefficients(every[:, :2], every[:, 2:])

    vertices = triangles[:, obs_triangle]
    covs = jnp.moveaxis(covariates, 1, 0)
    spread, weight, kept, sent, grad_cov = setup_stage(
        obs_count, vertices, obs_bary, obs_prec, obs_value, covs
    )
    diag_pair, off_pair = split_blocks(diag_blocks, off_blocks)
    bx, w0, message = start_stage(*scattered_pieces(kept, sent), probes, grad_cov, co)
    prior = prior_prec[None]
    padded_cov = jnp.pad(probes_cov, ((1, 0), (0, 0)))

    v1, message = precondition(w0, message, co)
    behind1 = behind_terms(off_pair, v1)
    kept, sent, cov1, whole1, c0 = first_stage(
        *gather_nodes(message), padded_cov, spread, covs, weight, behind1
    )
    image, dots = first_rows(diag_pair, off_pair, whole1, bx, v1)
    w1, message = image_stage(*scattered_pieces(kept, sent), image, v1, cov1, dots, co)

    v2, message = precondition(w1, message, co)
    behind2 = behind_terms(off_pair, v2)
    kept, sent, cov2, whole2, z1whole, z1cov, hcov1, scalars = second_stage(
        *gather_nodes(message), whole1, c0, prior, spread, covs, weight, behind1, behind2
    )
    image, dots, r1, z1 = second_rows(diag_pair, off_pair, z1whole, bx, v1, v2, w1, scalars)
    w2, message = image_stage(*scattered_pieces(kept, sent), image, z1, cov2, dots, co)

    v3, message = precondition(w2, message, co)
    sums, z2, p1, scalars, covs2 = third_stage(
        *gather_nodes(message), whole2, z1whole, scalars, c0, z1cov, hcov1, prior, spread, covs, weight,
        diag_pair, off_pair, r1, z1, w1, w2, v1, v2, v3,
    )
    sums = lax.all_to_all(sums, DAY + BLK, 0, 0, tiled=True)
    return final_stage(sums, scalars, v1, p1, z2, c0, covs2)


def solution(mesh):
    split = Mesh(mesh.devices.reshape(4, 4, 4, 2), ("day_0", "day_1", "blk_0", "blk_1"))
    in_specs = (
        P(DAY, BLK, None),
        P(DAY, BLK, None),
        P(DAY, BLK),
        P(DAY),
        P(DAY, BLK),
        P(None, DAY, BLK),
        P(DAY, BLK),
        P(DAY, BLK),
        P(None, DAY, BLK),
        P(),
        P(),
        P(None, DAY, BLK),
        P(),
    )
    out_specs = (P(None, DAY, BLK), P())
    return jax.shard_map(
        on_device, mesh=split, in_specs=in_specs, out_specs=out_specs, check_vma=False
    )
```

```python
import functools

import jax
import jax.numpy as jnp
from jax import lax
from jax.experimental import pallas as pl
from jax.experimental.pallas import tpu as pltpu
from jax.sharding import Mesh
from jax.sharding import PartitionSpec as P

DAY = ("day_0", "day_1")
BLK = ("blk_0", "blk_1")
F32 = jnp.float32
BF16 = jnp.bfloat16
NT = (((1,), (1,)), ((), ()))
NN = (((1,), (0,)), ((), ()))


def shift(value, axis, distance):
    size = lax.axis_size(axis)
    return lax.ppermute(value, axis, [(i, (i + distance) % size) for i in range(size)])


def swapped(value):
    return lax.ppermute(value, "blk_1", [(0, 1), (1, 0)])


def ring_gather(value, axis):
    return [value] + [shift(value, axis, k) for k in (1, 2, 3)]


def ring_sum(relative):
    return (relative[0] + relative[2]) + (relative[1] + relative[3])


def scattered_pieces(kept, sent):
    row = lax.axis_index("blk_0")
    half = kept + swapped(sent)
    pieces = [lax.dynamic_index_in_dim(half, (row + k) % 4, 0, False) for k in range(4)]
    return [pieces[0]] + [shift(pieces[k], "blk_0", k) for k in (1, 2, 3)]


def gather_nodes(message, ready):
    column, ready = lax.optimization_barrier((jnp.stack(ring_gather(message, "blk_0")), ready))
    return (column, swapped(column)), ready


def ring_message(w, co):
    g0, g1, gg, d1, dg = co[0:1], co[1:2], co[2:3], co[4:5], co[5:6]
    ahead = dg * (w[1] + d1 * w[0]) + w[2]
    behind = g0 * w[0] + d1 * (g1 * w[1] + dg * gg * w[2])
    return ahead, behind


def weighted(co, first, values):
    return sum(co[first + k : first + k + 1] * value for k, value in enumerate(values))


def middle_kernel(m0, m1, m2, m3, co, *refs):
    out1, out2, out3, local = refs[-4:]
    middle_body(m0, m1, m2, m3, co, out1, out2, out3, local)


def middle_body(m0, m1, m2, m3, co, out1, out2, out3, local):
    messages = (m0, m1, m2, m3)
    fs = [m[:, :320] for m in messages]
    bs = [m[:, 320:640] for m in messages]
    pack = ring_sum([m[:, 640:] for m in messages])
    local[0] = weighted(co, 6, fs[1:])
    local[1] = weighted(co, 9, bs[1:])
    local[2] = jnp.zeros((16, 320), F32)
    local[2, :, :128] = pack
    total_f = weighted(co, 12, fs)
    total_b = weighted(co, 16, bs)
    group = lax.axis_index("day_0")
    for k, out in ((1, out1), (2, out2), (3, out3)):
        out[:, :320] = jnp.where(group + k < 4, total_f, total_b)
        out[:, 320:] = pack


def last_kernel(r1, r2, r3, local, w, co, *refs):
    last_body(r1, r2, r3, local, w, co, *refs[-2:])


def last_body(r1, r2, r3, local, w, co, v, message):
    group = lax.axis_index("day_0")
    g0, g1, gg, d1, dg = co[0:1], co[1:2], co[2:3], co[4:5], co[5:6]
    far_f, far_b = jnp.zeros((16, 320), F32), jnp.zeros((16, 320), F32)
    packs = [local[2, :, :128]]
    for k, r in ((1, r1), (2, r2), (3, r3)):
        packs.append(r[:, 320:])
        value = co[19 + k : 20 + k] * r[:, :320]
        far_f = far_f + jnp.where(group >= k, value, 0.0)
        far_b = far_b + jnp.where(group >= k, 0.0, value)
    come_f = local[0] + co[23:24] * far_f
    come_b = local[1] + co[24:25] * far_b
    l0 = w[0] + come_f
    l1 = w[1] + d1 * l0
    u1 = dg * (come_b + gg * w[2])
    u0 = d1 * (g1 * w[1] + u1)
    days = (g0 * l0 + u0, g1 * l1 + u1, gg * (dg * l1 + w[2]) + come_b)
    for day, value in enumerate(days):
        v[day] = value
        message[:, day * 320 : day * 320 + 320] = value
    message[:, 960:] = ring_sum(packs)


def precondition(w, message, co, early=(), late=()):
    pieces = ring_gather(message, "day_1")
    one = shaped(16, 448)
    *out, local = call(
        middle_kernel, "middle", (one, one, one, shaped(3, 16, 320)),
        [VMEM_BLOCK] * 5 + [ANY_BLOCK] * len(early), *pieces, co, *early,
    )
    got = [shift(out[k - 1], "day_0", k) for k in (1, 2, 3)]
    return call(
        last_kernel, "last", (shaped(3, 16, 320), shaped(16, 1088)),
        [VMEM_BLOCK] * 6 + [ANY_BLOCK] * len(late), *got, local, w, co, *late,
    )


def halves(value):
    high = value.astype(BF16)
    return high, (value - high.astype(F32)).astype(BF16)


def stacked_halves(value):
    return jnp.concatenate(halves(value), axis=0)


def matmul(first, second, dims):
    return lax.dot_general(first, second, dims, preferred_element_type=F32)


def times_rows(value, pair):
    n = pair.shape[0] // 2
    out = matmul(stacked_halves(value), pair, NT)
    return (out[:16, :n] + out[16:, :n]) + (out[:16, n:] + out[16:, n:])


def times_matrix(value, pair):
    high, low = halves(value)
    both = jnp.concatenate(
        [jnp.concatenate([high, high], axis=1), jnp.concatenate([low, low], axis=1)], axis=0
    )
    out = matmul(both, pair, NN)
    return out[:16] + out[16:]


VMEM_BLOCK = pl.BlockSpec(memory_space=pltpu.VMEM)
SMEM_BLOCK = pl.BlockSpec(memory_space=pltpu.SMEM)
ANY_BLOCK = pl.BlockSpec(memory_space=pl.ANY)
HBM_BLOCK = pl.BlockSpec(memory_space=pltpu.HBM)


def shaped(*shape):
    return jax.ShapeDtypeStruct(shape, F32)


def whole_block(operand):
    return pl.BlockSpec(operand.shape, lambda i: (0,) * operand.ndim)


def call(kernel, name, outs, in_specs, *operands, scratch=(), limit=16, grid=()):
    return pl.pallas_call(
        kernel,
        grid=grid,
        out_shape=outs,
        in_specs=in_specs,
        out_specs=jax.tree.map(lambda _: VMEM_BLOCK, outs),
        scratch_shapes=scratch,
        compiler_params=pltpu.CompilerParams(vmem_limit_bytes=limit << 20),
        name=name,
    )(*operands)


CHUNK = 80


def split_kernel(day, source, target, buffer, sem):
    jobs = [(day, row) for row in range(0, 320, CHUNK)]

    def fetch(index):
        day, row = jobs[index]
        slot = index % 3
        return pltpu.make_async_copy(source.at[day, pl.ds(row, CHUNK)], buffer.at[slot], sem.at[slot])

    fetch(0).start()
    fetch(1).start()
    for index, (day, row) in enumerate(jobs):
        if index + 2 < len(jobs):
            fetch(index + 2).start()
        fetch(index).wait()
        high, low = halves(buffer[index % 3])
        target[pl.ds(row, CHUNK)] = high
        target[pl.ds(320 + row, CHUNK)] = low


def split_blocks(blocks, name, day):
    return call(
        functools.partial(split_kernel, day),
        name + str(day),
        pltpu.VMEM((640, 2560), BF16),
        [HBM_BLOCK],
        pltpu.with_memory_space_constraint(blocks, pltpu.HBM),
        scratch=[pltpu.VMEM((3, CHUNK, 2560), F32), pltpu.SemaphoreType.DMA((3,))],
    )


def chain_kernel(every, co, gains, decs, steps):
    group, place = lax.axis_index("day_0"), lax.axis_index("day_1")
    me = 4 * group + place
    zero, one = jnp.zeros((1, 320), F32), jnp.ones((1, 320), F32)
    follow = [every[day // 2, day % 2 : day % 2 + 1, :] for day in range(32)] + [zero]
    gain = zero
    for day in range(32, -1, -1):
        if day < 32:
            inverse = 1.0 / every[day // 2, 2 + day % 2 : 3 + day % 2, :]
            gain = inverse + follow[day + 1] * follow[day + 1] * gain
        gains[day : day + 1] = gain
        decs[day : day + 1] = follow[day]
    for device in range(16):
        steps[device : device + 1] = follow[2 * device + 1] * follow[2 * device + 2]
    mine = [steps[pl.ds(4 * group + device, 1), :] for device in range(4)]
    whole = []
    for other in range(4):
        rows = [steps[4 * other + device : 4 * other + device + 1] for device in range(4)]
        whole.append(rows[0] * rows[1] * rows[2] * rows[3])

    def product(factors, low, high):
        kept = [
            jnp.where((low <= index) & (index < high), factor, one)
            for index, factor in enumerate(factors)
        ]
        return kept[0] * kept[1] * kept[2] * kept[3]

    rows = [gains[pl.ds(2 * me + day, 1), :] for day in range(3)]
    rows += [decs[pl.ds(2 * me + day, 1), :] for day in range(3)]
    local_f, local_b, total_f, total_b, far = [], [], [], [], []
    for k in range(4):
        source = lax.rem(place + (4 - k), 4)
        total_f.append(product(mine, source + 1, 4))
        total_b.append(product(mine, 0, source))
        if k:
            local_f.append(jnp.where(source < place, product(mine, source + 1, place), zero))
            local_b.append(jnp.where(source > place, product(mine, place + 1, source), zero))
            origin = lax.rem(group + (4 - k), 4)
            far.append(product(whole, jnp.minimum(origin, group) + 1, jnp.maximum(origin, group)))
    rows += local_f + local_b + total_f + total_b + far
    rows += [product(mine, 0, place), product(mine, place + 1, 4)]
    for index, row in enumerate(rows):
        co[index : index + 1] = row


def chain_coefficients(every):
    return call(
        chain_kernel,
        "chain",
        shaped(25, 320),
        [VMEM_BLOCK],
        every,
        scratch=[pltpu.VMEM((40, 320), F32), pltpu.VMEM((40, 320), F32), pltpu.VMEM((16, 320), F32)],
    )


def own_terms_kernel(a0, a1, o0, o1, own, out):
    out[0] = times_matrix(own[0], a0[...])
    out[1] = times_matrix(own[1], a1[...]) + times_matrix(own[0], o0[...])
    out[2] = times_matrix(own[1], o1[...])


def own_terms(pairs, own):
    return call(own_terms_kernel, "own_terms", shaped(3, 16, 2560), [VMEM_BLOCK] * 5, *pairs, own)


def rows_into(pairs, whole, out):
    for day in range(2):
        out[day] = times_rows(whole[day + 1], pairs[day][...])


def lanes(*values):
    lane = lax.broadcasted_iota(jnp.int32, (16, 64), 1)
    out = jnp.zeros((16, 64), F32)
    for index, value in enumerate(values):
        out = jnp.where(lane == index, value, out)
    return out


def first_rows_kernel(o0, o1, whole, bx, v1, out, dots):
    rows_into((o0, o1), whole, out)
    dots[...] = lanes(sum(row_sum(bx[day] * v1[day]) for day in range(2)))


def first_rows(*operands):
    return call(
        first_rows_kernel, "first_rows", (shaped(2, 16, 320), shaped(16, 64)), [VMEM_BLOCK] * 5, *operands
    )


def second_rows_kernel(o0, o1, whole, bx, v1, v2, w1, scalars, out, dots, r1, z1):
    rows_into((o0, o1), whole, out)
    step0 = scalars[:, 0:1]
    norm = cross = jnp.zeros((16, 1), F32)
    for day in range(3):
        z = v1[day] - step0 * v2[day]
        r = (bx[day] if day < 2 else 0.0) - step0 * w1[day]
        z1[day] = z
        r1[day] = r
        norm = norm + row_sum(r * z)
        cross = cross + row_sum(z * w1[day])
    dots[...] = lanes(norm, 0.0, cross)


def second_rows(*operands):
    own = shaped(3, 16, 320)
    return call(
        second_rows_kernel,
        "second_rows",
        (shaped(2, 16, 320), shaped(16, 64), own, own),
        [VMEM_BLOCK] * 8,
        *operands,
    )


def start_kernel(p0, p1, p2, p3, probes, grad_cov, co, *refs):
    bx, w, message = refs[-3:]
    grad = ring_sum([p0[...], p1[...], p2[...], p3[...]])
    for day in range(2):
        bx[day, 0:1] = grad[day : day + 1]
        bx[day, 1:16] = probes[:, day, :]
        w[day] = bx[day]
    w[2] = jnp.zeros((16, 320), F32)
    ahead, behind = ring_message(w, co)
    message[:, :320] = ahead
    message[:, 320:640] = behind
    message[:, 640:] = jnp.zeros((16, 128), F32)
    message[0:1, 640:704] = grad_cov[...]


def start_stage(*operands):
    return call(
        start_kernel,
        "start_stage",
        (shaped(2, 16, 320), shaped(3, 16, 320), shaped(16, 768)),
        [VMEM_BLOCK] * 7 + [ANY_BLOCK] * (len(operands) - 7),
        *operands,
    )


def image_kernel(p0, p1, p2, p3, rows, vector, cov_terms, dots, co, w, message):
    pieces = (p0, p1, p2, p3)
    total = jnp.zeros((16, 1), F32)
    for day in range(3):
        value = ring_sum([p[day] for p in pieces])
        if day < 2:
            value = value + rows[day]
        w[day] = value
        total = total + row_sum(vector[day] * value)
    ahead, behind = ring_message(w, co)
    message[:, :320] = ahead
    message[:, 320:640] = behind
    message[:, 640:704] = cov_terms[...]
    message[:, 704:] = dots[...] + lanes(0.0, total)


def image_stage(*operands):
    return call(
        image_kernel,
        "image_stage",
        (shaped(3, 16, 320), shaped(16, 768)),
        [VMEM_BLOCK] * 9,
        *operands,
    )


def assemble(mine, other, whole):
    row, core = lax.axis_index("blk_0"), lax.axis_index("blk_1")
    packs = []
    for k in range(4):
        at = pl.multiple_of(lax.rem(row + (4 - k), 4) * 640, 128)
        for day in range(3):
            a = mine[k, :, day * 320 : day * 320 + 320]
            b = other[k, :, day * 320 : day * 320 + 320]
            first = jnp.where(core == 0, a, b)
            second = jnp.where(core == 0, b, a)
            whole[day, :, pl.ds(at, 640)] = jnp.concatenate([first, second], axis=1)
        packs.append(mine[k, :, 960:1088] + other[k, :, 960:1088])
    return (packs[0] + packs[2]) + (packs[1] + packs[3])


def scatter_parts(obs, terms, kept, sent):
    core = lax.axis_index("blk_1")
    last = lax.axis_index("day_0") * 4 + lax.axis_index("day_1") == 15
    days = (obs[0] + terms[0], obs[1] + terms[1], jnp.where(last, 0.0, terms[2]))
    for day, part in enumerate(days):
        for row in range(4):
            first = part[:, row * 640 : row * 640 + 320]
            second = part[:, row * 640 + 320 : row * 640 + 640]
            kept[row, day] = jnp.where(core == 0, first, second)
            sent[row, day] = jnp.where(core == 0, second, first)


def observe(whole, cov, spread, covariates, weight):
    result = []
    for day in range(2):
        out = matmul(stacked_halves(whole[day]), spread[day], NN)
        out = (out[:16, :128] + out[16:, :128]) + (out[:16, 128:] + out[16:, 128:])
        predictor = out + times_matrix(cov, covariates[day])
        result.append((predictor, weight[day : day + 1] * predictor))
    return result


def spread_out(value, pair):
    high, low = halves(value)
    both = jnp.concatenate(
        [jnp.concatenate([high, high], axis=1), jnp.concatenate([low, low], axis=1)], axis=0
    )
    out = matmul(both, pair, NT)
    return out[:16] + out[16:]


def observe_back(observed, behind, spread, covariates, kept, sent, cov_terms):
    weights = [pair[1] for pair in observed]
    obs = [spread_out(weights[day], spread[day]) for day in range(2)]
    scatter_parts(obs, behind, kept, sent)
    cov_terms[...] = sum(times_rows(weights[day], covariates[day]) for day in range(2))


def row_sum(value):
    return jnp.sum(value, axis=1, keepdims=True)


PARTS = (shaped(4, 3, 16, 320), shaped(4, 3, 16, 320), shaped(16, 64))


def first_kernel(mine, other, probes_cov, spread, covariates, weight, behind, kept, sent, cov_terms, whole, cov):
    pack = assemble(mine, other, whole)
    cov[...] = jnp.where(
        lax.broadcasted_iota(jnp.int32, (16, 64), 0) == 0, pack[:, :64], probes_cov[...]
    )
    observed = observe(whole, cov[...], spread, covariates, weight)
    observe_back(observed, behind, spread, covariates, kept, sent, cov_terms)


def first_stage(mine, other, probes_cov, spread, covariates, weight, behind):
    return call(
        first_kernel,
        "first_stage",
        PARTS + (shaped(3, 16, 2560), shaped(16, 64)),
        [VMEM_BLOCK] * 7,
        mine, other, probes_cov, spread, covariates, weight, behind,
    )


def second_kernel(
    mine, other, whole1, c0, prior, spread, covariates, weight, behind1, behind2,
    kept, sent, cov_terms, whole2, whole, cov, hcov, scalars, behind,
):
    pack = assemble(mine, other, whole2)
    hcov1 = pack[:, :64] + prior[...] * c0[...]
    norm0 = pack[:, 64:65] + row_sum(c0[...] * c0[...])
    curve0 = pack[:, 65:66] + row_sum(c0[...] * hcov1)
    step0 = norm0 / curve0
    for day in range(3):
        whole[day] = whole1[day] - step0 * whole2[day]
    for day in range(3):
        behind[day] = behind1[day] - step0 * behind2[day]
    cov[...] = c0[...] - step0 * hcov1
    hcov[...] = hcov1
    lane = lax.broadcasted_iota(jnp.int32, (16, 128), 1)
    scalars[...] = jnp.where(lane == 0, step0, jnp.where(lane == 1, norm0, curve0))
    observed = observe(whole, cov[...], spread, covariates, weight)
    observe_back(observed, behind, spread, covariates, kept, sent, cov_terms)


def second_stage(mine, other, whole1, c0, prior, spread, covariates, weight, behind1, behind2):
    whole = shaped(3, 16, 2560)
    return call(
        second_kernel,
        "second_stage",
        PARTS + (whole, whole, shaped(16, 64), shaped(16, 64), shaped(16, 128)),
        [VMEM_BLOCK] * 10,
        mine, other, whole1, c0, prior, spread, covariates, weight, behind1, behind2,
        scratch=[pltpu.VMEM((3, 16, 2560), F32)],
    )


def third_kernel(
    mine, other, whole2, z1whole, scalars, c0, z1cov, hcov1, prior, spread, covariates, weight,
    a0, a1, o0, o1, r1, z1, w1, w2, v1, v2, v3,
    sums, z2, p1, scalars_out, covs, whole,
):
    pack = assemble(mine, other, whole)
    norm0, curve0 = scalars[:, 1:2], scalars[:, 2:3]
    hcov2 = pack[:, :64] + prior[...] * z1cov[...]
    norm1 = pack[:, 64:65] + row_sum(z1cov[...] * z1cov[...])
    beta1 = norm1 / norm0
    curve1 = (
        pack[:, 65:66]
        + row_sum(z1cov[...] * hcov2)
        + 2.0 * beta1 * (pack[:, 66:67] + row_sum(z1cov[...] * hcov1[...]))
        + beta1 * beta1 * curve0
    )
    step1 = norm1 / curve1
    hp1cov = hcov2 + beta1 * hcov1[...]
    r2cov = z1cov[...] - step1 * hp1cov
    covs[0] = r2cov
    covs[1] = z1cov[...] + beta1 * c0[...]
    own_norm = jnp.zeros((16, 1), F32)
    cross = jnp.zeros((16, 1), F32)
    for day in range(3):
        hp1 = w2[day] + beta1 * w1[day]
        r2 = r1[day] - step1 * hp1
        z2day = z1[day] - step1 * (v3[day] + beta1 * v2[day])
        own_norm = own_norm + row_sum(r2 * z2day)
        cross = cross + row_sum(z2day * hp1)
        if day < 2:
            z2[day] = z2day
            p1[day] = z1[day] + beta1 * v1[day]
        whole[day] = z1whole[day] - step1 * (whole[day] + beta1 * whole2[day])
    observed = observe(whole, r2cov, spread, covariates, weight)
    quadratic = sum(row_sum(predictor * weighted) for predictor, weighted in observed)
    for day in range(2):
        quadratic = quadratic + row_sum(times_matrix(z2[day], (a0, a1)[day][...]) * whole[day])
        quadratic = quadratic + 2.0 * row_sum(
            times_matrix(z2[day], (o0, o1)[day][...]) * whole[day + 1]
        )
    lane = lax.broadcasted_iota(jnp.int32, (16, 128), 1)
    sub = lax.broadcasted_iota(jnp.int32, (16, 128), 0)
    line = jnp.zeros((16, 128), F32)
    for index, value in enumerate((own_norm, quadratic, cross)):
        line = jnp.where(lane == sub + 16 * index, value, line)
    sums[...] = jnp.broadcast_to(jnp.sum(line, axis=0, keepdims=True), (128, 128))
    norm2cov = row_sum(r2cov * r2cov)
    quadcov = row_sum(r2cov * prior[...] * r2cov)
    crosscov = row_sum(r2cov * hp1cov)
    values = (scalars[:, 0:1], step1, norm1, curve1, norm2cov, quadcov, crosscov)
    out = jnp.zeros((16, 128), F32)
    for index, value in enumerate(values):
        out = jnp.where(lane == index, value, out)
    scalars_out[...] = out


def third_stage(*operands):
    own = shaped(2, 16, 320)
    return call(
        third_kernel,
        "third_stage",
        (shaped(128, 128), own, own, shaped(16, 128), shaped(2, 16, 64)),
        [VMEM_BLOCK] * len(operands),
        *operands,
        scratch=[pltpu.VMEM((3, 16, 2560), F32)],
    )


def final_kernel(sums, scalars, v1, p1, z2, c0, covs, field, cov):
    step0, step1, norm1, curve1, norm2cov, quadcov, crosscov = (
        scalars[:, i : i + 1] for i in range(7)
    )
    lane = lax.broadcasted_iota(jnp.int32, (16, 128), 1)
    sub = lax.broadcasted_iota(jnp.int32, (16, 128), 0)
    line = jnp.sum(sums[...], axis=0, keepdims=True)
    own_norm, quadratic, cross = (
        row_sum(jnp.where(lane == sub + 16 * index, line, 0.0)) for index in range(3)
    )
    norm2 = own_norm + norm2cov
    beta2 = norm2 / norm1
    curve2 = (
        quadratic + quadcov + 2.0 * beta2 * (cross + crosscov) + beta2 * beta2 * curve1
    )
    step2 = norm2 / curve2
    middle = step1 + step2 * beta2
    for day in range(2):
        field[:, day, :] = step0 * v1[day] + middle * p1[day] + step2 * z2[day]
    cov[...] = step0 * c0[...] + middle * covs[1] + step2 * covs[0]


def final_stage(*operands):
    return call(
        final_kernel,
        "final_stage",
        (shaped(16, 2, 320), shaped(16, 64)),
        [VMEM_BLOCK] * len(operands),
        *operands,
    )


def setup_kernel(count, vertices, bary, prec, value, covs, after, spread, weight, kept, sent, grad_cov, covariates):
    core = lax.axis_index("blk_1")
    slot_start = (lax.axis_index("blk_0") * 2 + core) * 128
    cov_sum = jnp.zeros((1, 64), F32)
    for day in range(2):
        shares = [bary[k, day : day + 1, :] for k in range(3)]
        total = shares[0] + shares[1] + shares[2]
        nodes = lax.broadcasted_iota(jnp.int32, (2560, 128), 0)
        dense = jnp.zeros((2560, 128), F32)
        for k in range(3):
            dense = dense + jnp.where(nodes == vertices[k, day : day + 1, :], shares[k] / total, 0.0)
        high, low = halves(dense)
        spread[day, :, :128] = high
        spread[day, :, 128:] = low
        covariates[day] = stacked_halves(covs[:, day, :])
        slot = lax.broadcasted_iota(jnp.int32, (1, 128), 1) + slot_start
        slot_weight = jnp.where(slot < count[day], prec[day : day + 1], 0.0)
        weight[day : day + 1] = slot_weight
        weighted_value = jnp.broadcast_to(slot_weight * value[day : day + 1], (16, 128))
        grad = spread_out(weighted_value, spread[day])[:1]
        for row in range(4):
            first = grad[:, row * 640 : row * 640 + 320]
            second = grad[:, row * 640 + 320 : row * 640 + 640]
            kept[row, day : day + 1] = jnp.where(core == 0, first, second)
            sent[row, day : day + 1] = jnp.where(core == 0, second, first)
        cov_sum = cov_sum + times_rows(weighted_value, covariates[day])[:1]
    grad_cov[...] = cov_sum


def setup_stage(*operands):
    return call(
        setup_kernel,
        "setup_stage",
        (
            pltpu.VMEM((2, 2560, 256), BF16), shaped(2, 128), shaped(4, 2, 320), shaped(4, 2, 320),
            shaped(1, 64), pltpu.VMEM((2, 128, 128), BF16),
        ),
        [SMEM_BLOCK] + [whole_block(o) for o in operands[1:-1]] + [ANY_BLOCK],
        operands[0],
        *(pltpu.with_memory_space_constraint(o, pltpu.HBM) for o in operands[1:-1]),
        operands[-1],
        grid=(1,),
    )


def on_device(
    diag_blocks,
    off_blocks,
    leakage,
    obs_count,
    obs_triangle,
    obs_bary,
    obs_prec,
    obs_value,
    covariates,
    triangles,
    prior_prec,
    probes,
    probes_cov,
):
    row_start = lax.axis_index(BLK) * 320
    square = lax.dynamic_slice_in_dim(diag_blocks, row_start, 320, 2)
    rows = lax.broadcasted_iota(jnp.int32, (2, 320, 320), 1)
    columns = lax.broadcasted_iota(jnp.int32, (2, 320, 320), 2)
    dominant = jnp.sum(jnp.where(rows == columns, square, 0.0), axis=1)
    both = jnp.concatenate([1.0 - leakage, dominant])
    every = lax.all_to_all(jnp.broadcast_to(both, (16, 4, 320)), DAY, 0, 0, tiled=True)
    co = chain_coefficients(every)

    vertices = triangles[:, obs_triangle]
    spread, weight, kept, sent, grad_cov, covs = setup_stage(
        obs_count, vertices, obs_bary, obs_prec, obs_value, covariates, co
    )
    off_pair = [split_blocks(off_blocks, "split_off", day) for day in range(2)]
    diag_pair = [split_blocks(diag_blocks, "split_diag", day) for day in range(2)]
    bx, w0, message = start_stage(*scattered_pieces(kept, sent), probes, grad_cov, co, off_pair[0])
    prior = prior_prec[None]
    padded_cov = jnp.pad(probes_cov, ((1, 0), (0, 0)))

    pairs = (*diag_pair, *off_pair)
    v1, message = precondition(w0, message, co, (off_pair[1],), (diag_pair[0],))
    nodes, behind1 = gather_nodes(message, own_terms(pairs, v1))
    kept, sent, cov1, whole1, c0 = first_stage(
        *nodes, padded_cov, spread, covs, weight, behind1
    )
    image, dots = first_rows(*off_pair, whole1, bx, v1)
    w1, message = image_stage(*scattered_pieces(kept, sent), image, v1, cov1, dots, co)

    v2, message = precondition(w1, message, co)
    nodes, behind2 = gather_nodes(message, own_terms(pairs, v2))
    kept, sent, cov2, whole2, z1whole, z1cov, hcov1, scalars = second_stage(
        *nodes, whole1, c0, prior, spread, covs, weight, behind1, behind2
    )
    image, dots, r1, z1 = second_rows(*off_pair, z1whole, bx, v1, v2, w1, scalars)
    w2, message = image_stage(*scattered_pieces(kept, sent), image, z1, cov2, dots, co)

    v3, message = precondition(w2, message, co)
    sums, z2, p1, scalars, covs2 = third_stage(
        *gather_nodes(message, behind2)[0], whole2, z1whole, scalars, c0, z1cov, hcov1, prior, spread, covs, weight,
        *pairs, r1, z1, w1, w2, v1, v2, v3,
    )
    sums = lax.all_to_all(sums, DAY + BLK, 0, 0, tiled=True)
    return final_stage(sums, scalars, v1, p1, z2, c0, covs2)


def solution(mesh):
    split = Mesh(mesh.devices.reshape(4, 4, 4, 2), ("day_0", "day_1", "blk_0", "blk_1"))
    in_specs = (
        P(DAY, BLK, None),
        P(DAY, BLK, None),
        P(DAY, BLK),
        P(DAY),
        P(DAY, BLK),
        P(None, DAY, BLK),
        P(DAY, BLK),
        P(DAY, BLK),
        P(None, DAY, BLK),
        P(),
        P(),
        P(None, DAY, BLK),
        P(),
    )
    out_specs = (P(None, DAY, BLK), P())
    return jax.shard_map(
        on_device, mesh=split, in_specs=in_specs, out_specs=out_specs, check_vma=False
    )
```

```python
import functools

import jax
import jax.numpy as jnp
from jax import lax
from jax.experimental import pallas as pl
from jax.experimental.pallas import tpu as pltpu
from jax.sharding import Mesh
from jax.sharding import PartitionSpec as P

DAY = ("day_0", "day_1")
BLK = ("blk_0", "blk_1")
F32 = jnp.float32
BF16 = jnp.bfloat16
NT = (((1,), (1,)), ((), ()))
NN = (((1,), (0,)), ((), ()))


def shift(value, axis, distance):
    size = lax.axis_size(axis)
    return lax.ppermute(value, axis, [(i, (i + distance) % size) for i in range(size)])


def swapped(value):
    return lax.ppermute(value, "blk_1", [(0, 1), (1, 0)])


def ring_gather(value, axis):
    return [value] + [shift(value, axis, k) for k in (1, 2, 3)]


def ring_sum(relative):
    return (relative[0] + relative[2]) + (relative[1] + relative[3])


def scattered_pieces(kept, sent):
    row = lax.axis_index("blk_0")
    half = kept + swapped(sent)
    pieces = [lax.dynamic_index_in_dim(half, (row + k) % 4, 0, False) for k in range(4)]
    return [pieces[0]] + [shift(pieces[k], "blk_0", k) for k in (1, 2, 3)]


def gather_nodes(message, ready):
    column, ready = lax.optimization_barrier((jnp.stack(ring_gather(message, "blk_0")), ready))
    return (column, swapped(column)), ready


def ring_message(w, co):
    g0, g1, gg, d1, dg = co[0:1], co[1:2], co[2:3], co[4:5], co[5:6]
    ahead = dg * (w[1] + d1 * w[0]) + w[2]
    behind = g0 * w[0] + d1 * (g1 * w[1] + dg * gg * w[2])
    return ahead, behind


def weighted(co, first, values):
    return sum(co[first + k : first + k + 1] * value for k, value in enumerate(values))


def middle_kernel(m0, m1, m2, m3, co, *refs):
    out1, out2, out3, local = refs[-4:]
    middle_body(m0, m1, m2, m3, co, out1, out2, out3, local)


def middle_body(m0, m1, m2, m3, co, out1, out2, out3, local):
    messages = (m0, m1, m2, m3)
    fs = [m[:, :320] for m in messages]
    bs = [m[:, 320:640] for m in messages]
    pack = ring_sum([m[:, 640:] for m in messages])
    local[0] = weighted(co, 6, fs[1:])
    local[1] = weighted(co, 9, bs[1:])
    local[2] = jnp.zeros((16, 320), F32)
    local[2, :, :128] = pack
    total_f = weighted(co, 12, fs)
    total_b = weighted(co, 16, bs)
    group = lax.axis_index("day_0")
    for k, out in ((1, out1), (2, out2), (3, out3)):
        out[:, :320] = jnp.where(group + k < 4, total_f, total_b)
        out[:, 320:] = pack


def last_kernel(r1, r2, r3, local, w, co, *refs):
    last_body(r1, r2, r3, local, w, co, *refs[-2:])


def last_body(r1, r2, r3, local, w, co, v, message):
    group = lax.axis_index("day_0")
    far_f, far_b = jnp.zeros((16, 320), F32), jnp.zeros((16, 320), F32)
    packs = [local[2, :, :128]]
    for k, r in ((1, r1), (2, r2), (3, r3)):
        packs.append(r[:, 320:])
        value = co[19 + k : 20 + k] * r[:, :320]
        far_f = far_f + jnp.where(group >= k, value, 0.0)
        far_b = far_b + jnp.where(group >= k, 0.0, value)
    come_f = local[0] + co[23:24] * far_f
    come_b = local[1] + co[24:25] * far_b
    raise_days(come_f, come_b, w, co, v, message, ring_sum(packs))


def raise_days(come_f, come_b, w, co, v, message, pack):
    g0, g1, gg, d1, dg = co[0:1], co[1:2], co[2:3], co[4:5], co[5:6]
    l0 = w[0] + come_f
    l1 = w[1] + d1 * l0
    u1 = dg * (come_b + gg * w[2])
    u0 = d1 * (g1 * w[1] + u1)
    days = (g0 * l0 + u0, g1 * l1 + u1, gg * (dg * l1 + w[2]) + come_b)
    for day, value in enumerate(days):
        v[day] = value
        message[:, day * 320 : day * 320 + 320] = value
    message[:, 960:] = pack


def precondition(w, message, co, early=(), late=()):
    pieces = ring_gather(message, "day_1")
    one = shaped(16, 448)
    *out, local = call(
        middle_kernel, "middle", (one, one, one, shaped(3, 16, 320)),
        [VMEM_BLOCK] * 5 + [ANY_BLOCK] * len(early), *pieces, co, *early,
    )
    got = [shift(out[k - 1], "day_0", k) for k in (1, 2, 3)]
    return call(
        last_kernel, "last", (shaped(3, 16, 320), shaped(16, 1088)),
        [VMEM_BLOCK] * 6 + [ANY_BLOCK] * len(late), *got, local, w, co, *late,
    )


def halves(value):
    high = value.astype(BF16)
    return high, (value - high.astype(F32)).astype(BF16)


def stacked_halves(value):
    return jnp.concatenate(halves(value), axis=0)


def matmul(first, second, dims):
    return lax.dot_general(first, second, dims, preferred_element_type=F32)


def times_rows(value, pair):
    n = pair.shape[0] // 2
    out = matmul(stacked_halves(value), pair, NT)
    return (out[:16, :n] + out[16:, :n]) + (out[:16, n:] + out[16:, n:])


def times_matrix(value, pair):
    high, low = halves(value)
    both = jnp.concatenate(
        [jnp.concatenate([high, high], axis=1), jnp.concatenate([low, low], axis=1)], axis=0
    )
    out = matmul(both, pair, NN)
    return out[:16] + out[16:]


VMEM_BLOCK = pl.BlockSpec(memory_space=pltpu.VMEM)
SMEM_BLOCK = pl.BlockSpec(memory_space=pltpu.SMEM)
ANY_BLOCK = pl.BlockSpec(memory_space=pl.ANY)
HBM_BLOCK = pl.BlockSpec(memory_space=pltpu.HBM)


def shaped(*shape):
    return jax.ShapeDtypeStruct(shape, F32)


def whole_block(operand):
    return pl.BlockSpec(operand.shape, lambda i: (0,) * operand.ndim)


def call(kernel, name, outs, in_specs, *operands, scratch=(), limit=16, grid=()):
    return pl.pallas_call(
        kernel,
        grid=grid,
        out_shape=outs,
        in_specs=in_specs,
        out_specs=jax.tree.map(lambda _: VMEM_BLOCK, outs),
        scratch_shapes=scratch,
        compiler_params=pltpu.CompilerParams(vmem_limit_bytes=limit << 20),
        name=name,
    )(*operands)


CHUNK = 80


def split_kernel(day, source, target, buffer, sem):
    jobs = [(day, row) for row in range(0, 320, CHUNK)]

    def fetch(index):
        day, row = jobs[index]
        slot = index % 3
        return pltpu.make_async_copy(source.at[day, pl.ds(row, CHUNK)], buffer.at[slot], sem.at[slot])

    fetch(0).start()
    fetch(1).start()
    for index, (day, row) in enumerate(jobs):
        if index + 2 < len(jobs):
            fetch(index + 2).start()
        fetch(index).wait()
        high, low = halves(buffer[index % 3])
        target[pl.ds(row, CHUNK)] = high
        target[pl.ds(320 + row, CHUNK)] = low


def split_blocks(blocks, name, day):
    return call(
        functools.partial(split_kernel, day),
        name + str(day),
        pltpu.VMEM((640, 2560), BF16),
        [HBM_BLOCK],
        pltpu.with_memory_space_constraint(blocks, pltpu.HBM),
        scratch=[pltpu.VMEM((3, CHUNK, 2560), F32), pltpu.SemaphoreType.DMA((3,))],
    )


def pick(values, index):
    out = jnp.zeros_like(values[0])
    for place, value in enumerate(values):
        out = jnp.where(index == place, value, out)
    return out


def put_rows(message, values):
    for r, value in enumerate(values):
        for c, width in enumerate((128, 128, 64)):
            row = 1 + 3 * r + c
            message[row : row + 1, 640 : 640 + width] = value[:, 128 * c : 128 * c + width]


def get_rows(pack):
    return [
        jnp.concatenate(
            [pack[1 + 3 * r : 2 + 3 * r], pack[2 + 3 * r : 3 + 3 * r], pack[3 + 3 * r : 4 + 3 * r, :64]], axis=1
        )
        for r in range(4)
    ]


def only_first_row(value):
    return jnp.where(lax.broadcasted_iota(jnp.int32, value.shape, 0) == 0, value, 0.0)


def ordered(kept, messages, place):
    for k, message in enumerate(messages):
        kept[k] = message[...]
    return [kept[lax.rem(place + (4 - j), 4)] for j in range(4)]


def first_middle_kernel(m0, m1, m2, m3, *refs):
    out, ordered_out, kept = refs[-3:]
    messages = ordered(kept, (m0, m1, m2, m3), lax.axis_index("day_1"))
    for j, message in enumerate(messages):
        ordered_out[j] = message
    pack = ring_sum([m[:, 640:] for m in (m0, m1, m2, m3)])
    out[:, 640:] = only_first_row(pack)
    chain = [get_rows(m[:, 640:]) for m in messages]
    alpha, beta = jnp.zeros((1, 320), F32), jnp.ones((1, 320), F32)
    alphas = [None] * 4
    for j in (3, 2, 1, 0):
        dec0, dec1, dom0, dom1 = chain[j]
        alphas[j] = alpha
        const = 1.0 / dom0 + dec1 * dec1 * (1.0 / dom1 + alpha)
        slope = dec1 * dec1 * beta
        alpha, beta = dec0 * dec0 * const, dec0 * dec0 * slope
    moved = jnp.ones((1, 320), F32)
    total_f = total_p = jnp.zeros((16, 320), F32)
    for j in range(4):
        dec0, dec1 = chain[j][:2]
        f, p = messages[j][:, :320], messages[j][:, 320:640]
        if j:
            moved = moved * dec0
        total_f = f + dec0 * dec1 * total_f
        total_p = total_p + moved * (p + alphas[j] * dec1 * f)
        moved = moved * dec1
    out[:, :320] = total_f
    out[:, 320:640] = total_p
    put_rows(out, (moved, const, slope, chain[0][0]))


def first_last_kernel(z0, z1, z2, z3, near, bx, *refs):
    co, w, v, message, kept = refs[-5:]
    group, place = lax.axis_index("day_0"), lax.axis_index("day_1")
    zero, one = jnp.zeros((1, 320), F32), jnp.ones((1, 320), F32)
    groups = ordered(kept, (z0, z1, z2, z3), group)
    chain = [get_rows(near[j, :, 640:]) for j in range(4)]
    whole_chain = [get_rows(m[:, 640:]) for m in groups]
    moved = [c[0] for c in whole_chain]
    first_decay = [c[3] for c in whole_chain] + [zero]
    exits, entry = [zero] * 4, [zero] * 5
    for g in (3, 2, 1, 0):
        entry[g] = whole_chain[g][1] + whole_chain[g][2] * exits[g]
        if g:
            exits[g - 1] = first_decay[g] * first_decay[g] * entry[g]
    dec0 = [c[0] for c in chain]
    dec1 = [c[1] for c in chain]
    after_decay = dec0[1:] + [pick(first_decay[1:], group)]
    gain0, gain1, after_gain = [None] * 4, [None] * 4, [None] * 4
    beyond = pick(exits, group)
    for j in (3, 2, 1, 0):
        after_gain[j] = beyond
        gain1[j] = 1.0 / chain[j][3] + beyond
        gain0[j] = 1.0 / chain[j][2] + dec1[j] * dec1[j] * gain1[j]
        beyond = dec0[j] * dec0[j] * gain0[j]
    next_gain = gain0[1:] + [pick(entry[1:], group)]
    mine = [dec1[j] * after_decay[j] for j in range(4)]
    whole = [moved[g] * first_decay[g + 1] for g in range(4)]

    def product(factors, low, high):
        kept = [
            jnp.where((low <= index) & (index < high), factor, one)
            for index, factor in enumerate(factors)
        ]
        return kept[0] * kept[1] * kept[2] * kept[3]

    rows = [pick(values, place) for values in (gain0, gain1, next_gain, dec0, dec1, after_decay)]
    local_f, local_b, total_f, total_b, far = [], [], [], [], []
    for k in range(4):
        source = lax.rem(place + (4 - k), 4)
        total_f.append(product(mine, source + 1, 4))
        total_b.append(product(mine, 0, source))
        if k:
            local_f.append(jnp.where(source < place, product(mine, source + 1, place), zero))
            local_b.append(jnp.where(source > place, product(mine, place + 1, source), zero))
            origin = lax.rem(group + (4 - k), 4)
            far.append(product(whole, jnp.minimum(origin, group) + 1, jnp.maximum(origin, group)))
    before, after = product(mine, 0, place), product(mine, place + 1, 4)
    rows += local_f + local_b + total_f + total_b + far + [before, after]
    for index, row in enumerate(rows):
        co[index : index + 1] = row

    come_f = come_b = far_f = far_b = jnp.zeros((16, 320), F32)
    for j in range(4):
        f, p = near[j, :, :320], near[j, :, 320:640]
        ahead = after_decay[j] * f
        behind = p + after_gain[j] * dec1[j] * f
        come_f = come_f + jnp.where(j < place, product(mine, j + 1, place) * ahead, 0.0)
        come_b = come_b + jnp.where(j > place, product(mine, place + 1, j) * behind, 0.0)
        f, p = groups[j][:, :320], groups[j][:, 320:640]
        ahead = first_decay[j + 1] * f
        behind = p + exits[j] * moved[j] * f
        far_f = far_f + jnp.where(j < group, product(whole, j + 1, group) * ahead, 0.0)
        far_b = far_b + jnp.where(j > group, product(whole, group + 1, j) * behind, 0.0)
    w[0], w[1], w[2] = bx[0], bx[1], jnp.zeros((16, 320), F32)
    pack = only_first_row(ring_sum([z[:, 640:] for z in (z0, z1, z2, z3)]))
    raise_days(come_f + before * far_f, come_b + after * far_b, w, co, v, message, pack)


def first_precondition(bx, message, early, late):
    pieces = ring_gather(message, "day_1")
    out, near = call(
        first_middle_kernel,
        "first_middle",
        (shaped(16, 768), shaped(4, 16, 768)),
        [VMEM_BLOCK] * 4 + [ANY_BLOCK],
        *pieces, early,
        scratch=[pltpu.VMEM((4, 16, 768), F32)],
    )
    field = shaped(3, 16, 320)
    return call(
        first_last_kernel,
        "first_last",
        (shaped(25, 320), field, field, shaped(16, 1088)),
        [VMEM_BLOCK] * 6 + [ANY_BLOCK],
        *ring_gather(out, "day_0"), near, bx, late,
        scratch=[pltpu.VMEM((4, 16, 768), F32)],
    )


def own_terms_kernel(a0, a1, o0, o1, own, out):
    out[0] = times_matrix(own[0], a0[...])
    out[1] = times_matrix(own[1], a1[...]) + times_matrix(own[0], o0[...])
    out[2] = times_matrix(own[1], o1[...])


def own_terms(pairs, own):
    return call(own_terms_kernel, "own_terms", shaped(3, 16, 2560), [VMEM_BLOCK] * 5, *pairs, own)


def rows_into(pairs, whole, out):
    for day in range(2):
        out[day] = times_rows(whole[day + 1], pairs[day][...])


def lanes(*values):
    lane = lax.broadcasted_iota(jnp.int32, (16, 64), 1)
    out = jnp.zeros((16, 64), F32)
    for index, value in enumerate(values):
        out = jnp.where(lane == index, value, out)
    return out


def first_rows_kernel(o0, o1, whole, bx, v1, out, dots):
    rows_into((o0, o1), whole, out)
    dots[...] = lanes(sum(row_sum(bx[day] * v1[day]) for day in range(2)))


def first_rows(*operands):
    return call(
        first_rows_kernel, "first_rows", (shaped(2, 16, 320), shaped(16, 64)), [VMEM_BLOCK] * 5, *operands
    )


def second_rows_kernel(o0, o1, whole, bx, v1, v2, w1, scalars, out, dots, r1, z1):
    rows_into((o0, o1), whole, out)
    step0 = scalars[:, 0:1]
    norm = cross = jnp.zeros((16, 1), F32)
    for day in range(3):
        z = v1[day] - step0 * v2[day]
        r = (bx[day] if day < 2 else 0.0) - step0 * w1[day]
        z1[day] = z
        r1[day] = r
        norm = norm + row_sum(r * z)
        cross = cross + row_sum(z * w1[day])
    dots[...] = lanes(norm, 0.0, cross)


def second_rows(*operands):
    own = shaped(3, 16, 320)
    return call(
        second_rows_kernel,
        "second_rows",
        (shaped(2, 16, 320), shaped(16, 64), own, own),
        [VMEM_BLOCK] * 8,
        *operands,
    )


def start_kernel(p0, p1, p2, p3, probes, grad_cov, own_chain, *refs):
    bx, message = refs[-2:]
    grad = ring_sum([p0[...], p1[...], p2[...], p3[...]])
    for day in range(2):
        bx[day, 0:1] = grad[day : day + 1]
        bx[day, 1:16] = probes[:, day, :]
    dec1 = own_chain[1:2]
    ahead = bx[1] + dec1 * bx[0]
    message[:, :320] = ahead
    message[:, 320:640] = bx[0] / own_chain[2:3] + dec1 * ahead / own_chain[3:4]
    message[:, 640:] = jnp.zeros((16, 128), F32)
    message[0:1, 640:704] = grad_cov[...]
    put_rows(message, [own_chain[r : r + 1] for r in range(4)])


def start_stage(*operands):
    return call(
        start_kernel,
        "start_stage",
        (shaped(2, 16, 320), shaped(16, 768)),
        [VMEM_BLOCK] * 7 + [ANY_BLOCK] * (len(operands) - 7),
        *operands,
    )


def image_kernel(p0, p1, p2, p3, rows, vector, cov_terms, dots, co, w, message):
    pieces = (p0, p1, p2, p3)
    total = jnp.zeros((16, 1), F32)
    for day in range(3):
        value = ring_sum([p[day] for p in pieces])
        if day < 2:
            value = value + rows[day]
        w[day] = value
        total = total + row_sum(vector[day] * value)
    ahead, behind = ring_message(w, co)
    message[:, :320] = ahead
    message[:, 320:640] = behind
    message[:, 640:704] = cov_terms[...]
    message[:, 704:] = dots[...] + lanes(0.0, total)


def image_stage(*operands):
    return call(
        image_kernel,
        "image_stage",
        (shaped(3, 16, 320), shaped(16, 768)),
        [VMEM_BLOCK] * 9,
        *operands,
    )


def assemble(mine, other, whole):
    row, core = lax.axis_index("blk_0"), lax.axis_index("blk_1")
    packs = []
    for k in range(4):
        at = pl.multiple_of(lax.rem(row + (4 - k), 4) * 640, 128)
        for day in range(3):
            a = mine[k, :, day * 320 : day * 320 + 320]
            b = other[k, :, day * 320 : day * 320 + 320]
            first = jnp.where(core == 0, a, b)
            second = jnp.where(core == 0, b, a)
            whole[day, :, pl.ds(at, 640)] = jnp.concatenate([first, second], axis=1)
        packs.append(mine[k, :, 960:1088] + other[k, :, 960:1088])
    return (packs[0] + packs[2]) + (packs[1] + packs[3])


def scatter_parts(obs, terms, kept, sent):
    core = lax.axis_index("blk_1")
    last = lax.axis_index("day_0") * 4 + lax.axis_index("day_1") == 15
    days = (obs[0] + terms[0], obs[1] + terms[1], jnp.where(last, 0.0, terms[2]))
    for day, part in enumerate(days):
        for row in range(4):
            first = part[:, row * 640 : row * 640 + 320]
            second = part[:, row * 640 + 320 : row * 640 + 640]
            kept[row, day] = jnp.where(core == 0, first, second)
            sent[row, day] = jnp.where(core == 0, second, first)


def observe(whole, cov, spread, covariates, weight):
    result = []
    for day in range(2):
        out = matmul(stacked_halves(whole[day]), spread[day], NN)
        out = (out[:16, :128] + out[16:, :128]) + (out[:16, 128:] + out[16:, 128:])
        predictor = out + times_matrix(cov, covariates[day])
        result.append((predictor, weight[day : day + 1] * predictor))
    return result


def spread_out(value, pair):
    high, low = halves(value)
    both = jnp.concatenate(
        [jnp.concatenate([high, high], axis=1), jnp.concatenate([low, low], axis=1)], axis=0
    )
    out = matmul(both, pair, NT)
    return out[:16] + out[16:]


def observe_back(observed, behind, spread, covariates, kept, sent, cov_terms):
    weights = [pair[1] for pair in observed]
    obs = [spread_out(weights[day], spread[day]) for day in range(2)]
    scatter_parts(obs, behind, kept, sent)
    cov_terms[...] = sum(times_rows(weights[day], covariates[day]) for day in range(2))


def row_sum(value):
    return jnp.sum(value, axis=1, keepdims=True)


PARTS = (shaped(4, 3, 16, 320), shaped(4, 3, 16, 320), shaped(16, 64))


def first_kernel(mine, other, probes_cov, spread, covariates, weight, behind, kept, sent, cov_terms, whole, cov):
    pack = assemble(mine, other, whole)
    cov[...] = jnp.where(
        lax.broadcasted_iota(jnp.int32, (16, 64), 0) == 0, pack[:, :64], probes_cov[...]
    )
    observed = observe(whole, cov[...], spread, covariates, weight)
    observe_back(observed, behind, spread, covariates, kept, sent, cov_terms)


def first_stage(mine, other, probes_cov, spread, covariates, weight, behind):
    return call(
        first_kernel,
        "first_stage",
        PARTS + (shaped(3, 16, 2560), shaped(16, 64)),
        [VMEM_BLOCK] * 7,
        mine, other, probes_cov, spread, covariates, weight, behind,
    )


def second_kernel(
    mine, other, whole1, c0, prior, spread, covariates, weight, behind1, behind2,
    kept, sent, cov_terms, whole2, whole, cov, hcov, scalars, behind,
):
    pack = assemble(mine, other, whole2)
    hcov1 = pack[:, :64] + prior[...] * c0[...]
    norm0 = pack[:, 64:65] + row_sum(c0[...] * c0[...])
    curve0 = pack[:, 65:66] + row_sum(c0[...] * hcov1)
    step0 = norm0 / curve0
    for day in range(3):
        whole[day] = whole1[day] - step0 * whole2[day]
    for day in range(3):
        behind[day] = behind1[day] - step0 * behind2[day]
    cov[...] = c0[...] - step0 * hcov1
    hcov[...] = hcov1
    lane = lax.broadcasted_iota(jnp.int32, (16, 128), 1)
    scalars[...] = jnp.where(lane == 0, step0, jnp.where(lane == 1, norm0, curve0))
    observed = observe(whole, cov[...], spread, covariates, weight)
    observe_back(observed, behind, spread, covariates, kept, sent, cov_terms)


def second_stage(mine, other, whole1, c0, prior, spread, covariates, weight, behind1, behind2):
    whole = shaped(3, 16, 2560)
    return call(
        second_kernel,
        "second_stage",
        PARTS + (whole, whole, shaped(16, 64), shaped(16, 64), shaped(16, 128)),
        [VMEM_BLOCK] * 10,
        mine, other, whole1, c0, prior, spread, covariates, weight, behind1, behind2,
        scratch=[pltpu.VMEM((3, 16, 2560), F32)],
    )


def third_kernel(
    mine, other, whole2, z1whole, scalars, c0, z1cov, hcov1, prior, spread, covariates, weight,
    a0, a1, o0, o1, r1, z1, w1, w2, v1, v2, v3,
    sums, z2, p1, scalars_out, covs, whole,
):
    pack = assemble(mine, other, whole)
    norm0, curve0 = scalars[:, 1:2], scalars[:, 2:3]
    hcov2 = pack[:, :64] + prior[...] * z1cov[...]
    norm1 = pack[:, 64:65] + row_sum(z1cov[...] * z1cov[...])
    beta1 = norm1 / norm0
    curve1 = (
        pack[:, 65:66]
        + row_sum(z1cov[...] * hcov2)
        + 2.0 * beta1 * (pack[:, 66:67] + row_sum(z1cov[...] * hcov1[...]))
        + beta1 * beta1 * curve0
    )
    step1 = norm1 / curve1
    hp1cov = hcov2 + beta1 * hcov1[...]
    r2cov = z1cov[...] - step1 * hp1cov
    covs[0] = r2cov
    covs[1] = z1cov[...] + beta1 * c0[...]
    own_norm = jnp.zeros((16, 1), F32)
    cross = jnp.zeros((16, 1), F32)
    for day in range(3):
        hp1 = w2[day] + beta1 * w1[day]
        r2 = r1[day] - step1 * hp1
        z2day = z1[day] - step1 * (v3[day] + beta1 * v2[day])
        own_norm = own_norm + row_sum(r2 * z2day)
        cross = cross + row_sum(z2day * hp1)
        if day < 2:
            z2[day] = z2day
            p1[day] = z1[day] + beta1 * v1[day]
        whole[day] = z1whole[day] - step1 * (whole[day] + beta1 * whole2[day])
    observed = observe(whole, r2cov, spread, covariates, weight)
    quadratic = sum(row_sum(predictor * weighted) for predictor, weighted in observed)
    for day in range(2):
        quadratic = quadratic + row_sum(times_matrix(z2[day], (a0, a1)[day][...]) * whole[day])
        quadratic = quadratic + 2.0 * row_sum(
            times_matrix(z2[day], (o0, o1)[day][...]) * whole[day + 1]
        )
    lane = lax.broadcasted_iota(jnp.int32, (16, 128), 1)
    sub = lax.broadcasted_iota(jnp.int32, (16, 128), 0)
    line = jnp.zeros((16, 128), F32)
    for index, value in enumerate((own_norm, quadratic, cross)):
        line = jnp.where(lane == sub + 16 * index, value, line)
    sums[...] = jnp.broadcast_to(jnp.sum(line, axis=0, keepdims=True), (128, 128))
    norm2cov = row_sum(r2cov * r2cov)
    quadcov = row_sum(r2cov * prior[...] * r2cov)
    crosscov = row_sum(r2cov * hp1cov)
    values = (scalars[:, 0:1], step1, norm1, curve1, norm2cov, quadcov, crosscov)
    out = jnp.zeros((16, 128), F32)
    for index, value in enumerate(values):
        out = jnp.where(lane == index, value, out)
    scalars_out[...] = out


def third_stage(*operands):
    own = shaped(2, 16, 320)
    return call(
        third_kernel,
        "third_stage",
        (shaped(128, 128), own, own, shaped(16, 128), shaped(2, 16, 64)),
        [VMEM_BLOCK] * len(operands),
        *operands,
        scratch=[pltpu.VMEM((3, 16, 2560), F32)],
    )


def final_kernel(sums, scalars, v1, p1, z2, c0, covs, field, cov):
    step0, step1, norm1, curve1, norm2cov, quadcov, crosscov = (
        scalars[:, i : i + 1] for i in range(7)
    )
    lane = lax.broadcasted_iota(jnp.int32, (16, 128), 1)
    sub = lax.broadcasted_iota(jnp.int32, (16, 128), 0)
    line = jnp.sum(sums[...], axis=0, keepdims=True)
    own_norm, quadratic, cross = (
        row_sum(jnp.where(lane == sub + 16 * index, line, 0.0)) for index in range(3)
    )
    norm2 = own_norm + norm2cov
    beta2 = norm2 / norm1
    curve2 = (
        quadratic + quadcov + 2.0 * beta2 * (cross + crosscov) + beta2 * beta2 * curve1
    )
    step2 = norm2 / curve2
    middle = step1 + step2 * beta2
    for day in range(2):
        field[:, day, :] = step0 * v1[day] + middle * p1[day] + step2 * z2[day]
    cov[...] = step0 * c0[...] + middle * covs[1] + step2 * covs[0]


def final_stage(*operands):
    return call(
        final_kernel,
        "final_stage",
        (shaped(16, 2, 320), shaped(16, 64)),
        [VMEM_BLOCK] * len(operands),
        *operands,
    )


def setup_kernel(count, vertices, bary, prec, value, covs, spread, weight, kept, sent, grad_cov, covariates):
    core = lax.axis_index("blk_1")
    slot_start = (lax.axis_index("blk_0") * 2 + core) * 128
    cov_sum = jnp.zeros((1, 64), F32)
    for day in range(2):
        shares = [bary[k, day : day + 1, :] for k in range(3)]
        total = shares[0] + shares[1] + shares[2]
        nodes = lax.broadcasted_iota(jnp.int32, (2560, 128), 0)
        dense = jnp.zeros((2560, 128), F32)
        for k in range(3):
            dense = dense + jnp.where(nodes == vertices[k, day : day + 1, :], shares[k] / total, 0.0)
        high, low = halves(dense)
        spread[day, :, :128] = high
        spread[day, :, 128:] = low
        covariates[day] = stacked_halves(covs[:, day, :])
        slot = lax.broadcasted_iota(jnp.int32, (1, 128), 1) + slot_start
        slot_weight = jnp.where(slot < count[day], prec[day : day + 1], 0.0)
        weight[day : day + 1] = slot_weight
        weighted_value = jnp.broadcast_to(slot_weight * value[day : day + 1], (16, 128))
        grad = spread_out(weighted_value, spread[day])[:1]
        for row in range(4):
            first = grad[:, row * 640 : row * 640 + 320]
            second = grad[:, row * 640 + 320 : row * 640 + 640]
            kept[row, day : day + 1] = jnp.where(core == 0, first, second)
            sent[row, day : day + 1] = jnp.where(core == 0, second, first)
        cov_sum = cov_sum + times_rows(weighted_value, covariates[day])[:1]
    grad_cov[...] = cov_sum


def setup_stage(*operands):
    return call(
        setup_kernel,
        "setup_stage",
        (
            pltpu.VMEM((2, 2560, 256), BF16), shaped(2, 128), shaped(4, 2, 320), shaped(4, 2, 320),
            shaped(1, 64), pltpu.VMEM((2, 128, 128), BF16),
        ),
        [SMEM_BLOCK] + [whole_block(o) for o in operands[1:]],
        operands[0],
        *(pltpu.with_memory_space_constraint(o, pltpu.HBM) for o in operands[1:]),
        grid=(1,),
    )


def on_device(
    diag_blocks,
    off_blocks,
    leakage,
    obs_count,
    obs_triangle,
    obs_bary,
    obs_prec,
    obs_value,
    covariates,
    triangles,
    prior_prec,
    probes,
    probes_cov,
):
    row_start = lax.axis_index(BLK) * 320
    square = lax.dynamic_slice_in_dim(diag_blocks, row_start, 320, 2)
    rows = lax.broadcasted_iota(jnp.int32, (2, 320, 320), 1)
    columns = lax.broadcasted_iota(jnp.int32, (2, 320, 320), 2)
    dominant = jnp.sum(jnp.where(rows == columns, square, 0.0), axis=1)
    both = jnp.concatenate([1.0 - leakage, dominant])

    vertices = triangles[:, obs_triangle]
    spread, weight, kept, sent, grad_cov, covs = setup_stage(
        obs_count, vertices, obs_bary, obs_prec, obs_value, covariates
    )
    off_pair = [split_blocks(off_blocks, "split_off", day) for day in range(2)]
    diag_pair = [split_blocks(diag_blocks, "split_diag", day) for day in range(2)]
    bx, message = start_stage(*scattered_pieces(kept, sent), probes, grad_cov, both, off_pair[0])
    prior = prior_prec[None]
    padded_cov = jnp.pad(probes_cov, ((1, 0), (0, 0)))

    pairs = (*diag_pair, *off_pair)
    co, _, v1, message = first_precondition(bx, message, off_pair[1], diag_pair[0])
    nodes, behind1 = gather_nodes(message, own_terms(pairs, v1))
    kept, sent, cov1, whole1, c0 = first_stage(
        *nodes, padded_cov, spread, covs, weight, behind1
    )
    image, dots = first_rows(*off_pair, whole1, bx, v1)
    w1, message = image_stage(*scattered_pieces(kept, sent), image, v1, cov1, dots, co)

    v2, message = precondition(w1, message, co)
    nodes, behind2 = gather_nodes(message, own_terms(pairs, v2))
    kept, sent, cov2, whole2, z1whole, z1cov, hcov1, scalars = second_stage(
        *nodes, whole1, c0, prior, spread, covs, weight, behind1, behind2
    )
    image, dots, r1, z1 = second_rows(*off_pair, z1whole, bx, v1, v2, w1, scalars)
    w2, message = image_stage(*scattered_pieces(kept, sent), image, z1, cov2, dots, co)

    v3, message = precondition(w2, message, co)
    sums, z2, p1, scalars, covs2 = third_stage(
        *gather_nodes(message, behind2)[0], whole2, z1whole, scalars, c0, z1cov, hcov1, prior, spread, covs, weight,
        *pairs, r1, z1, w1, w2, v1, v2, v3,
    )
    sums = lax.all_to_all(sums, DAY + BLK, 0, 0, tiled=True)
    return final_stage(sums, scalars, v1, p1, z2, c0, covs2)


def solution(mesh):
    split = Mesh(mesh.devices.reshape(4, 4, 4, 2), ("day_0", "day_1", "blk_0", "blk_1"))
    in_specs = (
        P(DAY, BLK, None),
        P(DAY, BLK, None),
        P(DAY, BLK),
        P(DAY),
        P(DAY, BLK),
        P(None, DAY, BLK),
        P(DAY, BLK),
        P(DAY, BLK),
        P(None, DAY, BLK),
        P(),
        P(),
        P(None, DAY, BLK),
        P(),
    )
    out_specs = (P(None, DAY, BLK), P())
    return jax.shard_map(
        on_device, mesh=split, in_specs=in_specs, out_specs=out_specs, check_vma=False
    )
```

```python
import functools

import jax
import jax.numpy as jnp
from jax import lax
from jax.experimental import pallas as pl
from jax.experimental.pallas import tpu as pltpu
from jax.sharding import Mesh
from jax.sharding import PartitionSpec as P

DAY = ("day_0", "day_1")
BLK = ("blk_0", "blk_1")
F32 = jnp.float32
BF16 = jnp.bfloat16
NT = (((1,), (1,)), ((), ()))
NN = (((1,), (0,)), ((), ()))


def shift(value, axis, distance):
    size = lax.axis_size(axis)
    return lax.ppermute(value, axis, [(i, (i + distance) % size) for i in range(size)])


def swapped(value):
    return lax.ppermute(value, "blk_1", [(0, 1), (1, 0)])


def ring_gather(value, axis):
    return [value] + [shift(value, axis, k) for k in (1, 2, 3)]


def ring_sum(relative):
    return (relative[0] + relative[2]) + (relative[1] + relative[3])


def scattered_pieces(kept, sent):
    row = lax.axis_index("blk_0")
    half = kept + swapped(sent)
    pieces = [lax.dynamic_index_in_dim(half, (row + k) % 4, 0, False) for k in range(4)]
    return [pieces[0]] + [shift(pieces[k], "blk_0", k) for k in (1, 2, 3)]


def gather_nodes(message, ready):
    column, ready = lax.optimization_barrier((jnp.stack(ring_gather(message, "blk_0")), ready))
    return (column, swapped(column)), ready


def ring_message(w, co):
    g0, g1, gg, d1, dg = co[0:1], co[1:2], co[2:3], co[4:5], co[5:6]
    ahead = dg * (w[1] + d1 * w[0]) + w[2]
    behind = g0 * w[0] + d1 * (g1 * w[1] + dg * gg * w[2])
    return ahead, behind


def weighted(co, first, values):
    return sum(co[first + k : first + k + 1] * value for k, value in enumerate(values))


def middle_kernel(m0, m1, m2, m3, co, *refs):
    out1, out2, out3, local = refs[-4:]
    middle_body(m0, m1, m2, m3, co, out1, out2, out3, local)


def middle_body(m0, m1, m2, m3, co, out1, out2, out3, local):
    messages = (m0, m1, m2, m3)
    fs = [m[:, :320] for m in messages]
    bs = [m[:, 320:640] for m in messages]
    pack = ring_sum([m[:, 640:] for m in messages])
    local[0] = weighted(co, 6, fs[1:])
    local[1] = weighted(co, 9, bs[1:])
    local[2] = jnp.zeros((16, 320), F32)
    local[2, :, :128] = pack
    total_f = weighted(co, 12, fs)
    total_b = weighted(co, 16, bs)
    group = lax.axis_index("day_0")
    for k, out in ((1, out1), (2, out2), (3, out3)):
        out[:, :320] = jnp.where(group + k < 4, total_f, total_b)
        out[:, 320:] = pack


def last_kernel(r1, r2, r3, local, w, co, *refs):
    last_body(r1, r2, r3, local, w, co, *refs[-2:])


def last_body(r1, r2, r3, local, w, co, v, message):
    group = lax.axis_index("day_0")
    far_f, far_b = jnp.zeros((16, 320), F32), jnp.zeros((16, 320), F32)
    packs = [local[2, :, :128]]
    for k, r in ((1, r1), (2, r2), (3, r3)):
        packs.append(r[:, 320:])
        value = co[19 + k : 20 + k] * r[:, :320]
        far_f = far_f + jnp.where(group >= k, value, 0.0)
        far_b = far_b + jnp.where(group >= k, 0.0, value)
    come_f = local[0] + co[23:24] * far_f
    come_b = local[1] + co[24:25] * far_b
    raise_days(come_f, come_b, w, co, v, message, ring_sum(packs))


def raise_days(come_f, come_b, w, co, v, message, pack):
    g0, g1, gg, d1, dg = co[0:1], co[1:2], co[2:3], co[4:5], co[5:6]
    l0 = w[0] + come_f
    l1 = w[1] + d1 * l0
    u1 = dg * (come_b + gg * w[2])
    u0 = d1 * (g1 * w[1] + u1)
    days = (g0 * l0 + u0, g1 * l1 + u1, gg * (dg * l1 + w[2]) + come_b)
    for day, value in enumerate(days):
        v[day] = value
        message[:, day * 320 : day * 320 + 320] = value
    message[:, 960:] = pack


def precondition(w, message, co, early=(), late=()):
    pieces = ring_gather(message, "day_1")
    one = shaped(16, 448)
    *out, local = call(
        middle_kernel, "middle", (one, one, one, shaped(3, 16, 320)),
        [VMEM_BLOCK] * 5 + [ANY_BLOCK] * len(early), *pieces, co, *early,
    )
    got = [shift(out[k - 1], "day_0", k) for k in (1, 2, 3)]
    return call(
        last_kernel, "last", (shaped(3, 16, 320), shaped(16, 1088)),
        [VMEM_BLOCK] * 6 + [ANY_BLOCK] * len(late), *got, local, w, co, *late,
    )


def halves(value):
    high = value.astype(BF16)
    return high, (value - high.astype(F32)).astype(BF16)


def stacked_halves(value):
    return jnp.concatenate(halves(value), axis=0)


def matmul(first, second, dims):
    return lax.dot_general(first, second, dims, preferred_element_type=F32)


def times_rows(value, pair):
    n = pair.shape[0] // 2
    out = matmul(stacked_halves(value), pair, NT)
    return (out[:16, :n] + out[16:, :n]) + (out[:16, n:] + out[16:, n:])


def times_matrix(value, pair):
    high, low = halves(value)
    both = jnp.concatenate(
        [jnp.concatenate([high, high], axis=1), jnp.concatenate([low, low], axis=1)], axis=0
    )
    out = matmul(both, pair, NN)
    return out[:16] + out[16:]


VMEM_BLOCK = pl.BlockSpec(memory_space=pltpu.VMEM)
SMEM_BLOCK = pl.BlockSpec(memory_space=pltpu.SMEM)
ANY_BLOCK = pl.BlockSpec(memory_space=pl.ANY)
HBM_BLOCK = pl.BlockSpec(memory_space=pltpu.HBM)


def shaped(*shape):
    return jax.ShapeDtypeStruct(shape, F32)


def whole_block(operand):
    return pl.BlockSpec(operand.shape, lambda i: (0,) * operand.ndim)


def call(kernel, name, outs, in_specs, *operands, scratch=(), limit=16, grid=()):
    return pl.pallas_call(
        kernel,
        grid=grid,
        out_shape=outs,
        in_specs=in_specs,
        out_specs=jax.tree.map(lambda _: VMEM_BLOCK, outs),
        scratch_shapes=scratch,
        compiler_params=pltpu.CompilerParams(vmem_limit_bytes=limit << 20),
        name=name,
    )(*operands)


CHUNK = 80


def split_kernel(day, source, target, buffer, sem):
    jobs = [(day, row) for row in range(0, 320, CHUNK)]

    def fetch(index):
        day, row = jobs[index]
        return pltpu.make_async_copy(source.at[day, pl.ds(row, CHUNK)], buffer.at[index], sem.at[index])

    for index in range(len(jobs)):
        fetch(index).start()
    for index, (day, row) in enumerate(jobs):
        fetch(index).wait()
        high, low = halves(buffer[index])
        target[pl.ds(row, CHUNK)] = high
        target[pl.ds(320 + row, CHUNK)] = low


def split_blocks(blocks, name, day):
    return call(
        functools.partial(split_kernel, day),
        name + str(day),
        pltpu.VMEM((640, 2560), BF16),
        [HBM_BLOCK],
        pltpu.with_memory_space_constraint(blocks, pltpu.HBM),
        scratch=[pltpu.VMEM((4, CHUNK, 2560), F32), pltpu.SemaphoreType.DMA((4,))],
    )


def pick(values, index):
    out = jnp.zeros_like(values[0])
    for place, value in enumerate(values):
        out = jnp.where(index == place, value, out)
    return out


def put_rows(message, values):
    for r, value in enumerate(values):
        for c, width in enumerate((128, 128, 64)):
            row = 1 + 3 * r + c
            message[row : row + 1, 640 : 640 + width] = value[:, 128 * c : 128 * c + width]


def get_rows(pack):
    return [
        jnp.concatenate(
            [pack[1 + 3 * r : 2 + 3 * r], pack[2 + 3 * r : 3 + 3 * r], pack[3 + 3 * r : 4 + 3 * r, :64]], axis=1
        )
        for r in range(4)
    ]


def only_first_row(value):
    return jnp.where(lax.broadcasted_iota(jnp.int32, value.shape, 0) == 0, value, 0.0)


def ordered(kept, messages, place):
    for k, message in enumerate(messages):
        kept[k] = message[...]
    return [kept[lax.rem(place + (4 - j), 4)] for j in range(4)]


def first_middle_kernel(m0, m1, m2, m3, *refs):
    out, ordered_out, kept = refs[-3:]
    messages = ordered(kept, (m0, m1, m2, m3), lax.axis_index("day_1"))
    for j, message in enumerate(messages):
        ordered_out[j] = message
    pack = ring_sum([m[:, 640:] for m in (m0, m1, m2, m3)])
    out[:, 640:] = only_first_row(pack)
    chain = [get_rows(m[:, 640:]) for m in messages]
    alpha, beta = jnp.zeros((1, 320), F32), jnp.ones((1, 320), F32)
    alphas = [None] * 4
    for j in (3, 2, 1, 0):
        dec0, dec1, dom0, dom1 = chain[j]
        alphas[j] = alpha
        const = 1.0 / dom0 + dec1 * dec1 * (1.0 / dom1 + alpha)
        slope = dec1 * dec1 * beta
        alpha, beta = dec0 * dec0 * const, dec0 * dec0 * slope
    moved = jnp.ones((1, 320), F32)
    total_f = total_p = jnp.zeros((16, 320), F32)
    for j in range(4):
        dec0, dec1 = chain[j][:2]
        f, p = messages[j][:, :320], messages[j][:, 320:640]
        if j:
            moved = moved * dec0
        total_f = f + dec0 * dec1 * total_f
        total_p = total_p + moved * (p + alphas[j] * dec1 * f)
        moved = moved * dec1
    out[:, :320] = total_f
    out[:, 320:640] = total_p
    put_rows(out, (moved, const, slope, chain[0][0]))


def first_last_kernel(z0, z1, z2, z3, near, bx, *refs):
    co, w, v, message, kept = refs[-5:]
    group, place = lax.axis_index("day_0"), lax.axis_index("day_1")
    zero, one = jnp.zeros((1, 320), F32), jnp.ones((1, 320), F32)
    groups = ordered(kept, (z0, z1, z2, z3), group)
    chain = [get_rows(near[j, :, 640:]) for j in range(4)]
    whole_chain = [get_rows(m[:, 640:]) for m in groups]
    moved = [c[0] for c in whole_chain]
    first_decay = [c[3] for c in whole_chain] + [zero]
    exits, entry = [zero] * 4, [zero] * 5
    for g in (3, 2, 1, 0):
        entry[g] = whole_chain[g][1] + whole_chain[g][2] * exits[g]
        if g:
            exits[g - 1] = first_decay[g] * first_decay[g] * entry[g]
    dec0 = [c[0] for c in chain]
    dec1 = [c[1] for c in chain]
    after_decay = dec0[1:] + [pick(first_decay[1:], group)]
    gain0, gain1, after_gain = [None] * 4, [None] * 4, [None] * 4
    beyond = pick(exits, group)
    for j in (3, 2, 1, 0):
        after_gain[j] = beyond
        gain1[j] = 1.0 / chain[j][3] + beyond
        gain0[j] = 1.0 / chain[j][2] + dec1[j] * dec1[j] * gain1[j]
        beyond = dec0[j] * dec0[j] * gain0[j]
    next_gain = gain0[1:] + [pick(entry[1:], group)]
    mine = [dec1[j] * after_decay[j] for j in range(4)]
    whole = [moved[g] * first_decay[g + 1] for g in range(4)]

    def product(factors, low, high):
        kept = [
            jnp.where((low <= index) & (index < high), factor, one)
            for index, factor in enumerate(factors)
        ]
        return kept[0] * kept[1] * kept[2] * kept[3]

    rows = [pick(values, place) for values in (gain0, gain1, next_gain, dec0, dec1, after_decay)]
    local_f, local_b, total_f, total_b, far = [], [], [], [], []
    for k in range(4):
        source = lax.rem(place + (4 - k), 4)
        total_f.append(product(mine, source + 1, 4))
        total_b.append(product(mine, 0, source))
        if k:
            local_f.append(jnp.where(source < place, product(mine, source + 1, place), zero))
            local_b.append(jnp.where(source > place, product(mine, place + 1, source), zero))
            origin = lax.rem(group + (4 - k), 4)
            far.append(product(whole, jnp.minimum(origin, group) + 1, jnp.maximum(origin, group)))
    before, after = product(mine, 0, place), product(mine, place + 1, 4)
    rows += local_f + local_b + total_f + total_b + far + [before, after]
    for index, row in enumerate(rows):
        co[index : index + 1] = row

    come_f = come_b = far_f = far_b = jnp.zeros((16, 320), F32)
    for j in range(4):
        f, p = near[j, :, :320], near[j, :, 320:640]
        ahead = after_decay[j] * f
        behind = p + after_gain[j] * dec1[j] * f
        come_f = come_f + jnp.where(j < place, product(mine, j + 1, place) * ahead, 0.0)
        come_b = come_b + jnp.where(j > place, product(mine, place + 1, j) * behind, 0.0)
        f, p = groups[j][:, :320], groups[j][:, 320:640]
        ahead = first_decay[j + 1] * f
        behind = p + exits[j] * moved[j] * f
        far_f = far_f + jnp.where(j < group, product(whole, j + 1, group) * ahead, 0.0)
        far_b = far_b + jnp.where(j > group, product(whole, group + 1, j) * behind, 0.0)
    w[0], w[1], w[2] = bx[0], bx[1], jnp.zeros((16, 320), F32)
    pack = only_first_row(ring_sum([z[:, 640:] for z in (z0, z1, z2, z3)]))
    raise_days(come_f + before * far_f, come_b + after * far_b, w, co, v, message, pack)


def first_precondition(bx, message, early, late):
    pieces = ring_gather(message, "day_1")
    out, near = call(
        first_middle_kernel,
        "first_middle",
        (shaped(16, 768), shaped(4, 16, 768)),
        [VMEM_BLOCK] * 4 + [ANY_BLOCK],
        *pieces, early,
        scratch=[pltpu.VMEM((4, 16, 768), F32)],
    )
    field = shaped(3, 16, 320)
    return call(
        first_last_kernel,
        "first_last",
        (shaped(25, 320), field, field, shaped(16, 1088)),
        [VMEM_BLOCK] * 6 + [ANY_BLOCK],
        *ring_gather(out, "day_0"), near, bx, late,
        scratch=[pltpu.VMEM((4, 16, 768), F32)],
    )


def own_terms_kernel(a0, a1, o0, o1, own, out):
    out[0] = times_matrix(own[0], a0[...])
    out[1] = times_matrix(own[1], a1[...]) + times_matrix(own[0], o0[...])
    out[2] = times_matrix(own[1], o1[...])


def own_terms(pairs, own):
    return call(own_terms_kernel, "own_terms", shaped(3, 16, 2560), [VMEM_BLOCK] * 5, *pairs, own)


def rows_into(pairs, whole, out):
    for day in range(2):
        out[day] = times_rows(whole[day + 1], pairs[day][...])


def lanes(*values):
    lane = lax.broadcasted_iota(jnp.int32, (16, 64), 1)
    out = jnp.zeros((16, 64), F32)
    for index, value in enumerate(values):
        out = jnp.where(lane == index, value, out)
    return out


def first_rows_kernel(o0, o1, whole, bx, v1, out, dots):
    rows_into((o0, o1), whole, out)
    dots[...] = lanes(sum(row_sum(bx[day] * v1[day]) for day in range(2)))


def first_rows(*operands):
    return call(
        first_rows_kernel, "first_rows", (shaped(2, 16, 320), shaped(16, 64)), [VMEM_BLOCK] * 5, *operands
    )


def second_rows_kernel(o0, o1, whole, bx, v1, v2, w1, scalars, out, dots, r1, z1):
    rows_into((o0, o1), whole, out)
    step0 = scalars[:, 0:1]
    norm = cross = jnp.zeros((16, 1), F32)
    for day in range(3):
        z = v1[day] - step0 * v2[day]
        r = (bx[day] if day < 2 else 0.0) - step0 * w1[day]
        z1[day] = z
        r1[day] = r
        norm = norm + row_sum(r * z)
        cross = cross + row_sum(z * w1[day])
    dots[...] = lanes(norm, 0.0, cross)


def second_rows(*operands):
    own = shaped(3, 16, 320)
    return call(
        second_rows_kernel,
        "second_rows",
        (shaped(2, 16, 320), shaped(16, 64), own, own),
        [VMEM_BLOCK] * 8,
        *operands,
    )


def start_kernel(p0, p1, p2, p3, probes, grad_cov, own_chain, *refs):
    bx, message = refs[-2:]
    grad = ring_sum([p0[...], p1[...], p2[...], p3[...]])
    for day in range(2):
        bx[day, 0:1] = grad[day : day + 1]
        bx[day, 1:16] = probes[:, day, :]
    dec1 = own_chain[1:2]
    ahead = bx[1] + dec1 * bx[0]
    message[:, :320] = ahead
    message[:, 320:640] = bx[0] / own_chain[2:3] + dec1 * ahead / own_chain[3:4]
    message[:, 640:] = jnp.zeros((16, 128), F32)
    message[0:1, 640:704] = grad_cov[...]
    put_rows(message, [own_chain[r : r + 1] for r in range(4)])


def start_stage(*operands):
    return call(
        start_kernel,
        "start_stage",
        (shaped(2, 16, 320), shaped(16, 768)),
        [VMEM_BLOCK] * 7 + [ANY_BLOCK] * (len(operands) - 7),
        *operands,
    )


def image_kernel(p0, p1, p2, p3, rows, vector, cov_terms, dots, co, w, message):
    pieces = (p0, p1, p2, p3)
    total = jnp.zeros((16, 1), F32)
    for day in range(3):
        value = ring_sum([p[day] for p in pieces])
        if day < 2:
            value = value + rows[day]
        w[day] = value
        total = total + row_sum(vector[day] * value)
    ahead, behind = ring_message(w, co)
    message[:, :320] = ahead
    message[:, 320:640] = behind
    message[:, 640:704] = cov_terms[...]
    message[:, 704:] = dots[...] + lanes(0.0, total)


def image_stage(*operands):
    return call(
        image_kernel,
        "image_stage",
        (shaped(3, 16, 320), shaped(16, 768)),
        [VMEM_BLOCK] * 9,
        *operands,
    )


def assemble(mine, other, whole):
    row, core = lax.axis_index("blk_0"), lax.axis_index("blk_1")
    packs = []
    for k in range(4):
        at = pl.multiple_of(lax.rem(row + (4 - k), 4) * 640, 128)
        for day in range(3):
            a = mine[k, :, day * 320 : day * 320 + 320]
            b = other[k, :, day * 320 : day * 320 + 320]
            first = jnp.where(core == 0, a, b)
            second = jnp.where(core == 0, b, a)
            whole[day, :, pl.ds(at, 640)] = jnp.concatenate([first, second], axis=1)
        packs.append(mine[k, :, 960:1088] + other[k, :, 960:1088])
    return (packs[0] + packs[2]) + (packs[1] + packs[3])


def scatter_parts(obs, terms, kept, sent):
    core = lax.axis_index("blk_1")
    last = lax.axis_index("day_0") * 4 + lax.axis_index("day_1") == 15
    days = (obs[0] + terms[0], obs[1] + terms[1], jnp.where(last, 0.0, terms[2]))
    for day, part in enumerate(days):
        for row in range(4):
            first = part[:, row * 640 : row * 640 + 320]
            second = part[:, row * 640 + 320 : row * 640 + 640]
            kept[row, day] = jnp.where(core == 0, first, second)
            sent[row, day] = jnp.where(core == 0, second, first)


def observe(whole, cov, spread, covariates, weight):
    result = []
    for day in range(2):
        out = matmul(stacked_halves(whole[day]), spread[day], NN)
        out = (out[:16, :128] + out[16:, :128]) + (out[:16, 128:] + out[16:, 128:])
        predictor = out + times_matrix(cov, covariates[day])
        result.append((predictor, weight[day : day + 1] * predictor))
    return result


def spread_out(value, pair):
    high, low = halves(value)
    both = jnp.concatenate(
        [jnp.concatenate([high, high], axis=1), jnp.concatenate([low, low], axis=1)], axis=0
    )
    out = matmul(both, pair, NT)
    return out[:16] + out[16:]


def observe_back(observed, behind, spread, covariates, kept, sent, cov_terms):
    weights = [pair[1] for pair in observed]
    obs = [spread_out(weights[day], spread[day]) for day in range(2)]
    scatter_parts(obs, behind, kept, sent)
    cov_terms[...] = sum(times_rows(weights[day], covariates[day]) for day in range(2))


def row_sum(value):
    return jnp.sum(value, axis=1, keepdims=True)


PARTS = (shaped(4, 3, 16, 320), shaped(4, 3, 16, 320), shaped(16, 64))


def first_kernel(mine, other, probes_cov, spread, covariates, weight, behind, kept, sent, cov_terms, whole, cov):
    pack = assemble(mine, other, whole)
    cov[...] = jnp.where(
        lax.broadcasted_iota(jnp.int32, (16, 64), 0) == 0, pack[:, :64], probes_cov[...]
    )
    observed = observe(whole, cov[...], spread, covariates, weight)
    observe_back(observed, behind, spread, covariates, kept, sent, cov_terms)


def first_stage(mine, other, probes_cov, spread, covariates, weight, behind):
    return call(
        first_kernel,
        "first_stage",
        PARTS + (shaped(3, 16, 2560), shaped(16, 64)),
        [VMEM_BLOCK] * 7,
        mine, other, probes_cov, spread, covariates, weight, behind,
    )


def second_kernel(
    mine, other, whole1, c0, prior, spread, covariates, weight, behind1, behind2,
    kept, sent, cov_terms, whole2, whole, cov, hcov, scalars, behind,
):
    pack = assemble(mine, other, whole2)
    hcov1 = pack[:, :64] + prior[...] * c0[...]
    norm0 = pack[:, 64:65] + row_sum(c0[...] * c0[...])
    curve0 = pack[:, 65:66] + row_sum(c0[...] * hcov1)
    step0 = norm0 / curve0
    for day in range(3):
        whole[day] = whole1[day] - step0 * whole2[day]
    for day in range(3):
        behind[day] = behind1[day] - step0 * behind2[day]
    cov[...] = c0[...] - step0 * hcov1
    hcov[...] = hcov1
    lane = lax.broadcasted_iota(jnp.int32, (16, 128), 1)
    scalars[...] = jnp.where(lane == 0, step0, jnp.where(lane == 1, norm0, curve0))
    observed = observe(whole, cov[...], spread, covariates, weight)
    observe_back(observed, behind, spread, covariates, kept, sent, cov_terms)


def second_stage(mine, other, whole1, c0, prior, spread, covariates, weight, behind1, behind2):
    whole = shaped(3, 16, 2560)
    return call(
        second_kernel,
        "second_stage",
        PARTS + (whole, whole, shaped(16, 64), shaped(16, 64), shaped(16, 128)),
        [VMEM_BLOCK] * 10,
        mine, other, whole1, c0, prior, spread, covariates, weight, behind1, behind2,
        scratch=[pltpu.VMEM((3, 16, 2560), F32)],
    )


def third_kernel(
    mine, other, whole2, z1whole, scalars, c0, z1cov, hcov1, prior, spread, covariates, weight,
    a0, a1, o0, o1, r1, z1, w1, w2, v1, v2, v3,
    sums, z2, p1, scalars_out, covs, whole,
):
    pack = assemble(mine, other, whole)
    norm0, curve0 = scalars[:, 1:2], scalars[:, 2:3]
    hcov2 = pack[:, :64] + prior[...] * z1cov[...]
    norm1 = pack[:, 64:65] + row_sum(z1cov[...] * z1cov[...])
    beta1 = norm1 / norm0
    curve1 = (
        pack[:, 65:66]
        + row_sum(z1cov[...] * hcov2)
        + 2.0 * beta1 * (pack[:, 66:67] + row_sum(z1cov[...] * hcov1[...]))
        + beta1 * beta1 * curve0
    )
    step1 = norm1 / curve1
    hp1cov = hcov2 + beta1 * hcov1[...]
    r2cov = z1cov[...] - step1 * hp1cov
    covs[0] = r2cov
    covs[1] = z1cov[...] + beta1 * c0[...]
    own_norm = jnp.zeros((16, 1), F32)
    cross = jnp.zeros((16, 1), F32)
    for day in range(3):
        hp1 = w2[day] + beta1 * w1[day]
        r2 = r1[day] - step1 * hp1
        z2day = z1[day] - step1 * (v3[day] + beta1 * v2[day])
        own_norm = own_norm + row_sum(r2 * z2day)
        cross = cross + row_sum(z2day * hp1)
        if day < 2:
            z2[day] = z2day
            p1[day] = z1[day] + beta1 * v1[day]
        whole[day] = z1whole[day] - step1 * (whole[day] + beta1 * whole2[day])
    observed = observe(whole, r2cov, spread, covariates, weight)
    quadratic = sum(row_sum(predictor * weighted) for predictor, weighted in observed)
    for day in range(2):
        quadratic = quadratic + row_sum(times_matrix(z2[day], (a0, a1)[day][...]) * whole[day])
        quadratic = quadratic + 2.0 * row_sum(
            times_matrix(z2[day], (o0, o1)[day][...]) * whole[day + 1]
        )
    lane = lax.broadcasted_iota(jnp.int32, (16, 128), 1)
    sub = lax.broadcasted_iota(jnp.int32, (16, 128), 0)
    line = jnp.zeros((16, 128), F32)
    for index, value in enumerate((own_norm, quadratic, cross)):
        line = jnp.where(lane == sub + 16 * index, value, line)
    sums[...] = jnp.broadcast_to(jnp.sum(line, axis=0, keepdims=True), (128, 128))
    norm2cov = row_sum(r2cov * r2cov)
    quadcov = row_sum(r2cov * prior[...] * r2cov)
    crosscov = row_sum(r2cov * hp1cov)
    values = (scalars[:, 0:1], step1, norm1, curve1, norm2cov, quadcov, crosscov)
    out = jnp.zeros((16, 128), F32)
    for index, value in enumerate(values):
        out = jnp.where(lane == index, value, out)
    scalars_out[...] = out


def third_stage(*operands):
    own = shaped(2, 16, 320)
    return call(
        third_kernel,
        "third_stage",
        (shaped(128, 128), own, own, shaped(16, 128), shaped(2, 16, 64)),
        [VMEM_BLOCK] * len(operands),
        *operands,
        scratch=[pltpu.VMEM((3, 16, 2560), F32)],
    )


def final_kernel(sums, scalars, v1, p1, z2, c0, covs, field, cov):
    step0, step1, norm1, curve1, norm2cov, quadcov, crosscov = (
        scalars[:, i : i + 1] for i in range(7)
    )
    lane = lax.broadcasted_iota(jnp.int32, (16, 128), 1)
    sub = lax.broadcasted_iota(jnp.int32, (16, 128), 0)
    line = jnp.sum(sums[...], axis=0, keepdims=True)
    own_norm, quadratic, cross = (
        row_sum(jnp.where(lane == sub + 16 * index, line, 0.0)) for index in range(3)
    )
    norm2 = own_norm + norm2cov
    beta2 = norm2 / norm1
    curve2 = (
        quadratic + quadcov + 2.0 * beta2 * (cross + crosscov) + beta2 * beta2 * curve1
    )
    step2 = norm2 / curve2
    middle = step1 + step2 * beta2
    for day in range(2):
        field[:, day, :] = step0 * v1[day] + middle * p1[day] + step2 * z2[day]
    cov[...] = step0 * c0[...] + middle * covs[1] + step2 * covs[0]


def final_stage(*operands):
    return call(
        final_kernel,
        "final_stage",
        (shaped(16, 2, 320), shaped(16, 64)),
        [VMEM_BLOCK] * len(operands),
        *operands,
    )


def setup_kernel(count, triangles, cells, bary, prec, value, covs, spread, weight, kept, sent, grad_cov, covariates, table):
    core = lax.axis_index("blk_1")
    slot_start = (lax.axis_index("blk_0") * 2 + core) * 128
    cov_sum = jnp.zeros((1, 64), F32)
    table[...] = jnp.zeros((8, 5120), F32)
    table[0:3, 0:5116] = triangles[...].astype(F32)
    parts = stacked_halves(table[...])
    for day in range(2):
        cell = lax.broadcasted_iota(jnp.int32, (5120, 128), 0) == cells[day : day + 1, :]
        found = matmul(parts, jnp.where(cell, 1.0, 0.0).astype(BF16), NN)
        corners = (found[:8] + found[8:]).astype(jnp.int32)
        shares = [bary[k, day : day + 1, :] for k in range(3)]
        total = shares[0] + shares[1] + shares[2]
        nodes = lax.broadcasted_iota(jnp.int32, (2560, 128), 0)
        dense = jnp.zeros((2560, 128), F32)
        for k in range(3):
            dense = dense + jnp.where(nodes == corners[k : k + 1, :], shares[k] / total, 0.0)
        high, low = halves(dense)
        spread[day, :, :128] = high
        spread[day, :, 128:] = low
        covariates[day] = stacked_halves(covs[:, day, :])
        slot = lax.broadcasted_iota(jnp.int32, (1, 128), 1) + slot_start
        slot_weight = jnp.where(slot < count[day], prec[day : day + 1], 0.0)
        weight[day : day + 1] = slot_weight
        weighted_value = jnp.broadcast_to(slot_weight * value[day : day + 1], (16, 128))
        grad = spread_out(weighted_value, spread[day])[:1]
        for row in range(4):
            first = grad[:, row * 640 : row * 640 + 320]
            second = grad[:, row * 640 + 320 : row * 640 + 640]
            kept[row, day : day + 1] = jnp.where(core == 0, first, second)
            sent[row, day : day + 1] = jnp.where(core == 0, second, first)
        cov_sum = cov_sum + times_rows(weighted_value, covariates[day])[:1]
    grad_cov[...] = cov_sum


def setup_stage(*operands):
    return call(
        setup_kernel,
        "setup_stage",
        (
            pltpu.VMEM((2, 2560, 256), BF16), shaped(2, 128), shaped(4, 2, 320), shaped(4, 2, 320),
            shaped(1, 64), pltpu.VMEM((2, 128, 128), BF16),
        ),
        [SMEM_BLOCK] + [whole_block(o) for o in operands[1:]],
        operands[0],
        *(pltpu.with_memory_space_constraint(o, pltpu.HBM) for o in operands[1:]),
        grid=(1,),
        scratch=[pltpu.VMEM((8, 5120), F32)],
    )


def on_device(
    diag_blocks,
    off_blocks,
    leakage,
    obs_count,
    obs_triangle,
    obs_bary,
    obs_prec,
    obs_value,
    covariates,
    triangles,
    prior_prec,
    probes,
    probes_cov,
):
    row_start = lax.axis_index(BLK) * 320
    square = lax.dynamic_slice_in_dim(diag_blocks, row_start, 320, 2)
    rows = lax.broadcasted_iota(jnp.int32, (2, 320, 320), 1)
    columns = lax.broadcasted_iota(jnp.int32, (2, 320, 320), 2)
    dominant = jnp.sum(jnp.where(rows == columns, square, 0.0), axis=1)
    both = jnp.concatenate([1.0 - leakage, dominant])

    spread, weight, kept, sent, grad_cov, covs = setup_stage(
        obs_count, triangles, obs_triangle, obs_bary, obs_prec, obs_value, covariates
    )
    off_pair = [split_blocks(off_blocks, "split_off", day) for day in range(2)]
    diag_pair = [split_blocks(diag_blocks, "split_diag", day) for day in range(2)]
    bx, message = start_stage(*scattered_pieces(kept, sent), probes, grad_cov, both, off_pair[0])
    prior = prior_prec[None]
    padded_cov = jnp.pad(probes_cov, ((1, 0), (0, 0)))

    pairs = (*diag_pair, *off_pair)
    co, _, v1, message = first_precondition(bx, message, off_pair[1], diag_pair[0])
    nodes, behind1 = gather_nodes(message, own_terms(pairs, v1))
    kept, sent, cov1, whole1, c0 = first_stage(
        *nodes, padded_cov, spread, covs, weight, behind1
    )
    image, dots = first_rows(*off_pair, whole1, bx, v1)
    w1, message = image_stage(*scattered_pieces(kept, sent), image, v1, cov1, dots, co)

    v2, message = precondition(w1, message, co)
    nodes, behind2 = gather_nodes(message, own_terms(pairs, v2))
    kept, sent, cov2, whole2, z1whole, z1cov, hcov1, scalars = second_stage(
        *nodes, whole1, c0, prior, spread, covs, weight, behind1, behind2
    )
    image, dots, r1, z1 = second_rows(*off_pair, z1whole, bx, v1, v2, w1, scalars)
    w2, message = image_stage(*scattered_pieces(kept, sent), image, z1, cov2, dots, co)

    v3, message = precondition(w2, message, co)
    sums, z2, p1, scalars, covs2 = third_stage(
        *gather_nodes(message, behind2)[0], whole2, z1whole, scalars, c0, z1cov, hcov1, prior, spread, covs, weight,
        *pairs, r1, z1, w1, w2, v1, v2, v3,
    )
    sums = lax.all_to_all(sums, DAY + BLK, 0, 0, tiled=True)
    return final_stage(sums, scalars, v1, p1, z2, c0, covs2)


def solution(mesh):
    split = Mesh(mesh.devices.reshape(4, 4, 4, 2), ("day_0", "day_1", "blk_0", "blk_1"))
    in_specs = (
        P(DAY, BLK, None),
        P(DAY, BLK, None),
        P(DAY, BLK),
        P(DAY),
        P(DAY, BLK),
        P(None, DAY, BLK),
        P(DAY, BLK),
        P(DAY, BLK),
        P(None, DAY, BLK),
        P(),
        P(),
        P(None, DAY, BLK),
        P(),
    )
    out_specs = (P(None, DAY, BLK), P())
    return jax.shard_map(
        on_device, mesh=split, in_specs=in_specs, out_specs=out_specs, check_vma=False
    )
```

```python
import functools

import jax
import jax.numpy as jnp
from jax import lax
from jax.experimental import pallas as pl
from jax.experimental.pallas import tpu as pltpu
from jax.sharding import Mesh
from jax.sharding import PartitionSpec as P

DAY = ("day_0", "day_1")
BLK = ("blk_0", "blk_1")
F32 = jnp.float32
BF16 = jnp.bfloat16
NT = (((1,), (1,)), ((), ()))
NN = (((1,), (0,)), ((), ()))


def shift(value, axis, distance):
    size = lax.axis_size(axis)
    return lax.ppermute(value, axis, [(i, i ^ distance) for i in range(size)])


def swapped(value):
    return lax.ppermute(value, "blk_1", [(0, 1), (1, 0)])


def ring_gather(value, axis):
    return [value] + [shift(value, axis, k) for k in (1, 2, 3)]


def ring_sum(relative):
    return (relative[0] + relative[2]) + (relative[1] + relative[3])


def scattered_pieces(kept, sent):
    row = lax.axis_index("blk_0")
    half = kept + swapped(sent)
    pieces = [lax.dynamic_index_in_dim(half, row ^ k, 0, False) for k in range(4)]
    return [pieces[0]] + [shift(pieces[k], "blk_0", k) for k in (1, 2, 3)]


def gather_nodes(message, ready):
    column, ready = lax.optimization_barrier((jnp.stack(ring_gather(message, "blk_0")), ready))
    return (column, swapped(column)), ready


def ring_message(w, co):
    g0, g1, gg, d1, dg = co[0:1], co[1:2], co[2:3], co[4:5], co[5:6]
    ahead = dg * (w[1] + d1 * w[0]) + w[2]
    behind = g0 * w[0] + d1 * (g1 * w[1] + dg * gg * w[2])
    return ahead, behind


def weighted(co, first, values):
    return sum(co[first + k : first + k + 1] * value for k, value in enumerate(values))


def middle_kernel(m0, m1, m2, m3, co, *refs):
    out1, out2, out3, local = refs[-4:]
    middle_body(m0, m1, m2, m3, co, out1, out2, out3, local)


def middle_body(m0, m1, m2, m3, co, out1, out2, out3, local):
    messages = (m0, m1, m2, m3)
    fs = [m[:, :320] for m in messages]
    bs = [m[:, 320:640] for m in messages]
    pack = ring_sum([m[:, 640:] for m in messages])
    local[0] = weighted(co, 6, fs[1:])
    local[1] = weighted(co, 9, bs[1:])
    local[2] = jnp.zeros((16, 320), F32)
    local[2, :, :128] = pack
    total_f = weighted(co, 12, fs)
    total_b = weighted(co, 16, bs)
    group = lax.axis_index("day_0")
    for k, out in ((1, out1), (2, out2), (3, out3)):
        out[:, :320] = jnp.where((group ^ k) > group, total_f, total_b)
        out[:, 320:] = pack


def last_kernel(r1, r2, r3, local, w, co, *refs):
    last_body(r1, r2, r3, local, w, co, *refs[-2:])


def last_body(r1, r2, r3, local, w, co, v, message):
    group = lax.axis_index("day_0")
    far_f, far_b = jnp.zeros((16, 320), F32), jnp.zeros((16, 320), F32)
    packs = [local[2, :, :128]]
    for k, r in ((1, r1), (2, r2), (3, r3)):
        packs.append(r[:, 320:])
        value = co[19 + k : 20 + k] * r[:, :320]
        earlier = (group ^ k) < group
        far_f = far_f + jnp.where(earlier, value, 0.0)
        far_b = far_b + jnp.where(earlier, 0.0, value)
    come_f = local[0] + co[23:24] * far_f
    come_b = local[1] + co[24:25] * far_b
    raise_days(come_f, come_b, w, co, v, message, ring_sum(packs))


def raise_days(come_f, come_b, w, co, v, message, pack):
    g0, g1, gg, d1, dg = co[0:1], co[1:2], co[2:3], co[4:5], co[5:6]
    l0 = w[0] + come_f
    l1 = w[1] + d1 * l0
    u1 = dg * (come_b + gg * w[2])
    u0 = d1 * (g1 * w[1] + u1)
    days = (g0 * l0 + u0, g1 * l1 + u1, gg * (dg * l1 + w[2]) + come_b)
    for day, value in enumerate(days):
        v[day] = value
        message[:, day * 320 : day * 320 + 320] = value
    message[:, 960:] = pack


def precondition(w, message, co, early=(), late=()):
    pieces = ring_gather(message, "day_1")
    one = shaped(16, 448)
    *out, local = call(
        middle_kernel, "middle", (one, one, one, shaped(3, 16, 320)),
        [VMEM_BLOCK] * 5 + [ANY_BLOCK] * len(early), *pieces, co, *early,
    )
    got = [shift(out[k - 1], "day_0", k) for k in (1, 2, 3)]
    return call(
        last_kernel, "last", (shaped(3, 16, 320), shaped(16, 1088)),
        [VMEM_BLOCK] * 6 + [ANY_BLOCK] * len(late), *got, local, w, co, *late,
    )


def halves(value):
    high = value.astype(BF16)
    return high, (value - high.astype(F32)).astype(BF16)


def stacked_halves(value):
    return jnp.concatenate(halves(value), axis=0)


def matmul(first, second, dims):
    return lax.dot_general(first, second, dims, preferred_element_type=F32)


def times_rows(value, pair):
    n = pair.shape[0] // 2
    out = matmul(stacked_halves(value), pair, NT)
    return (out[:16, :n] + out[16:, :n]) + (out[:16, n:] + out[16:, n:])


def times_matrix(value, pair):
    high, low = halves(value)
    both = jnp.concatenate(
        [jnp.concatenate([high, high], axis=1), jnp.concatenate([low, low], axis=1)], axis=0
    )
    out = matmul(both, pair, NN)
    return out[:16] + out[16:]


VMEM_BLOCK = pl.BlockSpec(memory_space=pltpu.VMEM)
ANY_BLOCK = pl.BlockSpec(memory_space=pl.ANY)
HBM_BLOCK = pl.BlockSpec(memory_space=pltpu.HBM)


def shaped(*shape):
    return jax.ShapeDtypeStruct(shape, F32)


def whole_block(operand):
    return pl.BlockSpec(operand.shape, lambda i: (0,) * operand.ndim)


def call(kernel, name, outs, in_specs, *operands, scratch=(), limit=16, grid=()):
    return pl.pallas_call(
        kernel,
        grid=grid,
        out_shape=outs,
        in_specs=in_specs,
        out_specs=jax.tree.map(lambda _: VMEM_BLOCK, outs),
        scratch_shapes=scratch,
        compiler_params=pltpu.CompilerParams(vmem_limit_bytes=limit << 20),
        name=name,
    )(*operands)


CHUNK = 80


def split_kernel(day, source, target, buffer, sem):
    jobs = [(day, row) for row in range(0, 320, CHUNK)]

    def fetch(index):
        day, row = jobs[index]
        return pltpu.make_async_copy(source.at[day, pl.ds(row, CHUNK)], buffer.at[index], sem.at[index])

    for index in range(len(jobs)):
        fetch(index).start()
    for index, (day, row) in enumerate(jobs):
        fetch(index).wait()
        high, low = halves(buffer[index])
        target[pl.ds(row, CHUNK)] = high
        target[pl.ds(320 + row, CHUNK)] = low


def split_blocks(blocks, name, day):
    return call(
        functools.partial(split_kernel, day),
        name + str(day),
        pltpu.VMEM((640, 2560), BF16),
        [HBM_BLOCK],
        pltpu.with_memory_space_constraint(blocks, pltpu.HBM),
        scratch=[pltpu.VMEM((4, CHUNK, 2560), F32), pltpu.SemaphoreType.DMA((4,))],
    )


def pick(values, index):
    out = jnp.zeros_like(values[0])
    for place, value in enumerate(values):
        out = jnp.where(index == place, value, out)
    return out


def put_rows(message, values):
    for r, value in enumerate(values):
        for c, width in enumerate((128, 128, 64)):
            row = 1 + 3 * r + c
            message[row : row + 1, 640 : 640 + width] = value[:, 128 * c : 128 * c + width]


def get_rows(pack):
    return [
        jnp.concatenate(
            [pack[1 + 3 * r : 2 + 3 * r], pack[2 + 3 * r : 3 + 3 * r], pack[3 + 3 * r : 4 + 3 * r, :64]], axis=1
        )
        for r in range(4)
    ]


def only_first_row(value):
    return jnp.where(lax.broadcasted_iota(jnp.int32, value.shape, 0) == 0, value, 0.0)


def ordered(kept, messages, place):
    for k, message in enumerate(messages):
        kept[k] = message[...]
    return [kept[place ^ j] for j in range(4)]


def first_middle_kernel(m0, m1, m2, m3, *refs):
    out, ordered_out, kept = refs[-3:]
    messages = ordered(kept, (m0, m1, m2, m3), lax.axis_index("day_1"))
    for j, message in enumerate(messages):
        ordered_out[j] = message
    pack = ring_sum([m[:, 640:] for m in (m0, m1, m2, m3)])
    out[:, 640:] = only_first_row(pack)
    chain = [get_rows(m[:, 640:]) for m in messages]
    alpha, beta = jnp.zeros((1, 320), F32), jnp.ones((1, 320), F32)
    alphas = [None] * 4
    for j in (3, 2, 1, 0):
        dec0, dec1, dom0, dom1 = chain[j]
        alphas[j] = alpha
        const = 1.0 / dom0 + dec1 * dec1 * (1.0 / dom1 + alpha)
        slope = dec1 * dec1 * beta
        alpha, beta = dec0 * dec0 * const, dec0 * dec0 * slope
    moved = jnp.ones((1, 320), F32)
    total_f = total_p = jnp.zeros((16, 320), F32)
    for j in range(4):
        dec0, dec1 = chain[j][:2]
        f, p = messages[j][:, :320], messages[j][:, 320:640]
        if j:
            moved = moved * dec0
        total_f = f + dec0 * dec1 * total_f
        total_p = total_p + moved * (p + alphas[j] * dec1 * f)
        moved = moved * dec1
    out[:, :320] = total_f
    out[:, 320:640] = total_p
    put_rows(out, (moved, const, slope, chain[0][0]))


def first_last_kernel(z0, z1, z2, z3, near, bx, *refs):
    co, w, v, message, kept = refs[-5:]
    group, place = lax.axis_index("day_0"), lax.axis_index("day_1")
    zero, one = jnp.zeros((1, 320), F32), jnp.ones((1, 320), F32)
    groups = ordered(kept, (z0, z1, z2, z3), group)
    chain = [get_rows(near[j, :, 640:]) for j in range(4)]
    whole_chain = [get_rows(m[:, 640:]) for m in groups]
    moved = [c[0] for c in whole_chain]
    first_decay = [c[3] for c in whole_chain] + [zero]
    exits, entry = [zero] * 4, [zero] * 5
    for g in (3, 2, 1, 0):
        entry[g] = whole_chain[g][1] + whole_chain[g][2] * exits[g]
        if g:
            exits[g - 1] = first_decay[g] * first_decay[g] * entry[g]
    dec0 = [c[0] for c in chain]
    dec1 = [c[1] for c in chain]
    after_decay = dec0[1:] + [pick(first_decay[1:], group)]
    gain0, gain1, after_gain = [None] * 4, [None] * 4, [None] * 4
    beyond = pick(exits, group)
    for j in (3, 2, 1, 0):
        after_gain[j] = beyond
        gain1[j] = 1.0 / chain[j][3] + beyond
        gain0[j] = 1.0 / chain[j][2] + dec1[j] * dec1[j] * gain1[j]
        beyond = dec0[j] * dec0[j] * gain0[j]
    next_gain = gain0[1:] + [pick(entry[1:], group)]
    mine = [dec1[j] * after_decay[j] for j in range(4)]
    whole = [moved[g] * first_decay[g + 1] for g in range(4)]

    def product(factors, low, high):
        kept = [
            jnp.where((low <= index) & (index < high), factor, one)
            for index, factor in enumerate(factors)
        ]
        return kept[0] * kept[1] * kept[2] * kept[3]

    rows = [pick(values, place) for values in (gain0, gain1, next_gain, dec0, dec1, after_decay)]
    local_f, local_b, total_f, total_b, far = [], [], [], [], []
    for k in range(4):
        source = place ^ k
        total_f.append(product(mine, source + 1, 4))
        total_b.append(product(mine, 0, source))
        if k:
            local_f.append(jnp.where(source < place, product(mine, source + 1, place), zero))
            local_b.append(jnp.where(source > place, product(mine, place + 1, source), zero))
            origin = group ^ k
            far.append(product(whole, jnp.minimum(origin, group) + 1, jnp.maximum(origin, group)))
    before, after = product(mine, 0, place), product(mine, place + 1, 4)
    rows += local_f + local_b + total_f + total_b + far + [before, after]
    for index, row in enumerate(rows):
        co[index : index + 1] = row

    come_f = come_b = far_f = far_b = jnp.zeros((16, 320), F32)
    for j in range(4):
        f, p = near[j, :, :320], near[j, :, 320:640]
        ahead = after_decay[j] * f
        behind = p + after_gain[j] * dec1[j] * f
        come_f = come_f + jnp.where(j < place, product(mine, j + 1, place) * ahead, 0.0)
        come_b = come_b + jnp.where(j > place, product(mine, place + 1, j) * behind, 0.0)
        f, p = groups[j][:, :320], groups[j][:, 320:640]
        ahead = first_decay[j + 1] * f
        behind = p + exits[j] * moved[j] * f
        far_f = far_f + jnp.where(j < group, product(whole, j + 1, group) * ahead, 0.0)
        far_b = far_b + jnp.where(j > group, product(whole, group + 1, j) * behind, 0.0)
    w[0], w[1], w[2] = bx[0], bx[1], jnp.zeros((16, 320), F32)
    pack = only_first_row(ring_sum([z[:, 640:] for z in (z0, z1, z2, z3)]))
    raise_days(come_f + before * far_f, come_b + after * far_b, w, co, v, message, pack)


def first_precondition(bx, message, early, late):
    pieces = ring_gather(message, "day_1")
    out, near = call(
        first_middle_kernel,
        "first_middle",
        (shaped(16, 768), shaped(4, 16, 768)),
        [VMEM_BLOCK] * 4 + [ANY_BLOCK],
        *pieces, early,
        scratch=[pltpu.VMEM((4, 16, 768), F32)],
    )
    field = shaped(3, 16, 320)
    return call(
        first_last_kernel,
        "first_last",
        (shaped(25, 320), field, field, shaped(16, 1088)),
        [VMEM_BLOCK] * 6 + [ANY_BLOCK],
        *ring_gather(out, "day_0"), near, bx, late,
        scratch=[pltpu.VMEM((4, 16, 768), F32)],
    )


def own_terms_kernel(a0, a1, o0, o1, own, out):
    out[0] = times_matrix(own[0], a0[...])
    out[1] = times_matrix(own[1], a1[...]) + times_matrix(own[0], o0[...])
    out[2] = times_matrix(own[1], o1[...])


def own_terms(pairs, own):
    return call(own_terms_kernel, "own_terms", shaped(3, 16, 2560), [VMEM_BLOCK] * 5, *pairs, own)


def rows_into(pairs, whole, out):
    for day in range(2):
        out[day] = times_rows(whole[day + 1], pairs[day][...])


def lanes(*values):
    lane = lax.broadcasted_iota(jnp.int32, (16, 64), 1)
    out = jnp.zeros((16, 64), F32)
    for index, value in enumerate(values):
        out = jnp.where(lane == index, value, out)
    return out


def first_rows_kernel(o0, o1, whole, bx, v1, out, dots):
    rows_into((o0, o1), whole, out)
    dots[...] = lanes(sum(row_sum(bx[day] * v1[day]) for day in range(2)))


def first_rows(*operands):
    return call(
        first_rows_kernel, "first_rows", (shaped(2, 16, 320), shaped(16, 64)), [VMEM_BLOCK] * 5, *operands
    )


def second_rows_kernel(o0, o1, whole, bx, v1, v2, w1, scalars, out, dots, r1, z1):
    rows_into((o0, o1), whole, out)
    step0 = scalars[:, 0:1]
    norm = cross = jnp.zeros((16, 1), F32)
    for day in range(3):
        z = v1[day] - step0 * v2[day]
        r = (bx[day] if day < 2 else 0.0) - step0 * w1[day]
        z1[day] = z
        r1[day] = r
        norm = norm + row_sum(r * z)
        cross = cross + row_sum(z * w1[day])
    dots[...] = lanes(norm, 0.0, cross)


def second_rows(*operands):
    own = shaped(3, 16, 320)
    return call(
        second_rows_kernel,
        "second_rows",
        (shaped(2, 16, 320), shaped(16, 64), own, own),
        [VMEM_BLOCK] * 8,
        *operands,
    )


def start_kernel(p0, p1, p2, p3, probes, grad_cov, own_chain, *refs):
    bx, message = refs[-2:]
    grad = ring_sum([p0[...], p1[...], p2[...], p3[...]])
    for day in range(2):
        bx[day, 0:1] = grad[day : day + 1]
        bx[day, 1:16] = probes[:, day, :]
    dec1 = own_chain[1:2]
    ahead = bx[1] + dec1 * bx[0]
    message[:, :320] = ahead
    message[:, 320:640] = bx[0] / own_chain[2:3] + dec1 * ahead / own_chain[3:4]
    message[:, 640:] = jnp.zeros((16, 128), F32)
    message[0:1, 640:704] = grad_cov[...]
    put_rows(message, [own_chain[r : r + 1] for r in range(4)])


def start_stage(*operands):
    return call(
        start_kernel,
        "start_stage",
        (shaped(2, 16, 320), shaped(16, 768)),
        [VMEM_BLOCK] * 7 + [ANY_BLOCK] * (len(operands) - 7),
        *operands,
    )


def image_kernel(p0, p1, p2, p3, rows, vector, cov_terms, dots, co, w, message):
    pieces = (p0, p1, p2, p3)
    total = jnp.zeros((16, 1), F32)
    for day in range(3):
        value = ring_sum([p[day] for p in pieces])
        if day < 2:
            value = value + rows[day]
        w[day] = value
        total = total + row_sum(vector[day] * value)
    ahead, behind = ring_message(w, co)
    message[:, :320] = ahead
    message[:, 320:640] = behind
    message[:, 640:704] = cov_terms[...]
    message[:, 704:] = dots[...] + lanes(0.0, total)


def image_stage(*operands):
    return call(
        image_kernel,
        "image_stage",
        (shaped(3, 16, 320), shaped(16, 768)),
        [VMEM_BLOCK] * 9,
        *operands,
    )


def assemble(mine, other, whole):
    row, core = lax.axis_index("blk_0"), lax.axis_index("blk_1")
    packs = []
    for k in range(4):
        at = pl.multiple_of((row ^ k) * 640, 128)
        for day in range(3):
            a = mine[k, :, day * 320 : day * 320 + 320]
            b = other[k, :, day * 320 : day * 320 + 320]
            first = jnp.where(core == 0, a, b)
            second = jnp.where(core == 0, b, a)
            whole[day, :, pl.ds(at, 640)] = jnp.concatenate([first, second], axis=1)
        packs.append(mine[k, :, 960:1088] + other[k, :, 960:1088])
    return (packs[0] + packs[2]) + (packs[1] + packs[3])


def scatter_parts(obs, terms, kept, sent):
    core = lax.axis_index("blk_1")
    last = lax.axis_index("day_0") * 4 + lax.axis_index("day_1") == 15
    days = (obs[0] + terms[0], obs[1] + terms[1], jnp.where(last, 0.0, terms[2]))
    for day, part in enumerate(days):
        for row in range(4):
            first = part[:, row * 640 : row * 640 + 320]
            second = part[:, row * 640 + 320 : row * 640 + 640]
            kept[row, day] = jnp.where(core == 0, first, second)
            sent[row, day] = jnp.where(core == 0, second, first)


def observe(whole, cov, spread, covariates, weight):
    result = []
    for day in range(2):
        out = matmul(stacked_halves(whole[day]), spread[day], NN)
        out = (out[:16, :128] + out[16:, :128]) + (out[:16, 128:] + out[16:, 128:])
        predictor = out + times_matrix(cov, covariates[day])
        result.append((predictor, weight[day : day + 1] * predictor))
    return result


def spread_out(value, pair):
    high, low = halves(value)
    both = jnp.concatenate(
        [jnp.concatenate([high, high], axis=1), jnp.concatenate([low, low], axis=1)], axis=0
    )
    out = matmul(both, pair, NT)
    return out[:16] + out[16:]


def observe_back(observed, behind, spread, covariates, kept, sent, cov_terms):
    weights = [pair[1] for pair in observed]
    obs = [spread_out(weights[day], spread[day]) for day in range(2)]
    scatter_parts(obs, behind, kept, sent)
    cov_terms[...] = sum(times_rows(weights[day], covariates[day]) for day in range(2))


def row_sum(value):
    return jnp.sum(value, axis=1, keepdims=True)


PARTS = (shaped(4, 3, 16, 320), shaped(4, 3, 16, 320), shaped(16, 64))


def first_kernel(mine, other, probes_cov, spread, covariates, weight, behind, kept, sent, cov_terms, whole, cov):
    pack = assemble(mine, other, whole)
    cov[...] = jnp.where(
        lax.broadcasted_iota(jnp.int32, (16, 64), 0) == 0, pack[:, :64], probes_cov[...]
    )
    observed = observe(whole, cov[...], spread, covariates, weight)
    observe_back(observed, behind, spread, covariates, kept, sent, cov_terms)


def first_stage(mine, other, probes_cov, spread, covariates, weight, behind):
    return call(
        first_kernel,
        "first_stage",
        PARTS + (shaped(3, 16, 2560), shaped(16, 64)),
        [VMEM_BLOCK] * 7,
        mine, other, probes_cov, spread, covariates, weight, behind,
    )


def second_kernel(
    mine, other, whole1, c0, prior, spread, covariates, weight, behind1, behind2,
    kept, sent, cov_terms, whole2, whole, cov, hcov, scalars, behind,
):
    pack = assemble(mine, other, whole2)
    hcov1 = pack[:, :64] + prior[...] * c0[...]
    norm0 = pack[:, 64:65] + row_sum(c0[...] * c0[...])
    curve0 = pack[:, 65:66] + row_sum(c0[...] * hcov1)
    step0 = norm0 / curve0
    for day in range(3):
        whole[day] = whole1[day] - step0 * whole2[day]
    for day in range(3):
        behind[day] = behind1[day] - step0 * behind2[day]
    cov[...] = c0[...] - step0 * hcov1
    hcov[...] = hcov1
    lane = lax.broadcasted_iota(jnp.int32, (16, 128), 1)
    scalars[...] = jnp.where(lane == 0, step0, jnp.where(lane == 1, norm0, curve0))
    observed = observe(whole, cov[...], spread, covariates, weight)
    observe_back(observed, behind, spread, covariates, kept, sent, cov_terms)


def second_stage(mine, other, whole1, c0, prior, spread, covariates, weight, behind1, behind2):
    whole = shaped(3, 16, 2560)
    return call(
        second_kernel,
        "second_stage",
        PARTS + (whole, whole, shaped(16, 64), shaped(16, 64), shaped(16, 128)),
        [VMEM_BLOCK] * 10,
        mine, other, whole1, c0, prior, spread, covariates, weight, behind1, behind2,
        scratch=[pltpu.VMEM((3, 16, 2560), F32)],
    )


def third_kernel(
    mine, other, whole2, z1whole, scalars, c0, z1cov, hcov1, prior, spread, covariates, weight,
    a0, a1, o0, o1, r1, z1, w1, w2, v1, v2, v3,
    sums, z2, p1, scalars_out, covs, whole,
):
    pack = assemble(mine, other, whole)
    norm0, curve0 = scalars[:, 1:2], scalars[:, 2:3]
    hcov2 = pack[:, :64] + prior[...] * z1cov[...]
    norm1 = pack[:, 64:65] + row_sum(z1cov[...] * z1cov[...])
    beta1 = norm1 / norm0
    curve1 = (
        pack[:, 65:66]
        + row_sum(z1cov[...] * hcov2)
        + 2.0 * beta1 * (pack[:, 66:67] + row_sum(z1cov[...] * hcov1[...]))
        + beta1 * beta1 * curve0
    )
    step1 = norm1 / curve1
    hp1cov = hcov2 + beta1 * hcov1[...]
    r2cov = z1cov[...] - step1 * hp1cov
    covs[0] = r2cov
    covs[1] = z1cov[...] + beta1 * c0[...]
    own_norm = jnp.zeros((16, 1), F32)
    cross = jnp.zeros((16, 1), F32)
    for day in range(3):
        hp1 = w2[day] + beta1 * w1[day]
        r2 = r1[day] - step1 * hp1
        z2day = z1[day] - step1 * (v3[day] + beta1 * v2[day])
        own_norm = own_norm + row_sum(r2 * z2day)
        cross = cross + row_sum(z2day * hp1)
        if day < 2:
            z2[day] = z2day
            p1[day] = z1[day] + beta1 * v1[day]
        whole[day] = z1whole[day] - step1 * (whole[day] + beta1 * whole2[day])
    observed = observe(whole, r2cov, spread, covariates, weight)
    quadratic = sum(row_sum(predictor * weighted) for predictor, weighted in observed)
    for day in range(2):
        quadratic = quadratic + row_sum(times_matrix(z2[day], (a0, a1)[day][...]) * whole[day])
        quadratic = quadratic + 2.0 * row_sum(
            times_matrix(z2[day], (o0, o1)[day][...]) * whole[day + 1]
        )
    lane = lax.broadcasted_iota(jnp.int32, (16, 128), 1)
    sub = lax.broadcasted_iota(jnp.int32, (16, 128), 0)
    line = jnp.zeros((16, 128), F32)
    for index, value in enumerate((own_norm, quadratic, cross)):
        line = jnp.where(lane == sub + 16 * index, value, line)
    sums[...] = jnp.broadcast_to(jnp.sum(line, axis=0, keepdims=True), (128, 128))
    norm2cov = row_sum(r2cov * r2cov)
    quadcov = row_sum(r2cov * prior[...] * r2cov)
    crosscov = row_sum(r2cov * hp1cov)
    values = (scalars[:, 0:1], step1, norm1, curve1, norm2cov, quadcov, crosscov)
    out = jnp.zeros((16, 128), F32)
    for index, value in enumerate(values):
        out = jnp.where(lane == index, value, out)
    scalars_out[...] = out


def third_stage(*operands):
    own = shaped(2, 16, 320)
    return call(
        third_kernel,
        "third_stage",
        (shaped(128, 128), own, own, shaped(16, 128), shaped(2, 16, 64)),
        [VMEM_BLOCK] * len(operands),
        *operands,
        scratch=[pltpu.VMEM((3, 16, 2560), F32)],
    )


def final_kernel(sums, scalars, v1, p1, z2, c0, covs, field, cov):
    step0, step1, norm1, curve1, norm2cov, quadcov, crosscov = (
        scalars[:, i : i + 1] for i in range(7)
    )
    lane = lax.broadcasted_iota(jnp.int32, (16, 128), 1)
    sub = lax.broadcasted_iota(jnp.int32, (16, 128), 0)
    line = jnp.sum(sums[...], axis=0, keepdims=True)
    own_norm, quadratic, cross = (
        row_sum(jnp.where(lane == sub + 16 * index, line, 0.0)) for index in range(3)
    )
    norm2 = own_norm + norm2cov
    beta2 = norm2 / norm1
    curve2 = (
        quadratic + quadcov + 2.0 * beta2 * (cross + crosscov) + beta2 * beta2 * curve1
    )
    step2 = norm2 / curve2
    middle = step1 + step2 * beta2
    for day in range(2):
        field[:, day, :] = step0 * v1[day] + middle * p1[day] + step2 * z2[day]
    cov[...] = step0 * c0[...] + middle * covs[1] + step2 * covs[0]


def final_stage(*operands):
    return call(
        final_kernel,
        "final_stage",
        (shaped(16, 2, 320), shaped(16, 64)),
        [VMEM_BLOCK] * len(operands),
        *operands,
    )


def setup_kernel(count, triangles, cells, bary, prec, value, covs, spread, weight, kept, sent, grad_cov, covariates, table):
    core = lax.axis_index("blk_1")
    slot_start = (lax.axis_index("blk_0") * 2 + core) * 128
    cov_sum = jnp.zeros((1, 64), F32)
    table[...] = jnp.zeros((8, 5120), F32)
    table[0:3, 0:5116] = triangles[...].astype(F32)
    parts = stacked_halves(table[...])
    for day in range(2):
        cell = lax.broadcasted_iota(jnp.int32, (5120, 128), 0) == cells[day : day + 1, :]
        found = matmul(parts, jnp.where(cell, 1.0, 0.0).astype(BF16), NN)
        corners = (found[:8] + found[8:]).astype(jnp.int32)
        shares = [bary[k, day : day + 1, :] for k in range(3)]
        total = shares[0] + shares[1] + shares[2]
        nodes = lax.broadcasted_iota(jnp.int32, (2560, 128), 0)
        dense = jnp.zeros((2560, 128), F32)
        for k in range(3):
            dense = dense + jnp.where(nodes == corners[k : k + 1, :], shares[k] / total, 0.0)
        high, low = halves(dense)
        spread[day, :, :128] = high
        spread[day, :, 128:] = low
        covariates[day] = stacked_halves(covs[:, day, :])
        slot = lax.broadcasted_iota(jnp.int32, (1, 128), 1) + slot_start
        slot_weight = jnp.where(slot < count[0:1, day : day + 1], prec[day : day + 1], 0.0)
        weight[day : day + 1] = slot_weight
        weighted_value = jnp.broadcast_to(slot_weight * value[day : day + 1], (16, 128))
        grad = spread_out(weighted_value, spread[day])[:1]
        for row in range(4):
            first = grad[:, row * 640 : row * 640 + 320]
            second = grad[:, row * 640 + 320 : row * 640 + 640]
            kept[row, day : day + 1] = jnp.where(core == 0, first, second)
            sent[row, day : day + 1] = jnp.where(core == 0, second, first)
        cov_sum = cov_sum + times_rows(weighted_value, covariates[day])[:1]
    grad_cov[...] = cov_sum


def setup_stage(*operands):
    return call(
        setup_kernel,
        "setup_stage",
        (
            pltpu.VMEM((2, 2560, 256), BF16), shaped(2, 128), shaped(4, 2, 320), shaped(4, 2, 320),
            shaped(1, 64), pltpu.VMEM((2, 128, 128), BF16),
        ),
        [whole_block(o) for o in operands],
        *(pltpu.with_memory_space_constraint(o, pltpu.HBM) for o in operands),
        grid=(1,),
        scratch=[pltpu.VMEM((8, 5120), F32)],
    )


def on_device(
    diag_blocks,
    off_blocks,
    leakage,
    obs_count,
    obs_triangle,
    obs_bary,
    obs_prec,
    obs_value,
    covariates,
    triangles,
    prior_prec,
    probes,
    probes_cov,
):
    row_start = lax.axis_index(BLK) * 320
    square = lax.dynamic_slice_in_dim(diag_blocks, row_start, 320, 2)
    rows = lax.broadcasted_iota(jnp.int32, (2, 320, 320), 1)
    columns = lax.broadcasted_iota(jnp.int32, (2, 320, 320), 2)
    dominant = jnp.sum(jnp.where(rows == columns, square, 0.0), axis=1)
    both = jnp.concatenate([1.0 - leakage, dominant])

    spread, weight, kept, sent, grad_cov, covs = setup_stage(
        obs_count.reshape(1, 2), triangles, obs_triangle, obs_bary, obs_prec, obs_value, covariates
    )
    off_pair = [split_blocks(off_blocks, "split_off", day) for day in range(2)]
    diag_pair = [split_blocks(diag_blocks, "split_diag", day) for day in range(2)]
    bx, message = start_stage(*scattered_pieces(kept, sent), probes, grad_cov, both, off_pair[0])
    prior = prior_prec[None]
    padded_cov = jnp.pad(probes_cov, ((1, 0), (0, 0)))

    pairs = (*diag_pair, *off_pair)
    co, _, v1, message = first_precondition(bx, message, off_pair[1], diag_pair[0])
    nodes, behind1 = gather_nodes(message, own_terms(pairs, v1))
    kept, sent, cov1, whole1, c0 = first_stage(
        *nodes, padded_cov, spread, covs, weight, behind1
    )
    image, dots = first_rows(*off_pair, whole1, bx, v1)
    w1, message = image_stage(*scattered_pieces(kept, sent), image, v1, cov1, dots, co)

    v2, message = precondition(w1, message, co)
    nodes, behind2 = gather_nodes(message, own_terms(pairs, v2))
    kept, sent, cov2, whole2, z1whole, z1cov, hcov1, scalars = second_stage(
        *nodes, whole1, c0, prior, spread, covs, weight, behind1, behind2
    )
    image, dots, r1, z1 = second_rows(*off_pair, z1whole, bx, v1, v2, w1, scalars)
    w2, message = image_stage(*scattered_pieces(kept, sent), image, z1, cov2, dots, co)

    v3, message = precondition(w2, message, co)
    sums, z2, p1, scalars, covs2 = third_stage(
        *gather_nodes(message, behind2)[0], whole2, z1whole, scalars, c0, z1cov, hcov1, prior, spread, covs, weight,
        *pairs, r1, z1, w1, w2, v1, v2, v3,
    )
    sums = lax.all_to_all(sums, DAY + BLK, 0, 0, tiled=True)
    return final_stage(sums, scalars, v1, p1, z2, c0, covs2)


def solution(mesh):
    split = Mesh(mesh.devices.reshape(4, 4, 4, 2), ("day_0", "day_1", "blk_0", "blk_1"))
    in_specs = (
        P(DAY, BLK, None),
        P(DAY, BLK, None),
        P(DAY, BLK),
        P(DAY),
        P(DAY, BLK),
        P(None, DAY, BLK),
        P(DAY, BLK),
        P(DAY, BLK),
        P(None, DAY, BLK),
        P(),
        P(),
        P(None, DAY, BLK),
        P(),
    )
    out_specs = (P(None, DAY, BLK), P())
    return jax.shard_map(
        on_device, mesh=split, in_specs=in_specs, out_specs=out_specs, check_vma=False
    )
```

```python
import functools

import jax
import jax.numpy as jnp
from jax import lax
from jax.experimental import pallas as pl
from jax.experimental.pallas import tpu as pltpu
from jax.sharding import Mesh
from jax.sharding import PartitionSpec as P

DAY = ("day_0", "day_1")
BLK = ("blk_0", "blk_1")
F32 = jnp.float32
BF16 = jnp.bfloat16
NT = (((1,), (1,)), ((), ()))
NN = (((1,), (0,)), ((), ()))


def shift(value, axis, distance):
    size = lax.axis_size(axis)
    return lax.ppermute(value, axis, [(i, i ^ distance) for i in range(size)])


def swapped(value):
    return lax.ppermute(value, "blk_1", [(0, 1), (1, 0)])


def ring_gather(value, axis):
    return [value] + [shift(value, axis, k) for k in (1, 2, 3)]


def ring_sum(relative):
    return (relative[0] + relative[2]) + (relative[1] + relative[3])


def scattered_pieces(kept, sent):
    row = lax.axis_index("blk_0")
    half = kept + swapped(sent)
    pieces = [lax.dynamic_index_in_dim(half, row ^ k, 0, False) for k in range(4)]
    return [pieces[0]] + [shift(pieces[k], "blk_0", k) for k in (1, 2, 3)]


def gather_nodes(message, ready):
    column, ready = lax.optimization_barrier((jnp.stack(ring_gather(message, "blk_0")), ready))
    return (column, swapped(column)), ready


def ring_message(w, co):
    g0, g1, gg, d1, dg = co[0:1], co[1:2], co[2:3], co[4:5], co[5:6]
    ahead = dg * (w[1] + d1 * w[0]) + w[2]
    behind = g0 * w[0] + d1 * (g1 * w[1] + dg * gg * w[2])
    return ahead, behind


def weighted(co, first, values):
    return sum(co[first + k : first + k + 1] * value for k, value in enumerate(values))


def middle_kernel(m0, m1, m2, m3, co, *refs):
    out1, out2, out3, local = refs[-4:]
    middle_body(m0, m1, m2, m3, co, out1, out2, out3, local)


def middle_body(m0, m1, m2, m3, co, out1, out2, out3, local):
    messages = (m0, m1, m2, m3)
    fs = [m[:, :320] for m in messages]
    bs = [m[:, 320:640] for m in messages]
    pack = ring_sum([m[:, 640:] for m in messages])
    local[0] = weighted(co, 6, fs[1:])
    local[1] = weighted(co, 9, bs[1:])
    local[2] = jnp.zeros((16, 320), F32)
    local[2, :, :128] = pack
    total_f = weighted(co, 12, fs)
    total_b = weighted(co, 16, bs)
    group = lax.axis_index("day_0")
    for k, out in ((1, out1), (2, out2), (3, out3)):
        out[:, :320] = jnp.where((group ^ k) > group, total_f, total_b)
        out[:, 320:] = pack


def last_kernel(r1, r2, r3, local, w, co, *refs):
    last_body(r1, r2, r3, local, w, co, *refs[-2:])


def last_body(r1, r2, r3, local, w, co, v, message):
    group = lax.axis_index("day_0")
    far_f, far_b = jnp.zeros((16, 320), F32), jnp.zeros((16, 320), F32)
    packs = [local[2, :, :128]]
    for k, r in ((1, r1), (2, r2), (3, r3)):
        packs.append(r[:, 320:])
        value = co[19 + k : 20 + k] * r[:, :320]
        earlier = (group ^ k) < group
        far_f = far_f + jnp.where(earlier, value, 0.0)
        far_b = far_b + jnp.where(earlier, 0.0, value)
    come_f = local[0] + co[23:24] * far_f
    come_b = local[1] + co[24:25] * far_b
    raise_days(come_f, come_b, w, co, v, message, ring_sum(packs))


def raise_days(come_f, come_b, w, co, v, message, pack):
    g0, g1, gg, d1, dg = co[0:1], co[1:2], co[2:3], co[4:5], co[5:6]
    l0 = w[0] + come_f
    l1 = w[1] + d1 * l0
    u1 = dg * (come_b + gg * w[2])
    u0 = d1 * (g1 * w[1] + u1)
    days = (g0 * l0 + u0, g1 * l1 + u1, gg * (dg * l1 + w[2]) + come_b)
    for day, value in enumerate(days):
        v[day] = value
        message[:, day * 320 : day * 320 + 320] = value
    message[:, 960:] = pack


def precondition(w, message, co, early=(), late=()):
    pieces = ring_gather(message, "day_1")
    one = shaped(16, 448)
    *out, local = call(
        middle_kernel, "middle", (one, one, one, shaped(3, 16, 320)),
        [VMEM_BLOCK] * 5 + [ANY_BLOCK] * len(early), *pieces, co, *early,
    )
    got = [shift(out[k - 1], "day_0", k) for k in (1, 2, 3)]
    return call(
        last_kernel, "last", (shaped(3, 16, 320), shaped(16, 1088)),
        [VMEM_BLOCK] * 6 + [ANY_BLOCK] * len(late), *got, local, w, co, *late,
    )


def halves(value):
    high = value.astype(BF16)
    return high, (value - high.astype(F32)).astype(BF16)


def stacked_halves(value):
    return jnp.concatenate(halves(value), axis=0)


def matmul(first, second, dims):
    return lax.dot_general(first, second, dims, preferred_element_type=F32)


def times_rows(value, pair):
    n = pair.shape[0] // 2
    out = matmul(stacked_halves(value), pair, NT)
    return (out[:16, :n] + out[16:, :n]) + (out[:16, n:] + out[16:, n:])


def times_matrix(value, pair):
    high, low = halves(value)
    both = jnp.concatenate(
        [jnp.concatenate([high, high], axis=1), jnp.concatenate([low, low], axis=1)], axis=0
    )
    out = matmul(both, pair, NN)
    return out[:16] + out[16:]


VMEM_BLOCK = pl.BlockSpec(memory_space=pltpu.VMEM)
ANY_BLOCK = pl.BlockSpec(memory_space=pl.ANY)
HBM_BLOCK = pl.BlockSpec(memory_space=pltpu.HBM)


def shaped(*shape):
    return jax.ShapeDtypeStruct(shape, F32)


def whole_block(operand):
    return pl.BlockSpec(operand.shape, lambda i: (0,) * operand.ndim)


def call(kernel, name, outs, in_specs, *operands, scratch=(), limit=16, grid=()):
    return pl.pallas_call(
        kernel,
        grid=grid,
        out_shape=outs,
        in_specs=in_specs,
        out_specs=jax.tree.map(lambda _: VMEM_BLOCK, outs),
        scratch_shapes=scratch,
        compiler_params=pltpu.CompilerParams(vmem_limit_bytes=limit << 20),
        name=name,
    )(*operands)


CHUNK = 80


def split_kernel(day, source, target, buffer, sem):
    jobs = [(day, row) for row in range(0, 320, CHUNK)]

    def fetch(index):
        day, row = jobs[index]
        return pltpu.make_async_copy(source.at[day, pl.ds(row, CHUNK)], buffer.at[index], sem.at[index])

    for index in range(len(jobs)):
        fetch(index).start()
    for index, (day, row) in enumerate(jobs):
        fetch(index).wait()
        high, low = halves(buffer[index])
        target[pl.ds(row, CHUNK)] = high
        target[pl.ds(320 + row, CHUNK)] = low


def split_blocks(blocks, name, day):
    return call(
        functools.partial(split_kernel, day),
        name + str(day),
        pltpu.VMEM((640, 2560), BF16),
        [HBM_BLOCK],
        pltpu.with_memory_space_constraint(blocks, pltpu.HBM),
        scratch=[pltpu.VMEM((4, CHUNK, 2560), F32), pltpu.SemaphoreType.DMA((4,))],
    )


def pick(values, index):
    out = jnp.zeros_like(values[0])
    for place, value in enumerate(values):
        out = jnp.where(index == place, value, out)
    return out


def put_rows(message, values):
    for r, value in enumerate(values):
        for c, width in enumerate((128, 128, 64)):
            row = 1 + 3 * r + c
            message[row : row + 1, 640 : 640 + width] = value[:, 128 * c : 128 * c + width]


def get_rows(pack):
    return [
        jnp.concatenate(
            [pack[1 + 3 * r : 2 + 3 * r], pack[2 + 3 * r : 3 + 3 * r], pack[3 + 3 * r : 4 + 3 * r, :64]], axis=1
        )
        for r in range(4)
    ]


def only_first_row(value):
    return jnp.where(lax.broadcasted_iota(jnp.int32, value.shape, 0) == 0, value, 0.0)


def ordered(kept, messages, place):
    for k, message in enumerate(messages):
        kept[k] = message[...]
    return [kept[place ^ j] for j in range(4)]


def first_middle_kernel(m0, m1, m2, m3, *refs):
    out, ordered_out, kept = refs[-3:]
    messages = ordered(kept, (m0, m1, m2, m3), lax.axis_index("day_1"))
    for j, message in enumerate(messages):
        ordered_out[j] = message
    pack = ring_sum([m[:, 640:] for m in (m0, m1, m2, m3)])
    out[:, 640:] = only_first_row(pack)
    chain = [get_rows(m[:, 640:]) for m in messages]
    alpha, beta = jnp.zeros((1, 320), F32), jnp.ones((1, 320), F32)
    alphas = [None] * 4
    for j in (3, 2, 1, 0):
        dec0, dec1, dom0, dom1 = chain[j]
        alphas[j] = alpha
        const = 1.0 / dom0 + dec1 * dec1 * (1.0 / dom1 + alpha)
        slope = dec1 * dec1 * beta
        alpha, beta = dec0 * dec0 * const, dec0 * dec0 * slope
    moved = jnp.ones((1, 320), F32)
    total_f = total_p = jnp.zeros((16, 320), F32)
    for j in range(4):
        dec0, dec1 = chain[j][:2]
        f, p = messages[j][:, :320], messages[j][:, 320:640]
        if j:
            moved = moved * dec0
        total_f = f + dec0 * dec1 * total_f
        total_p = total_p + moved * (p + alphas[j] * dec1 * f)
        moved = moved * dec1
    out[:, :320] = total_f
    out[:, 320:640] = total_p
    put_rows(out, (moved, const, slope, chain[0][0]))


def first_last_kernel(z0, z1, z2, z3, near, bx, *refs):
    co, w, v, message, kept = refs[-5:]
    group, place = lax.axis_index("day_0"), lax.axis_index("day_1")
    zero, one = jnp.zeros((1, 320), F32), jnp.ones((1, 320), F32)
    groups = ordered(kept, (z0, z1, z2, z3), group)
    chain = [get_rows(near[j, :, 640:]) for j in range(4)]
    whole_chain = [get_rows(m[:, 640:]) for m in groups]
    moved = [c[0] for c in whole_chain]
    first_decay = [c[3] for c in whole_chain] + [zero]
    exits, entry = [zero] * 4, [zero] * 5
    for g in (3, 2, 1, 0):
        entry[g] = whole_chain[g][1] + whole_chain[g][2] * exits[g]
        if g:
            exits[g - 1] = first_decay[g] * first_decay[g] * entry[g]
    dec0 = [c[0] for c in chain]
    dec1 = [c[1] for c in chain]
    after_decay = dec0[1:] + [pick(first_decay[1:], group)]
    gain0, gain1, after_gain = [None] * 4, [None] * 4, [None] * 4
    beyond = pick(exits, group)
    for j in (3, 2, 1, 0):
        after_gain[j] = beyond
        gain1[j] = 1.0 / chain[j][3] + beyond
        gain0[j] = 1.0 / chain[j][2] + dec1[j] * dec1[j] * gain1[j]
        beyond = dec0[j] * dec0[j] * gain0[j]
    next_gain = gain0[1:] + [pick(entry[1:], group)]
    mine = [dec1[j] * after_decay[j] for j in range(4)]
    whole = [moved[g] * first_decay[g + 1] for g in range(4)]

    def product(factors, low, high):
        kept = [
            jnp.where((low <= index) & (index < high), factor, one)
            for index, factor in enumerate(factors)
        ]
        return kept[0] * kept[1] * kept[2] * kept[3]

    rows = [pick(values, place) for values in (gain0, gain1, next_gain, dec0, dec1, after_decay)]
    local_f, local_b, total_f, total_b, far = [], [], [], [], []
    for k in range(4):
        source = place ^ k
        total_f.append(product(mine, source + 1, 4))
        total_b.append(product(mine, 0, source))
        if k:
            local_f.append(jnp.where(source < place, product(mine, source + 1, place), zero))
            local_b.append(jnp.where(source > place, product(mine, place + 1, source), zero))
            origin = group ^ k
            far.append(product(whole, jnp.minimum(origin, group) + 1, jnp.maximum(origin, group)))
    before, after = product(mine, 0, place), product(mine, place + 1, 4)
    rows += local_f + local_b + total_f + total_b + far + [before, after]
    for index, row in enumerate(rows):
        co[index : index + 1] = row

    come_f = come_b = far_f = far_b = jnp.zeros((16, 320), F32)
    for j in range(4):
        f, p = near[j, :, :320], near[j, :, 320:640]
        ahead = after_decay[j] * f
        behind = p + after_gain[j] * dec1[j] * f
        come_f = come_f + jnp.where(j < place, product(mine, j + 1, place) * ahead, 0.0)
        come_b = come_b + jnp.where(j > place, product(mine, place + 1, j) * behind, 0.0)
        f, p = groups[j][:, :320], groups[j][:, 320:640]
        ahead = first_decay[j + 1] * f
        behind = p + exits[j] * moved[j] * f
        far_f = far_f + jnp.where(j < group, product(whole, j + 1, group) * ahead, 0.0)
        far_b = far_b + jnp.where(j > group, product(whole, group + 1, j) * behind, 0.0)
    w[0], w[1], w[2] = bx[0], bx[1], jnp.zeros((16, 320), F32)
    pack = only_first_row(ring_sum([z[:, 640:] for z in (z0, z1, z2, z3)]))
    raise_days(come_f + before * far_f, come_b + after * far_b, w, co, v, message, pack)


def first_precondition(bx, message, early, late):
    pieces = ring_gather(message, "day_1")
    out, near = call(
        first_middle_kernel,
        "first_middle",
        (shaped(16, 768), shaped(4, 16, 768)),
        [VMEM_BLOCK] * 4 + [ANY_BLOCK],
        *pieces, early,
        scratch=[pltpu.VMEM((4, 16, 768), F32)],
    )
    field = shaped(3, 16, 320)
    return call(
        first_last_kernel,
        "first_last",
        (shaped(25, 320), field, field, shaped(16, 1088)),
        [VMEM_BLOCK] * 6 + [ANY_BLOCK],
        *ring_gather(out, "day_0"), near, bx, late,
        scratch=[pltpu.VMEM((4, 16, 768), F32)],
    )


def own_terms_kernel(a0, a1, o0, o1, own, out):
    out[0] = times_matrix(own[0], a0[...])
    out[1] = times_matrix(own[1], a1[...]) + times_matrix(own[0], o0[...])
    out[2] = times_matrix(own[1], o1[...])


def own_terms(pairs, own):
    return call(own_terms_kernel, "own_terms", shaped(3, 16, 2560), [VMEM_BLOCK] * 5, *pairs, own)


def rows_into(pairs, whole, out):
    for day in range(2):
        out[day] = times_rows(whole[day + 1], pairs[day][...])


def lanes(*values):
    lane = lax.broadcasted_iota(jnp.int32, (16, 64), 1)
    out = jnp.zeros((16, 64), F32)
    for index, value in enumerate(values):
        out = jnp.where(lane == index, value, out)
    return out


def first_rows_kernel(o0, o1, whole, bx, v1, out, dots):
    rows_into((o0, o1), whole, out)
    dots[...] = lanes(sum(row_sum(bx[day] * v1[day]) for day in range(2)))


def first_rows(*operands):
    return call(
        first_rows_kernel, "first_rows", (shaped(2, 16, 320), shaped(16, 64)), [VMEM_BLOCK] * 5, *operands
    )


def second_rows_kernel(o0, o1, whole, bx, v1, v2, w1, scalars, out, dots, r1, z1):
    rows_into((o0, o1), whole, out)
    step0 = scalars[:, 0:1]
    norm = cross = jnp.zeros((16, 1), F32)
    for day in range(3):
        z = v1[day] - step0 * v2[day]
        r = (bx[day] if day < 2 else 0.0) - step0 * w1[day]
        z1[day] = z
        r1[day] = r
        norm = norm + row_sum(r * z)
        cross = cross + row_sum(z * w1[day])
    dots[...] = lanes(norm, 0.0, cross)


def second_rows(*operands):
    own = shaped(3, 16, 320)
    return call(
        second_rows_kernel,
        "second_rows",
        (shaped(2, 16, 320), shaped(16, 64), own, own),
        [VMEM_BLOCK] * 8,
        *operands,
    )


def start_kernel(p0, p1, p2, p3, probes, grad_cov, leakage, dominant, *refs):
    bx, message = refs[-2:]
    grad = ring_sum([p0[...], p1[...], p2[...], p3[...]])
    for day in range(2):
        bx[day, 0:1] = grad[day : day + 1]
        bx[day, 1:16] = probes[:, day, :]
    dec0, dec1 = 1.0 - leakage[0:1], 1.0 - leakage[1:2]
    dom0, dom1 = dominant[0:1], dominant[1:2]
    ahead = bx[1] + dec1 * bx[0]
    message[:, :320] = ahead
    message[:, 320:640] = bx[0] / dom0 + dec1 * ahead / dom1
    message[:, 640:] = jnp.zeros((16, 128), F32)
    message[0:1, 640:704] = grad_cov[...]
    put_rows(message, (dec0, dec1, dom0, dom1))


def start_stage(*operands):
    return call(
        start_kernel,
        "start_stage",
        (shaped(2, 16, 320), shaped(16, 768)),
        [VMEM_BLOCK] * 8 + [ANY_BLOCK] * (len(operands) - 8),
        *operands,
    )


def image_kernel(p0, p1, p2, p3, rows, vector, cov_terms, dots, co, w, message):
    pieces = (p0, p1, p2, p3)
    total = jnp.zeros((16, 1), F32)
    for day in range(3):
        value = ring_sum([p[day] for p in pieces])
        if day < 2:
            value = value + rows[day]
        w[day] = value
        total = total + row_sum(vector[day] * value)
    ahead, behind = ring_message(w, co)
    message[:, :320] = ahead
    message[:, 320:640] = behind
    message[:, 640:704] = cov_terms[...]
    message[:, 704:] = dots[...] + lanes(0.0, total)


def image_stage(*operands):
    return call(
        image_kernel,
        "image_stage",
        (shaped(3, 16, 320), shaped(16, 768)),
        [VMEM_BLOCK] * 9,
        *operands,
    )


def assemble(mine, other, whole):
    row, core = lax.axis_index("blk_0"), lax.axis_index("blk_1")
    packs = []
    for k in range(4):
        at = pl.multiple_of((row ^ k) * 640, 128)
        for day in range(3):
            a = mine[k, :, day * 320 : day * 320 + 320]
            b = other[k, :, day * 320 : day * 320 + 320]
            first = jnp.where(core == 0, a, b)
            second = jnp.where(core == 0, b, a)
            whole[day, :, pl.ds(at, 640)] = jnp.concatenate([first, second], axis=1)
        packs.append(mine[k, :, 960:1088] + other[k, :, 960:1088])
    return (packs[0] + packs[2]) + (packs[1] + packs[3])


def scatter_parts(obs, terms, kept, sent):
    core = lax.axis_index("blk_1")
    last = lax.axis_index("day_0") * 4 + lax.axis_index("day_1") == 15
    days = (obs[0] + terms[0], obs[1] + terms[1], jnp.where(last, 0.0, terms[2]))
    for day, part in enumerate(days):
        for row in range(4):
            first = part[:, row * 640 : row * 640 + 320]
            second = part[:, row * 640 + 320 : row * 640 + 640]
            kept[row, day] = jnp.where(core == 0, first, second)
            sent[row, day] = jnp.where(core == 0, second, first)


def observe(whole, cov, spread, covariates, weight):
    result = []
    for day in range(2):
        out = matmul(stacked_halves(whole[day]), spread[day], NN)
        out = (out[:16, :128] + out[16:, :128]) + (out[:16, 128:] + out[16:, 128:])
        predictor = out + times_matrix(cov, covariates[day])
        result.append((predictor, weight[day : day + 1] * predictor))
    return result


def spread_out(value, pair):
    high, low = halves(value)
    both = jnp.concatenate(
        [jnp.concatenate([high, high], axis=1), jnp.concatenate([low, low], axis=1)], axis=0
    )
    out = matmul(both, pair, NT)
    return out[:16] + out[16:]


def observe_back(observed, behind, spread, covariates, kept, sent, cov_terms):
    weights = [pair[1] for pair in observed]
    obs = [spread_out(weights[day], spread[day]) for day in range(2)]
    scatter_parts(obs, behind, kept, sent)
    cov_terms[...] = sum(times_rows(weights[day], covariates[day]) for day in range(2))


def row_sum(value):
    return jnp.sum(value, axis=1, keepdims=True)


PARTS = (shaped(4, 3, 16, 320), shaped(4, 3, 16, 320), shaped(16, 64))


def first_kernel(mine, other, probes_cov, spread, covariates, weight, behind, kept, sent, cov_terms, whole, cov):
    pack = assemble(mine, other, whole)
    cov[...] = jnp.where(
        lax.broadcasted_iota(jnp.int32, (16, 64), 0) == 0, pack[:, :64], probes_cov[...]
    )
    observed = observe(whole, cov[...], spread, covariates, weight)
    observe_back(observed, behind, spread, covariates, kept, sent, cov_terms)


def first_stage(mine, other, probes_cov, spread, covariates, weight, behind):
    return call(
        first_kernel,
        "first_stage",
        PARTS + (shaped(3, 16, 2560), shaped(16, 64)),
        [VMEM_BLOCK] * 7,
        mine, other, probes_cov, spread, covariates, weight, behind,
    )


def second_kernel(
    mine, other, whole1, c0, prior, spread, covariates, weight, behind1, behind2,
    kept, sent, cov_terms, whole2, whole, cov, hcov, scalars, behind,
):
    pack = assemble(mine, other, whole2)
    hcov1 = pack[:, :64] + prior[...] * c0[...]
    norm0 = pack[:, 64:65] + row_sum(c0[...] * c0[...])
    curve0 = pack[:, 65:66] + row_sum(c0[...] * hcov1)
    step0 = norm0 / curve0
    for day in range(3):
        whole[day] = whole1[day] - step0 * whole2[day]
    for day in range(3):
        behind[day] = behind1[day] - step0 * behind2[day]
    cov[...] = c0[...] - step0 * hcov1
    hcov[...] = hcov1
    lane = lax.broadcasted_iota(jnp.int32, (16, 128), 1)
    scalars[...] = jnp.where(lane == 0, step0, jnp.where(lane == 1, norm0, curve0))
    observed = observe(whole, cov[...], spread, covariates, weight)
    observe_back(observed, behind, spread, covariates, kept, sent, cov_terms)


def second_stage(mine, other, whole1, c0, prior, spread, covariates, weight, behind1, behind2):
    whole = shaped(3, 16, 2560)
    return call(
        second_kernel,
        "second_stage",
        PARTS + (whole, whole, shaped(16, 64), shaped(16, 64), shaped(16, 128)),
        [VMEM_BLOCK] * 10,
        mine, other, whole1, c0, prior, spread, covariates, weight, behind1, behind2,
        scratch=[pltpu.VMEM((3, 16, 2560), F32)],
    )


def third_kernel(
    mine, other, whole2, z1whole, scalars, c0, z1cov, hcov1, prior, spread, covariates, weight,
    a0, a1, o0, o1, r1, z1, w1, w2, v1, v2, v3,
    sums, z2, p1, scalars_out, covs, whole,
):
    pack = assemble(mine, other, whole)
    norm0, curve0 = scalars[:, 1:2], scalars[:, 2:3]
    hcov2 = pack[:, :64] + prior[...] * z1cov[...]
    norm1 = pack[:, 64:65] + row_sum(z1cov[...] * z1cov[...])
    beta1 = norm1 / norm0
    curve1 = (
        pack[:, 65:66]
        + row_sum(z1cov[...] * hcov2)
        + 2.0 * beta1 * (pack[:, 66:67] + row_sum(z1cov[...] * hcov1[...]))
        + beta1 * beta1 * curve0
    )
    step1 = norm1 / curve1
    hp1cov = hcov2 + beta1 * hcov1[...]
    r2cov = z1cov[...] - step1 * hp1cov
    covs[0] = r2cov
    covs[1] = z1cov[...] + beta1 * c0[...]
    own_norm = jnp.zeros((16, 1), F32)
    cross = jnp.zeros((16, 1), F32)
    for day in range(3):
        hp1 = w2[day] + beta1 * w1[day]
        r2 = r1[day] - step1 * hp1
        z2day = z1[day] - step1 * (v3[day] + beta1 * v2[day])
        own_norm = own_norm + row_sum(r2 * z2day)
        cross = cross + row_sum(z2day * hp1)
        if day < 2:
            z2[day] = z2day
            p1[day] = z1[day] + beta1 * v1[day]
        whole[day] = z1whole[day] - step1 * (whole[day] + beta1 * whole2[day])
    observed = observe(whole, r2cov, spread, covariates, weight)
    quadratic = sum(row_sum(predictor * weighted) for predictor, weighted in observed)
    for day in range(2):
        quadratic = quadratic + row_sum(times_matrix(z2[day], (a0, a1)[day][...]) * whole[day])
        quadratic = quadratic + 2.0 * row_sum(
            times_matrix(z2[day], (o0, o1)[day][...]) * whole[day + 1]
        )
    lane = lax.broadcasted_iota(jnp.int32, (16, 128), 1)
    sub = lax.broadcasted_iota(jnp.int32, (16, 128), 0)
    line = jnp.zeros((16, 128), F32)
    for index, value in enumerate((own_norm, quadratic, cross)):
        line = jnp.where(lane == sub + 16 * index, value, line)
    sums[...] = jnp.broadcast_to(jnp.sum(line, axis=0, keepdims=True), (128, 128))
    norm2cov = row_sum(r2cov * r2cov)
    quadcov = row_sum(r2cov * prior[...] * r2cov)
    crosscov = row_sum(r2cov * hp1cov)
    values = (scalars[:, 0:1], step1, norm1, curve1, norm2cov, quadcov, crosscov)
    out = jnp.zeros((16, 128), F32)
    for index, value in enumerate(values):
        out = jnp.where(lane == index, value, out)
    scalars_out[...] = out


def third_stage(*operands):
    own = shaped(2, 16, 320)
    return call(
        third_kernel,
        "third_stage",
        (shaped(128, 128), own, own, shaped(16, 128), shaped(2, 16, 64)),
        [VMEM_BLOCK] * len(operands),
        *operands,
        scratch=[pltpu.VMEM((3, 16, 2560), F32)],
    )


def final_kernel(sums, scalars, v1, p1, z2, c0, covs, field, cov):
    step0, step1, norm1, curve1, norm2cov, quadcov, crosscov = (
        scalars[:, i : i + 1] for i in range(7)
    )
    lane = lax.broadcasted_iota(jnp.int32, (16, 128), 1)
    sub = lax.broadcasted_iota(jnp.int32, (16, 128), 0)
    line = jnp.sum(sums[...], axis=0, keepdims=True)
    own_norm, quadratic, cross = (
        row_sum(jnp.where(lane == sub + 16 * index, line, 0.0)) for index in range(3)
    )
    norm2 = own_norm + norm2cov
    beta2 = norm2 / norm1
    curve2 = (
        quadratic + quadcov + 2.0 * beta2 * (cross + crosscov) + beta2 * beta2 * curve1
    )
    step2 = norm2 / curve2
    middle = step1 + step2 * beta2
    for day in range(2):
        field[:, day, :] = step0 * v1[day] + middle * p1[day] + step2 * z2[day]
    cov[...] = step0 * c0[...] + middle * covs[1] + step2 * covs[0]


def final_stage(*operands):
    return call(
        final_kernel,
        "final_stage",
        (shaped(16, 2, 320), shaped(16, 64)),
        [VMEM_BLOCK] * len(operands),
        *operands,
    )


def setup_kernel(count, triangles, cells, bary, prec, value, covs, spread, weight, kept, sent, grad_cov, covariates, table):
    core = lax.axis_index("blk_1")
    slot_start = (lax.axis_index("blk_0") * 2 + core) * 128
    cov_sum = jnp.zeros((1, 64), F32)
    table[...] = jnp.zeros((8, 5120), F32)
    table[0:3, 0:5116] = triangles[...].astype(F32)
    parts = stacked_halves(table[...])
    for day in range(2):
        cell = lax.broadcasted_iota(jnp.int32, (5120, 128), 0) == cells[day : day + 1, :]
        found = matmul(parts, jnp.where(cell, 1.0, 0.0).astype(BF16), NN)
        corners = (found[:8] + found[8:]).astype(jnp.int32)
        shares = [bary[k, day : day + 1, :] for k in range(3)]
        total = shares[0] + shares[1] + shares[2]
        nodes = lax.broadcasted_iota(jnp.int32, (2560, 128), 0)
        dense = jnp.zeros((2560, 128), F32)
        for k in range(3):
            dense = dense + jnp.where(nodes == corners[k : k + 1, :], shares[k] / total, 0.0)
        high, low = halves(dense)
        spread[day, :, :128] = high
        spread[day, :, 128:] = low
        covariates[day] = stacked_halves(covs[:, day, :])
        slot = lax.broadcasted_iota(jnp.int32, (1, 128), 1) + slot_start
        slot_weight = jnp.where(slot < count[0:1, day : day + 1], prec[day : day + 1], 0.0)
        weight[day : day + 1] = slot_weight
        weighted_value = jnp.broadcast_to(slot_weight * value[day : day + 1], (16, 128))
        grad = spread_out(weighted_value, spread[day])[:1]
        for row in range(4):
            first = grad[:, row * 640 : row * 640 + 320]
            second = grad[:, row * 640 + 320 : row * 640 + 640]
            kept[row, day : day + 1] = jnp.where(core == 0, first, second)
            sent[row, day : day + 1] = jnp.where(core == 0, second, first)
        cov_sum = cov_sum + times_rows(weighted_value, covariates[day])[:1]
    grad_cov[...] = cov_sum


def setup_stage(*operands):
    return call(
        setup_kernel,
        "setup_stage",
        (
            pltpu.VMEM((2, 2560, 256), BF16), shaped(2, 128), shaped(4, 2, 320), shaped(4, 2, 320),
            shaped(1, 64), pltpu.VMEM((2, 128, 128), BF16),
        ),
        [whole_block(o) for o in operands],
        *(pltpu.with_memory_space_constraint(o, pltpu.HBM) for o in operands),
        grid=(1,),
        scratch=[pltpu.VMEM((8, 5120), F32)],
    )


def on_device(
    diag_blocks,
    off_blocks,
    leakage,
    obs_count,
    obs_triangle,
    obs_bary,
    obs_prec,
    obs_value,
    covariates,
    triangles,
    prior_prec,
    probes,
    probes_cov,
):
    row_start = lax.axis_index(BLK) * 320
    square = lax.dynamic_slice_in_dim(diag_blocks, row_start, 320, 2)
    rows = lax.broadcasted_iota(jnp.int32, (2, 320, 320), 1)
    columns = lax.broadcasted_iota(jnp.int32, (2, 320, 320), 2)
    dominant = jnp.sum(jnp.where(rows == columns, square, 0.0), axis=1)

    spread, weight, kept, sent, grad_cov, covs = setup_stage(
        obs_count.reshape(1, 2), triangles, obs_triangle, obs_bary, obs_prec, obs_value, covariates
    )
    off_pair = [split_blocks(off_blocks, "split_off", day) for day in range(2)]
    diag_pair = [split_blocks(diag_blocks, "split_diag", day) for day in range(2)]
    bx, message = start_stage(*scattered_pieces(kept, sent), probes, grad_cov, leakage, dominant, off_pair[0])
    prior = prior_prec[None]
    padded_cov = jnp.pad(probes_cov, ((1, 0), (0, 0)))

    pairs = (*diag_pair, *off_pair)
    co, _, v1, message = first_precondition(bx, message, off_pair[1], diag_pair[0])
    nodes, behind1 = gather_nodes(message, own_terms(pairs, v1))
    kept, sent, cov1, whole1, c0 = first_stage(
        *nodes, padded_cov, spread, covs, weight, behind1
    )
    image, dots = first_rows(*off_pair, whole1, bx, v1)
    w1, message = image_stage(*scattered_pieces(kept, sent), image, v1, cov1, dots, co)

    v2, message = precondition(w1, message, co)
    nodes, behind2 = gather_nodes(message, own_terms(pairs, v2))
    kept, sent, cov2, whole2, z1whole, z1cov, hcov1, scalars = second_stage(
        *nodes, whole1, c0, prior, spread, covs, weight, behind1, behind2
    )
    image, dots, r1, z1 = second_rows(*off_pair, z1whole, bx, v1, v2, w1, scalars)
    w2, message = image_stage(*scattered_pieces(kept, sent), image, z1, cov2, dots, co)

    v3, message = precondition(w2, message, co)
    sums, z2, p1, scalars, covs2 = third_stage(
        *gather_nodes(message, behind2)[0], whole2, z1whole, scalars, c0, z1cov, hcov1, prior, spread, covs, weight,
        *pairs, r1, z1, w1, w2, v1, v2, v3,
    )
    sums = lax.all_to_all(sums, DAY + BLK, 0, 0, tiled=True)
    return final_stage(sums, scalars, v1, p1, z2, c0, covs2)


def solution(mesh):
    split = Mesh(mesh.devices.reshape(4, 4, 4, 2), ("day_0", "day_1", "blk_0", "blk_1"))
    in_specs = (
        P(DAY, BLK, None),
        P(DAY, BLK, None),
        P(DAY, BLK),
        P(DAY),
        P(DAY, BLK),
        P(None, DAY, BLK),
        P(DAY, BLK),
        P(DAY, BLK),
        P(None, DAY, BLK),
        P(),
        P(),
        P(None, DAY, BLK),
        P(),
    )
    out_specs = (P(None, DAY, BLK), P())
    return jax.shard_map(
        on_device, mesh=split, in_specs=in_specs, out_specs=out_specs, check_vma=False
    )
```
